1024 devices in a mesh: gx: 16 (over x, y), gy: 64 (over z, core).
Axes of the slice: x: 4, y: 4, z: 32, core: 2. Of those that a mesh axis runs over, the one named last changes fastest.
Arguments:
- right_side: float32 [112, 448, 168], P('gx', 'gy'), may hold values from -18 to 18
- stiff_coef: float32 [16, 64, 24], P('gx', 'gy'), may hold values from 0.3 to 3
- mass_coef: float32 [16, 64, 24], P('gx', 'gy'), may hold values from 2 to 200
- coarse_factor: float32 [8192, 8192], P(('gx', 'gy')), may hold values from -0.0068359375 to 0.0068359375
Outputs:
- solution: float32 [112, 448, 168], P('gx', 'gy')
- residual: float32 [112, 448, 168], P('gx', 'gy')
The draws below stay inside these ranges and needn't reach their ends.
All inputs are finite; a program needn't handle non-finite values.
Results may differ from the reference program's by a relative error of at most 0.0003.
Values sent between devices are 32-bit elements; how exact they have to be, the bound alone decides.
No kernel may reach another device: no remote copies, remote signals or barrier semaphores. Data moves between devices by JAX's collectives and lax.ppermute only.
A program may use at most 32 MiB of HBM per device.

```python
import math
import jax
import jax.numpy as jnp
import numpy as np
from jax import lax

EZ = 24
C_DEV = 8
ITERS = 2
ELX = 16
ELY = 64
NX = 112
NY = 448
NZ = 168
NC = 8192
N_GX = 16
N_GY = 64


def draw_right_side(key, part):
    first_pos = jnp.arange(NX, dtype=jnp.float32)[:, None, None] / NX
    second_pos = jnp.arange(NY, dtype=jnp.float32)[None, :, None] / NY
    rising = 1.0 + first_pos + second_pos
    jitter = jax.random.normal(key, (NX, NY, NZ), jnp.float32)
    return jnp.clip(jitter * rising, -18.0, 18.0)


def block_levels(stream_key, dims, split, low, high):
    def one(dim, shards_of):
        draws = jax.random.uniform(jax.random.fold_in(jax.random.fold_in(stream_key, 6), dim), (shards_of,), jnp.float32, low / len(split), high / len(split))
        return jnp.repeat(jnp.exp(draws), dims[dim] // shards_of).reshape((-1,) + (1,) * (len(dims) - dim - 1))

    level = one(*split[0])
    for cut in split[1:]:
        level = level * one(*cut)
    return level


def scatter_about(stream_key, shape, width, most, cuts=(), kind=jnp.bfloat16):
    values = jax.random.normal(stream_key, shape, jnp.float32) * width
    if len(cuts) > 0:
        values = block_levels(stream_key, shape, cuts, -0.22, 0.18) * values
    return jnp.clip(values, min=-most, max=most).astype(kind)


def setup_inputs(seed: int = 0) -> dict:
    streams_of = jax.random.split(jax.random.key(seed), 5)
    right_side = draw_right_side(jax.random.fold_in(streams_of[4], 71), 0)
    stiff_coef = jnp.clip(jnp.exp(math.log(3.0) - 2.3025851 * jax.random.uniform(streams_of[1], (ELX, ELY, EZ), jnp.float32) ** block_levels(streams_of[1], (ELX, ELY, EZ), ((0, 16), (1, 64)), -0.2, 0.2)), 0.3, 3.0)
    mass_coef = jnp.clip(jnp.exp(math.log(200.0) - 4.6051702 * jax.random.uniform(streams_of[2], (ELX, ELY, EZ), jnp.float32) ** block_levels(streams_of[2], (ELX, ELY, EZ), ((0, 16), (1, 64)), -0.2, 0.2)), 2.0, 200.0)
    coarse_factor = scatter_about(streams_of[3], (NC, NC), (NC * 96) ** -0.5, 0.0068359375, ((0, 1024),), jnp.float32)
    return dict(right_side=right_side, stiff_coef=stiff_coef, mass_coef=mass_coef, coarse_factor=coarse_factor)


exact_mode = lax.Precision.HIGHEST

def legendre_pair(position, degree):
    p_prev = 1.0
    p_now = position
    for order in range(2, degree + 1):
        p_next = ((2 * order - 1) * position * p_now - (order - 1) * p_prev) / order
        p_prev = p_now
        p_now = p_next
    return (p_now, p_prev)

def jacobi_eigen(matrix):
    size_n = matrix.shape[0]
    current = np.array(matrix)
    vectors = np.eye(size_n)
    for sweep in range(20):
        for row_p in range(size_n - 1):
            for row_q in range(row_p + 1, size_n):
                off_value = current[row_p, row_q]
                if abs(off_value) > 1e-300:
                    theta = (current[row_q, row_q] - current[row_p, row_p]) / (2.0 * off_value)
                    sign_t = 1.0 if theta >= 0.0 else -1.0
                    tangent = sign_t / (abs(theta) + math.sqrt(theta * theta + 1.0))
                    cosine = 1.0 / math.sqrt(tangent * tangent + 1.0)
                    sine = tangent * cosine
                    rotation = np.eye(size_n)
                    rotation[row_p, row_p] = cosine
                    rotation[row_q, row_q] = cosine
                    rotation[row_p, row_q] = sine
                    rotation[row_q, row_p] = -sine
                    current = rotation.T @ current @ rotation
                    vectors = vectors @ rotation
    return (np.array([current[idx, idx] for idx in range(size_n)]), vectors)

def gll_tables():
    degree = 7
    guesses = [-0.8717401485096066, -0.5917001814331423, -0.2092992179024789, 0.2092992179024789, 0.5917001814331423, 0.8717401485096066]
    interior = []
    for guess in guesses:
        position = guess
        for newton in range(30):
            p_now, p_prev = legendre_pair(position, degree)
            first = degree * (position * p_now - p_prev) / (position * position - 1.0)
            second = (2.0 * position * first - degree * (degree + 1) * p_now) / (1.0 - position * position)
            position = position - first / second
        interior.append(position)
    points = np.array([-1.0] + interior + [1.0])
    values = np.array([legendre_pair(float(pt), degree)[0] for pt in points])
    weights = 2.0 / (degree * (degree + 1) * values ** 2)
    deriv_mat = np.zeros((8, 8))
    for left_idx in range(8):
        for right_idx in range(8):
            if left_idx != right_idx:
                deriv_mat[left_idx, right_idx] = values[left_idx] / (values[right_idx] * (points[left_idx] - points[right_idx]))
    deriv_mat[0, 0] = -degree * (degree + 1) / 4.0
    deriv_mat[7, 7] = degree * (degree + 1) / 4.0
    stiffness = deriv_mat.T @ (weights[:, None] * deriv_mat)
    ext_stiff = np.zeros((10, 10))
    ext_stiff[1:9, 1:9] += stiffness
    ext_stiff[0:2, 0:2] += stiffness[6:8, 6:8]
    ext_stiff[8:10, 8:10] += stiffness[0:2, 0:2]
    ext_mass = np.zeros(10)
    ext_mass[1:9] += weights
    ext_mass[0:2] += weights[6:8]
    ext_mass[8:10] += weights[0:2]
    inv_root = 1.0 / np.sqrt(ext_mass)
    eigen_vals, eigen_vecs = jacobi_eigen(inv_root[:, None] * ext_stiff * inv_root[None, :])
    eigen_basis = inv_root[:, None] * eigen_vecs
    return (jnp.asarray(stiffness, jnp.float32), jnp.asarray(weights, jnp.float32), jnp.asarray(eigen_basis, jnp.float32), jnp.asarray(eigen_vals, jnp.float32))

def take_rows(widened, low, high, fold_axis):
    return lax.slice_in_dim(widened, low, high, axis=fold_axis)

def face_fold(widened, fold_axis):
    pieces = [take_rows(widened, 0, 1, fold_axis), take_rows(widened, 2, 3, fold_axis) + take_rows(widened, 1, 2, fold_axis), take_rows(widened, 3, 9, fold_axis), take_rows(widened, 9, 10, fold_axis) + take_rows(widened, 10, 11, fold_axis), take_rows(widened, 11, 12, fold_axis)]
    return jnp.concatenate(pieces, axis=fold_axis)

def spread_fold(widened, fold_axis):
    pieces = [take_rows(widened, 3, 5, fold_axis) + take_rows(widened, 0, 2, fold_axis), take_rows(widened, 5, 9, fold_axis), take_rows(widened, 9, 11, fold_axis) + take_rows(widened, 12, 14, fold_axis)]
    return jnp.concatenate(pieces, axis=fold_axis)

def z_windows(field_in, span):
    leading = field_in.shape[:2]
    elements = field_in.shape[2] // 7
    blocks = jnp.moveaxis(field_in.reshape(leading + (elements, 7)), 2, 3)
    if span == 8:
        return jnp.concatenate([blocks, jnp.roll(blocks[:, :, 0:1], -1, axis=3)], axis=2)
    behind = jnp.roll(blocks[:, :, 6:7], 1, axis=3)
    forward = jnp.roll(blocks[:, :, 0:2], -1, axis=3)
    return jnp.concatenate([behind, blocks, forward], axis=2)

def z_fold(blocks):
    if blocks.shape[2] == 8:
        owned = jnp.concatenate([blocks[:, :, 0:1] + jnp.roll(blocks[:, :, 7:8], 1, axis=3), blocks[:, :, 1:7]], axis=2)
    else:
        first_two = blocks[:, :, 1:3] + jnp.roll(blocks[:, :, 8:10], 1, axis=3)
        last_one = blocks[:, :, 7:8] + jnp.roll(blocks[:, :, 0:1], -1, axis=3)
        owned = jnp.concatenate([first_two, blocks[:, :, 3:7], last_one], axis=2)
    leading = owned.shape[:2]
    return jnp.moveaxis(owned, 2, 3).reshape(leading + (-1,))

def element_apply(blocks, stiff_line, mass_line, stiffness, weights):
    along_x = jnp.einsum('ai,ijte->ajte', stiffness, blocks, precision=exact_mode)
    along_y = jnp.einsum('aj,ijte->iate', stiffness, blocks, precision=exact_mode)
    along_z = jnp.einsum('at,ijte->ijae', stiffness, blocks, precision=exact_mode)
    weight_x = weights[:, None, None, None]
    weight_y = weights[None, :, None, None]
    weight_z = weights[None, None, :, None]
    laplace = along_x * weight_y * weight_z + along_y * weight_x * weight_z + along_z * weight_x * weight_y
    return stiff_line * laplace + mass_line * (weight_x * weight_y * weight_z) * blocks

def local_solve(blocks, stiff_line, mass_line, eigen_basis, eigen_vals):
    spectral = jnp.einsum('ia,ijte->ajte', eigen_basis, blocks, precision=exact_mode)
    spectral = jnp.einsum('jb,ajte->abte', eigen_basis, spectral, precision=exact_mode)
    spectral = jnp.einsum('tc,abte->abce', eigen_basis, spectral, precision=exact_mode)
    eigen_sum = eigen_vals[:, None, None] + eigen_vals[None, :, None] + eigen_vals[None, None, :]
    spectral = spectral / (stiff_line * eigen_sum[..., None] + mass_line)
    restored = jnp.einsum('ai,ijte->ajte', eigen_basis, spectral, precision=exact_mode)
    restored = jnp.einsum('bj,ajte->abte', eigen_basis, restored, precision=exact_mode)
    return jnp.einsum('ct,abte->abce', eigen_basis, restored, precision=exact_mode)

def ref_halo(blocks):
    from_left = jnp.roll(blocks, 1, axis=0)[:, :, -2:]
    from_right = jnp.roll(blocks, -1, axis=0)[:, :, :2]
    widened = jnp.concatenate([from_left, blocks, from_right], axis=2)
    from_below = jnp.roll(widened, 1, axis=1)[:, :, :, -2:]
    from_above = jnp.roll(widened, -1, axis=1)[:, :, :, :2]
    return jnp.concatenate([from_below, widened, from_above], axis=3)

def reference(right_side, stiff_coef, mass_coef, coarse_factor):
    stiffness, weights, eigen_basis, eigen_vals = gll_tables()
    z_points = right_side.shape[2]
    blocks = right_side.reshape(N_GX, 7, N_GY, 7, z_points).transpose(0, 2, 1, 3, 4)

    def per_column(worker, fields):

        def one_row(packed):
            return jax.vmap(worker)(packed[0], packed[1], packed[2])
        return lax.map(one_row, (fields, stiff_coef, mass_coef))

    def element_sum(field_in, stiff_line, mass_line):
        return z_fold(element_apply(z_windows(field_in, 8), stiff_line, mass_line, stiffness, weights))

    def schwarz_sum(field_in, stiff_line, mass_line):
        return z_fold(local_solve(z_windows(field_in, 10), stiff_line, mass_line, eigen_basis, eigen_vals))

    def operate(direction):
        return face_fold(face_fold(ref_halo(per_column(element_sum, direction)), 2), 3)

    def precondition(current):
        smooth = spread_fold(spread_fold(ref_halo(per_column(schwarz_sum, current)), 2), 3)
        coarse_in = lax.optimization_barrier(jnp.sum(current[:, :, 2:8, 2:8], axis=(2, 3))).reshape(N_GX * N_GY * C_DEV, -1).sum(axis=1)
        coarse_y = jnp.dot(coarse_in, coarse_factor, precision=exact_mode)
        coarse_out = jnp.dot(coarse_factor, coarse_y, precision=exact_mode).reshape(N_GX, N_GY, C_DEV, 1)
        coarse_line = jnp.broadcast_to(coarse_out, (N_GX, N_GY, C_DEV, z_points // C_DEV)).reshape(N_GX, N_GY, 1, 1, z_points)
        coarse_plate = jnp.pad(jnp.broadcast_to(coarse_line, (N_GX, N_GY, 6, 6, z_points)), ((0, 0), (0, 0), (1, 1), (1, 1), (0, 0)))
        return smooth + coarse_plate
    padded = jnp.pad(blocks, ((0, 0), (0, 0), (0, 1), (0, 1), (0, 0)))
    current = face_fold(face_fold(ref_halo(padded), 2), 3)
    solution = jnp.zeros(blocks.shape, jnp.float32)
    smooth = precondition(current)
    direction = smooth
    rho_now = jnp.sum(current[:, :, 1:8, 1:8] * smooth[:, :, :7, :7])
    for iteration in range(ITERS):
        applied = operate(direction)
        step_len = rho_now / jnp.sum(direction[:, :, :7, :7] * applied[:, :, 1:8, 1:8])
        solution = solution + step_len * direction[:, :, :7, :7]
        current = current - step_len * applied
        if iteration + 1 < ITERS:
            smooth = precondition(current)
            rho_next = jnp.sum(current[:, :, 1:8, 1:8] * smooth[:, :, :7, :7])
            direction = smooth + rho_next / rho_now * direction
            rho_now = rho_next
    solution_out = solution.transpose(0, 2, 1, 3, 4).reshape(NX, NY, NZ)
    residual_out = current[:, :, 1:8, 1:8].transpose(0, 2, 1, 3, 4).reshape(NX, NY, NZ)
    return (solution_out, residual_out)
```

```python
import math

import jax
import jax.numpy as jnp
import numpy as np
from jax import lax
from jax.experimental import pallas as pl
from jax.experimental.pallas import tpu as pltpu
from jax.sharding import PartitionSpec as P

HI = lax.Precision.HIGHEST
LANES = 128


def legendre_pair(position, degree):
    p_prev = 1.0
    p_now = position
    for order in range(2, degree + 1):
        p_next = ((2 * order - 1) * position * p_now - (order - 1) * p_prev) / order
        p_prev = p_now
        p_now = p_next
    return (p_now, p_prev)


def jacobi_eigen(matrix):
    size_n = matrix.shape[0]
    current = np.array(matrix)
    vectors = np.eye(size_n)
    for sweep in range(20):
        for row_p in range(size_n - 1):
            for row_q in range(row_p + 1, size_n):
                off_value = current[row_p, row_q]
                if abs(off_value) > 1e-300:
                    theta = (current[row_q, row_q] - current[row_p, row_p]) / (2.0 * off_value)
                    sign_t = 1.0 if theta >= 0.0 else -1.0
                    tangent = sign_t / (abs(theta) + math.sqrt(theta * theta + 1.0))
                    cosine = 1.0 / math.sqrt(tangent * tangent + 1.0)
                    sine = tangent * cosine
                    rotation = np.eye(size_n)
                    rotation[row_p, row_p] = cosine
                    rotation[row_q, row_q] = cosine
                    rotation[row_p, row_q] = sine
                    rotation[row_q, row_p] = -sine
                    current = rotation.T @ current @ rotation
                    vectors = vectors @ rotation
    return (np.array([current[idx, idx] for idx in range(size_n)]), vectors)


def gll_tables():
    degree = 7
    guesses = [
        -0.8717401485096066,
        -0.5917001814331423,
        -0.2092992179024789,
        0.2092992179024789,
        0.5917001814331423,
        0.8717401485096066,
    ]
    interior = []
    for guess in guesses:
        position = guess
        for newton in range(30):
            p_now, p_prev = legendre_pair(position, degree)
            first = degree * (position * p_now - p_prev) / (position * position - 1.0)
            second = (2.0 * position * first - degree * (degree + 1) * p_now) / (
                1.0 - position * position
            )
            position = position - first / second
        interior.append(position)
    points = np.array([-1.0] + interior + [1.0])
    values = np.array([legendre_pair(float(pt), degree)[0] for pt in points])
    weights = 2.0 / (degree * (degree + 1) * values**2)
    deriv_mat = np.zeros((8, 8))
    for left_idx in range(8):
        for right_idx in range(8):
            if left_idx != right_idx:
                deriv_mat[left_idx, right_idx] = values[left_idx] / (
                    values[right_idx] * (points[left_idx] - points[right_idx])
                )
    deriv_mat[0, 0] = -degree * (degree + 1) / 4.0
    deriv_mat[7, 7] = degree * (degree + 1) / 4.0
    stiffness = deriv_mat.T @ (weights[:, None] * deriv_mat)
    ext_stiff = np.zeros((10, 10))
    ext_stiff[1:9, 1:9] += stiffness
    ext_stiff[0:2, 0:2] += stiffness[6:8, 6:8]
    ext_stiff[8:10, 8:10] += stiffness[0:2, 0:2]
    ext_mass = np.zeros(10)
    ext_mass[1:9] += weights
    ext_mass[0:2] += weights[6:8]
    ext_mass[8:10] += weights[0:2]
    inv_root = 1.0 / np.sqrt(ext_mass)
    eigen_vals, eigen_vecs = jacobi_eigen(inv_root[:, None] * ext_stiff * inv_root[None, :])
    eigen_basis = inv_root[:, None] * eigen_vecs
    return (stiffness, weights, eigen_basis, eigen_vals)


def dot(left, right):
    return jnp.dot(left, right, precision=HI, preferred_element_type=jnp.float32)


def make_tables(ez, c_dev):
    stiffness, weights, basis, vals = gll_tables()
    stiffness = stiffness.astype(np.float32).astype(np.float64)
    weights = weights.astype(np.float32).astype(np.float64)
    basis = basis.astype(np.float32).astype(np.float64)
    vals = vals.astype(np.float32).astype(np.float64)
    nz = 7 * ez
    span = nz // c_dev
    f32 = lambda table: np.asarray(table, np.float32)

    qq = np.zeros((10, 16, 10, 16))
    qq[:, :10, :, :10] = np.einsum("ia,jb->ijab", basis, basis)
    qq = qq.reshape(160, 160)
    lam_ab = np.ones((10, 16))
    lam_ab[:, :10] = vals[:, None] + vals[None, :]
    lam_c = np.repeat(vals, ez)[None]
    zf = np.zeros((nz, 10, ez))
    g8 = np.zeros((nz, 8, ez))
    zk = np.zeros((nz, 8, ez))
    for elem in range(ez):
        for k in range(10):
            zf[(7 * elem - 1 + k) % nz, :, elem] += basis[k]
        for k in range(8):
            g8[(7 * elem + k) % nz, k, elem] += 1.0
            zk[(7 * elem + k) % nz, :, elem] += stiffness[:, k]
    zf, g8, zk = zf.reshape(nz, -1), g8.reshape(nz, -1), zk.reshape(nz, -1)
    diag = np.diag(weights)
    kk = np.einsum("ai,bj->abij", stiffness, diag) + np.einsum("ai,bj->abij", diag, stiffness)
    kk = kk.reshape(64, 64)
    ww = np.outer(weights, weights).reshape(64, 1)
    inner = np.zeros((8, 8))
    inner[1:7, 1:7] = 1.0
    owned = np.zeros((8, 8))
    owned[:7, :7] = 1.0
    plate = inner.reshape(64, 1)
    first = np.array([1.0] * 7 + [0.0])
    last = 1.0 - first
    k_parts = {}
    m_parts = {}
    for name, left, right in (("11", first, first), ("12", first, last), ("22", last, last)):
        wz = float(np.sum(left * weights * right))
        kz = float(left @ stiffness @ right)
        k_parts[name] = float((plate.T @ kk @ plate).item()) * wz + float(np.sum(plate * ww)) * kz
        m_parts[name] = float(np.sum(plate * ww)) * wz
    elems = np.arange(ez)
    per = ez // c_dev
    r1 = (elems[None, :] // per == np.arange(c_dev)[:, None]).astype(np.float64)
    r2 = (((elems[None, :] + 1) % ez) // per == np.arange(c_dev)[:, None]).astype(np.float64)
    wide = LANES // c_dev
    zc = (np.arange(nz)[:, None] // span == np.arange(c_dev)[None, :]).astype(np.float64)
    return dict(
        qq=f32(qq), qqt=f32(qq.T), zf=f32(zf), zft=f32(zf.T), lam_ab=f32(lam_ab.reshape(160, 1)), lam_c=f32(lam_c),
        rep10=f32(np.tile(np.eye(ez), (1, 10))), rep8=f32(np.tile(np.eye(ez), (1, 8))),
        g8=f32(g8), g8t=f32(g8.T), zk=f32(zk), kk=f32(kk), ww=f32(ww), wz=f32(np.repeat(weights, ez)[None]),
        inner=f32(plate), owned=f32(owned.reshape(64, 1)),
        r1=f32(r1), r2=f32(r2), r1t=f32(np.tile(r1.T, (1, wide))), r2t=f32(np.tile(r2.T, (1, wide))),
        zct=f32(np.tile(zc, (1, wide))), eye=f32(np.eye(LANES)),
        zl=f32(np.tile(zc.T, (wide, 1))),
        k_parts=k_parts, m_parts=m_parts,
    )


def run(kernel, outs, *args, scratch=()):
    shapes = [jax.ShapeDtypeStruct(shape, jnp.float32) for shape in outs]
    size = sum(math.prod(s) for s in outs) + sum(math.prod(a.shape) for a in args)
    return pl.pallas_call(
        kernel,
        out_shape=shapes,
        in_specs=[pl.BlockSpec(memory_space=pltpu.VMEM)] * len(args),
        out_specs=[pl.BlockSpec(memory_space=pltpu.VMEM)] * len(outs),
        scratch_shapes=[pltpu.VMEM(shape, jnp.float32) for shape in scratch],
        cost_estimate=pl.CostEstimate(flops=2 * 6 * 160 * 240 * 168, bytes_accessed=4 * size, transcendentals=0),
    )(*args)


def total(value):
    return jnp.sum(jnp.sum(value, axis=1, keepdims=True), axis=0, keepdims=True)


def total_row(row):
    return jnp.sum(row, axis=1, keepdims=True)


def as_col(row, eye):
    return jnp.sum(eye * row, axis=1, keepdims=True)


def as_row(col, eye):
    return jnp.sum(eye * col, axis=0, keepdims=True)


def lane_put(values):
    lane = lax.broadcasted_iota(jnp.int32, (1, LANES), 1)
    row = jnp.zeros((1, LANES), jnp.float32)
    for spot, value in enumerate(values):
        row = jnp.where(lane == spot, value, row)
    return row


def lane_get(row, spot):
    lane = lax.broadcasted_iota(jnp.int32, row.shape, 1)
    return jnp.sum(jnp.where(lane == spot, row, 0.0), axis=1, keepdims=True)


def rows_tile(rows):
    spot = lax.broadcasted_iota(jnp.int32, (8, LANES), 0)
    tile = jnp.zeros((8, LANES), jnp.float32)
    for place, row in enumerate(rows):
        tile = jnp.where(spot == place, row, tile)
    return tile


def first_kernel(k_parts, m_parts, width, b_ref, k_ref, m_ref, x_ref, sel_ref, r1_ref, r2_ref, r1t_ref, r2t_ref, zct_ref, out_ref):
    k, m = k_ref[...], m_ref[...]
    e11, e12, e22 = (k * k_parts[name] + m * m_parts[name] for name in ("11", "12", "22"))
    r1, r2 = r1_ref[...], r2_ref[...]
    sel = sel_ref[...]
    small = (dot(r1 * e11 + r2 * e12, r1t_ref[...]) + dot(r1 * e12 + r2 * e22, r2t_ref[...])) * sel
    acc = b_ref[1]
    for x in range(2, 7):
        acc = acc + b_ref[x]
    line = jnp.sum(acc[1:7], axis=0, keepdims=True)
    rc = dot(line, zct_ref[...]) * sel
    rc_tile = rows_tile([rc])
    for peer in range(out_ref.shape[0]):
        out_ref[peer, :, :width] = x_ref[:, peer * width : (peer + 1) * width]
        out_ref[peer, :, width : width + LANES] = small
        out_ref[peer, :, width + LANES :] = rc_tile


def split_group(xl_ref, width):
    rows = xl_ref.shape[0] * xl_ref.shape[1]
    wide = xl_ref[...].reshape(rows, xl_ref.shape[2])
    rc = jnp.sum(wide[:, width + LANES :], axis=0, keepdims=True)
    return wide[:, :width], wide[:, width : width + LANES], rc


def spread(out_ref, row):
    out_ref[...] = jnp.broadcast_to(row[None], out_ref.shape)


def coarse_in_kernel(width, xl_ref, eye_ref, out_ref):
    factor, _, rc = split_group(xl_ref, width)
    rows = factor.shape[0]
    rc_col = as_col(rc, eye_ref[:rows])
    part = jnp.sum(rc_col * factor, axis=0, keepdims=True)
    spread(out_ref, jnp.concatenate([part, jnp.zeros((1, LANES), jnp.float32)], axis=1))


def coarse_out_kernel(width, sums_ref, xl_ref, eye_ref, h_ref, out_ref):
    factor, _, _ = split_group(xl_ref, width)
    rows = factor.shape[0]
    sums = jnp.sum(sums_ref[...], axis=0)
    part = jnp.sum(factor * sums[:, :width], axis=1, keepdims=True)
    x_part = as_row(part, eye_ref[:rows])
    spot = lax.broadcasted_iota(jnp.int32, (8, LANES), 0)
    tile = jnp.where(spot == 0, x_part, h_ref[...])
    out_ref[...] = jnp.broadcast_to(tile[None], out_ref.shape)


def coarse_mid_kernel(width, got_ref, xl_ref, eye_ref, out_ref, x_ref):
    factor, small, rc = split_group(xl_ref, width)
    rows = factor.shape[0]
    eye = eye_ref[:rows]
    got = jnp.sum(got_ref[...], axis=0)
    x0, h, scal = got[0:1], got[1:2], got[2:3]
    rc1_col = jnp.sum(small * x0 + eye * h, axis=1, keepdims=True)
    rc1 = as_row(rc1_col, eye)
    part = jnp.sum(rc1_col * factor, axis=0, keepdims=True)
    rho = lane_get(scal, 0) + total_row(rc * x0)
    den = lane_get(scal, 1) + total_row(x0 * (h + rc1))
    spread(out_ref, jnp.concatenate([part, lane_put([rho, den])], axis=1))
    x_ref[...] = x0


def pair_kernel(width, sums_ref, xl_ref, eye_ref, b_ref, q_ref, u_ref, au_ref, s_ref, as_ref, inner_ref, owned_ref, zct_ref, sel_ref,
                out_ref, scal_ref, r_ref, qo_ref):
    factor, _, _ = split_group(xl_ref, width)
    rows = factor.shape[0]
    sums = jnp.sum(sums_ref[...], axis=0)
    part = jnp.sum(factor * sums[:, :width], axis=1, keepdims=True)
    x_part = as_row(part, eye_ref[:rows])
    scal = sums[:, width:]
    rho, den = lane_get(scal, 0), lane_get(scal, 1)
    step = rho / den
    for x in range(7):
        qo = q_ref[x + 1, 1:8]
        qo_ref[x, :7] = qo
        r_ref[x, :7] = b_ref[x] - step * qo
        qo_ref[x, 7:] = jnp.zeros_like(qo_ref[x, 7:])
        r_ref[x, 7:] = jnp.zeros_like(r_ref[x, 7:])
    qo_ref[7] = jnp.zeros_like(qo_ref[7])
    r_ref[7] = jnp.zeros_like(r_ref[7])
    nz = b_ref.shape[2]
    flat = lambda ref: ref[...].reshape(64, nz)
    resid = flat(r_ref)
    t = flat(u_ref) - step * flat(s_ref)
    at = flat(au_ref) - step * flat(as_ref)
    inner = inner_ref[...]
    wr = dot(jnp.sum(inner * resid, axis=0, keepdims=True), zct_ref[...]) * sel_ref[...]
    wt = dot(jnp.sum(inner * at, axis=0, keepdims=True), zct_ref[...]) * sel_ref[...]
    tile = rows_tile([x_part, wr, wt, lane_put([total(resid * t), total(t * at)])])
    out_ref[...] = jnp.broadcast_to(tile[None], out_ref.shape)
    scal_ref[...] = lane_put([rho, den])


def last_in_kernel(width, got_ref, xl_ref, x0_ref, scal_ref, eye_ref, out_ref, x_ref):
    _, small, _ = split_group(xl_ref, width)
    eye = eye_ref[: small.shape[0]]
    got = jnp.sum(got_ref[...], axis=0)
    x1, wr, wt, scal = got[0:1], got[1:2], got[2:3], got[3:4]
    step = lane_get(scal_ref[...], 0) / lane_get(scal_ref[...], 1)
    c = x0_ref[...] - step * x1
    tc = as_row(jnp.sum(small * c, axis=1, keepdims=True), eye)
    rho1 = lane_get(scal, 0) + total_row(wr * c)
    en1 = lane_get(scal, 1) + total_row(c * (2.0 * wt + tc))
    spread(out_ref, lane_put([rho1, en1]))
    x_ref[...] = x1


def final_kernel(sums_ref, scal_ref, p_ref, w_ref, r_ref, qo_ref, v_ref, vl_ref, sol_ref, res_ref):
    got = jnp.sum(sums_ref[...], axis=0)
    rho1, en1 = lane_get(got, 0), lane_get(got, 1)
    rho, den = lane_get(scal_ref[...], 0), lane_get(scal_ref[...], 1)
    step = rho / den
    beta = rho1 / rho
    step1 = rho1 / (en1 - beta * rho1 / step)
    p_mult = step + step1 * (1.0 + beta)
    w_mult = step1 * step
    q_mult = step1 * (1.0 + beta)
    for x in range(7):
        sol_ref[x] = p_mult * p_ref[x, :7] - w_mult * w_ref[x, :7]
        top = w_mult * vl_ref[x]
        res_ref[x] = r_ref[x, :7] - q_mult * qo_ref[x, :7] + w_mult * v_ref[x, :7]
        res_ref[x, 0:1] = res_ref[x, 0:1] + top


def solve(block, k, m, rep10, lam_ab, lam_c, qq, qqt, zf, zft):
    den = dot(k, rep10) * (lam_ab + lam_c) + dot(m, rep10)
    spectral = dot(dot(qqt, block), zf) / den
    return dot(dot(qq, spectral), zft)


SOLVE = ("rep10", "lam_ab", "lam_c", "qq", "qqt", "zf", "zft")
APPLY = ("rep8", "wz", "g8", "g8t", "zk", "kk", "ww")


def apply(block, k, m, rep8, wz, g8, g8t, zk, kk, ww):
    k_line, m_line = dot(k, rep8), dot(m, rep8) * wz
    spread_u = dot(block, g8)
    out = (k_line * wz) * dot(kk, spread_u) + ww * (k_line * dot(block, zk) + m_line * spread_u)
    return dot(out, g8t)


def schwarz_b_kernel(bx_ref, yl_ref, yh_ref, k_ref, m_ref, *refs):
    consts, (out_ref, hi_ref, lo_ref, scr) = refs[:-4], refs[-4:]
    scr[...] = jnp.zeros_like(scr)
    scr[:, 1:8] = bx_ref[...]
    scr[:, 0:1] = yl_ref[...]
    scr[:, 8:10] = yh_ref[...]
    schwarz_tail(scr, k_ref, m_ref, consts, out_ref, hi_ref, lo_ref)


def schwarz_q_kernel(qx_ref, yl_ref, yh_ref, k_ref, m_ref, *refs):
    consts, (q_ref, out_ref, hi_ref, lo_ref) = refs[:-4], refs[-4:]
    q_ref[...] = jnp.zeros_like(q_ref)
    q_ref[:, 1:9] = qx_ref[...]
    q_ref[:, 0:1] = yl_ref[:, 0:1]
    q_ref[:, 1:2] = q_ref[:, 1:2] + yl_ref[:, 1:2]
    q_ref[:, 8:9] = q_ref[:, 8:9] + yh_ref[:, 0:1]
    q_ref[:, 9:10] = yh_ref[:, 1:2]
    schwarz_tail(q_ref, k_ref, m_ref, consts, out_ref, hi_ref, lo_ref)


def schwarz_tail(src, k_ref, m_ref, consts, out_ref, hi_ref, lo_ref):
    nz = src.shape[2]
    block = solve(src[...].reshape(160, nz), k_ref[...], m_ref[...], *(ref[...] for ref in consts))
    block = block.reshape(10, 16, nz)
    out_ref[...] = block
    hi_ref[...] = block[8:10]
    lo_ref[...] = block[0:2]


def fold_s_kernel(y_ref, xl_ref, xh_ref, out_ref, hi_ref, lo_ref):
    out_ref[0:2] = y_ref[1:3] + xl_ref[...]
    out_ref[2:6] = y_ref[3:7]
    out_ref[6:8] = y_ref[7:9] + xh_ref[...]
    hi_ref[...] = out_ref[:, 8:10]
    lo_ref[...] = out_ref[:, 0:2]


def fold_a_kernel(q_ref, xl_ref, xh_ref, out_ref, hi_ref, lo_ref):
    out_ref[0] = xl_ref[0]
    out_ref[1] = q_ref[0] + xl_ref[1]
    out_ref[2:8] = q_ref[1:7]
    out_ref[8] = q_ref[7] + xh_ref[0]
    out_ref[9] = xh_ref[1]
    hi_ref[...] = out_ref[:, 6:8]
    lo_ref[...] = out_ref[:, 0:2]


def fold_b_kernel(b_ref, xl_ref, xh_ref, out_ref, hi_ref, lo_ref):
    out_ref[0:1] = xl_ref[...]
    out_ref[1:8] = b_ref[...]
    out_ref[8:10] = xh_ref[...]
    hi_ref[...] = out_ref[:, 6:7]
    lo_ref[...] = out_ref[:, 0:2]


def fold_v_kernel(v_ref, xl_ref, out_ref, hi_ref):
    out_ref[...] = v_ref[0:7]
    out_ref[0] = out_ref[0] + xl_ref[0]
    hi_ref[...] = out_ref[:, 7:8]


def gather_s(u_ref, y_ref, yl_ref, yh_ref):
    u_ref[...] = y_ref[:, 1:9]
    u_ref[:, 0:2] = u_ref[:, 0:2] + yl_ref[...]
    u_ref[:, 6:8] = u_ref[:, 6:8] + yh_ref[...]


def apply_u_kernel(b_ref, y_ref, yl_ref, yh_ref, k_ref, m_ref, inner_ref, zct_ref, sel_ref, *refs):
    consts, (u_ref, au_ref, h_ref) = refs[:-3], refs[-3:]
    nz = u_ref.shape[2]
    gather_s(u_ref, y_ref, yl_ref, yh_ref)
    u = u_ref[...].reshape(64, nz)
    au = apply(u, k_ref[...], m_ref[...], *(ref[...] for ref in consts))
    au_ref[...] = au.reshape(8, 8, nz)
    h = dot(jnp.sum(inner_ref[...] * au, axis=0, keepdims=True), zct_ref[...]) * sel_ref[...]
    acc = b_ref[0] * u_ref[0, :7]
    for x in range(1, 7):
        acc = acc + b_ref[x] * u_ref[x, :7]
    h_ref[...] = rows_tile([jnp.zeros((1, LANES), jnp.float32), h, lane_put([total(acc), total(u * au)])])


def apply_s_kernel(y_ref, yl_ref, yh_ref, k_ref, m_ref, *refs):
    consts, (s_ref, as_ref) = refs[:-2], refs[-2:]
    nz = s_ref.shape[2]
    gather_s(s_ref, y_ref, yl_ref, yh_ref)
    out = apply(s_ref[...].reshape(64, nz), k_ref[...], m_ref[...], *(ref[...] for ref in consts))
    as_ref[...] = out.reshape(8, 8, nz)


def apply_p_kernel(u_ref, x_ref, k_ref, m_ref, inner_ref, zl_ref, sel_ref, eye_ref, *refs):
    consts, (p_ref, q_ref, hi_ref, lo_ref) = refs[:-4], refs[-4:]
    nz = u_ref.shape[2]
    col = as_col(x_ref[...] * sel_ref[...], eye_ref[...])
    line = jnp.sum(col * zl_ref[...], axis=0, keepdims=True)
    p = u_ref[...].reshape(64, nz) + inner_ref[...] * line
    p_ref[...] = p.reshape(8, 8, nz)
    out = apply(p, k_ref[...], m_ref[...], *(ref[...] for ref in consts)).reshape(8, 8, nz)
    q_ref[...] = out
    hi_ref[...] = out[8 - hi_ref.shape[0] :]
    lo_ref[...] = out[0:2]


def shift(value, axis, step):
    count = lax.axis_size(axis)
    return lax.ppermute(value, axis, [(i, (i + step) % count) for i in range(count)])


def local(right_side, stiff_coef, mass_coef, coarse_factor):
    nz = right_side.shape[2]
    c_dev, n_coarse = coarse_factor.shape
    ez = stiff_coef.shape[2]
    n_gx, n_gy = lax.axis_size("gx"), lax.axis_size("gy")
    width = n_coarse // n_gx
    tab = {name: jnp.asarray(value) if isinstance(value, np.ndarray) else value for name, value in make_tables(ez, c_dev).items()}
    k = stiff_coef.reshape(1, ez)
    m = mass_coef.reshape(1, ez)
    b = right_side
    sel = (jnp.arange(LANES)[None] // c_dev == lax.axis_index("gx")).astype(jnp.float32)
    solve_tab = [tab[name] for name in SOLVE]
    apply_tab = [tab[name] for name in APPLY]
    inner, owned, zct, zl, eye = (tab[name] for name in ("inner", "owned", "zct", "zl", "eye"))

    def kernel(fn, *fixed):
        def call(*refs):
            return fn(*fixed, *refs)

        call.__name__ = fn.__name__
        return call

    def swap_gx(value):
        return lax.all_to_all(value, "gx", 0, 0)

    def swap_gy(value):
        return lax.all_to_all(value, "gy", 0, 0)

    group = (n_gx, c_dev, LANES)
    (pay,) = run(kernel(first_kernel, tab["k_parts"], tab["m_parts"], width), [(n_gx, c_dev, width + 2 * LANES)],
                 b, k, m, coarse_factor, sel, tab["r1"], tab["r2"], tab["r1t"], tab["r2t"], zct)
    b_low, b_high = shift(b[6:7], "gx", 1), shift(b[0:2], "gx", -1)
    xl = swap_gx(pay)

    (pay,) = run(kernel(coarse_in_kernel, width), [(n_gy, 1, width + LANES)], xl, eye)
    sums = swap_gy(pay)

    bx, hi, lo = run(fold_b_kernel, [(10, 7, nz), (10, 1, nz), (10, 2, nz)], b, b_low, b_high)
    y_low, y_high = shift(hi, "gy", 1), shift(lo, "gy", -1)

    strips = [(2, 16, nz), (2, 16, nz)]
    sides = [(8, 2, nz), (8, 2, nz)]
    y, hi, lo = run(schwarz_b_kernel, [(10, 16, nz)] + strips, bx, y_low, y_high, k, m, *solve_tab, scratch=[(10, 16, nz)])
    x_low, x_high = shift(hi, "gx", 1), shift(lo, "gx", -1)
    y, hi, lo = run(fold_s_kernel, [(8, 16, nz)] + sides, y, x_low, x_high)
    y_low, y_high = shift(hi, "gy", 1), shift(lo, "gy", -1)
    cube = (8, 8, nz)
    u, au, h = run(apply_u_kernel, [cube, cube, (8, LANES)], b, y, y_low, y_high, k, m, inner, zct, sel, *apply_tab)

    (pay,) = run(kernel(coarse_out_kernel, width), [group], sums, xl, eye, h)
    got = swap_gx(pay)
    pay, x0 = run(kernel(coarse_mid_kernel, width), [(n_gy, 1, width + LANES), (1, LANES)], got, xl, eye)
    sums = swap_gy(pay)

    p, q, hi, lo = run(apply_p_kernel, [cube, cube, (2, 8, nz), (2, 8, nz)], u, x0, k, m, inner, zl, sel, eye, *apply_tab)
    x_low, x_high = shift(hi, "gx", 1), shift(lo, "gx", -1)
    qx, hi, lo = run(fold_a_kernel, [(10, 8, nz), (10, 2, nz), (10, 2, nz)], q, x_low, x_high)
    y_low, y_high = shift(hi, "gy", 1), shift(lo, "gy", -1)
    q, y, hi, lo = run(schwarz_q_kernel, [(10, 16, nz), (10, 16, nz)] + strips, qx, y_low, y_high, k, m, *solve_tab)
    x_low, x_high = shift(hi, "gx", 1), shift(lo, "gx", -1)
    y, hi, lo = run(fold_s_kernel, [(8, 16, nz)] + sides, y, x_low, x_high)
    y_low, y_high = shift(hi, "gy", 1), shift(lo, "gy", -1)
    s, a_s = run(apply_s_kernel, [cube, cube], y, y_low, y_high, k, m, *apply_tab)

    pay, scal, resid, q_own = run(kernel(pair_kernel, width), [group, (1, LANES), cube, cube],
                                  sums, xl, eye, b, q, u, au, s, a_s, inner, owned, zct, sel)
    got = swap_gx(pay)
    pay, x1 = run(kernel(last_in_kernel, width), [(n_gy, 1, LANES), (1, LANES)], got, xl, x0, scal, eye)
    sums = swap_gy(pay)

    w, v, hi, _ = run(apply_p_kernel, [cube, cube, (1, 8, nz), (2, 8, nz)], s, x1, k, m, inner, zl, sel, eye, *apply_tab)
    x_low = shift(hi, "gx", 1)
    v, hi = run(fold_v_kernel, [(7, 8, nz), (7, 1, nz)], v, x_low)
    y_low = shift(hi, "gy", 1)
    sol, res = run(final_kernel, [(7, 7, nz), (7, 7, nz)], sums, scal, p, w, resid, q_own, v, y_low)
    return sol, res


def solution(mesh):
    placed = (P("gx", "gy", None), P("gx", "gy", None), P("gx", "gy", None), P(("gx", "gy"), None))
    return jax.shard_map(
        local,
        mesh=mesh,
        in_specs=placed,
        out_specs=(P("gx", "gy", None), P("gx", "gy", None)),
        check_vma=False,
    )
```

```python
import math

import jax
import jax.numpy as jnp
import numpy as np
from jax import lax
from jax.experimental import pallas as pl
from jax.experimental.pallas import tpu as pltpu
from jax.sharding import PartitionSpec as P

HI = lax.Precision.HIGHEST
LANES = 128


def legendre_pair(position, degree):
    p_prev = 1.0
    p_now = position
    for order in range(2, degree + 1):
        p_next = ((2 * order - 1) * position * p_now - (order - 1) * p_prev) / order
        p_prev = p_now
        p_now = p_next
    return (p_now, p_prev)


def jacobi_eigen(matrix):
    size_n = matrix.shape[0]
    current = np.array(matrix)
    vectors = np.eye(size_n)
    for sweep in range(20):
        for row_p in range(size_n - 1):
            for row_q in range(row_p + 1, size_n):
                off_value = current[row_p, row_q]
                if abs(off_value) > 1e-300:
                    theta = (current[row_q, row_q] - current[row_p, row_p]) / (2.0 * off_value)
                    sign_t = 1.0 if theta >= 0.0 else -1.0
                    tangent = sign_t / (abs(theta) + math.sqrt(theta * theta + 1.0))
                    cosine = 1.0 / math.sqrt(tangent * tangent + 1.0)
                    sine = tangent * cosine
                    rotation = np.eye(size_n)
                    rotation[row_p, row_p] = cosine
                    rotation[row_q, row_q] = cosine
                    rotation[row_p, row_q] = sine
                    rotation[row_q, row_p] = -sine
                    current = rotation.T @ current @ rotation
                    vectors = vectors @ rotation
    return (np.array([current[idx, idx] for idx in range(size_n)]), vectors)


def gll_tables():
    degree = 7
    guesses = [
        -0.8717401485096066,
        -0.5917001814331423,
        -0.2092992179024789,
        0.2092992179024789,
        0.5917001814331423,
        0.8717401485096066,
    ]
    interior = []
    for guess in guesses:
        position = guess
        for newton in range(30):
            p_now, p_prev = legendre_pair(position, degree)
            first = degree * (position * p_now - p_prev) / (position * position - 1.0)
            second = (2.0 * position * first - degree * (degree + 1) * p_now) / (
                1.0 - position * position
            )
            position = position - first / second
        interior.append(position)
    points = np.array([-1.0] + interior + [1.0])
    values = np.array([legendre_pair(float(pt), degree)[0] for pt in points])
    weights = 2.0 / (degree * (degree + 1) * values**2)
    deriv_mat = np.zeros((8, 8))
    for left_idx in range(8):
        for right_idx in range(8):
            if left_idx != right_idx:
                deriv_mat[left_idx, right_idx] = values[left_idx] / (
                    values[right_idx] * (points[left_idx] - points[right_idx])
                )
    deriv_mat[0, 0] = -degree * (degree + 1) / 4.0
    deriv_mat[7, 7] = degree * (degree + 1) / 4.0
    stiffness = deriv_mat.T @ (weights[:, None] * deriv_mat)
    ext_stiff = np.zeros((10, 10))
    ext_stiff[1:9, 1:9] += stiffness
    ext_stiff[0:2, 0:2] += stiffness[6:8, 6:8]
    ext_stiff[8:10, 8:10] += stiffness[0:2, 0:2]
    ext_mass = np.zeros(10)
    ext_mass[1:9] += weights
    ext_mass[0:2] += weights[6:8]
    ext_mass[8:10] += weights[0:2]
    inv_root = 1.0 / np.sqrt(ext_mass)
    eigen_vals, eigen_vecs = jacobi_eigen(inv_root[:, None] * ext_stiff * inv_root[None, :])
    eigen_basis = inv_root[:, None] * eigen_vecs
    return (stiffness, weights, eigen_basis, eigen_vals)


def dot(left, right):
    return jnp.dot(left, right, precision=HI, preferred_element_type=jnp.float32)


def make_tables(ez, c_dev):
    stiffness, weights, basis, vals = gll_tables()
    stiffness = stiffness.astype(np.float32).astype(np.float64)
    weights = weights.astype(np.float32).astype(np.float64)
    basis = basis.astype(np.float32).astype(np.float64)
    vals = vals.astype(np.float32).astype(np.float64)
    nz = 7 * ez
    span = nz // c_dev
    f32 = lambda table: np.asarray(table, np.float32)

    qq = np.zeros((10, 16, 10, 16))
    qq[:, :10, :, :10] = np.einsum("ia,jb->ijab", basis, basis)
    qq = qq.reshape(160, 160)
    lam_ab = np.ones((10, 16))
    lam_ab[:, :10] = vals[:, None] + vals[None, :]
    lam_c = np.repeat(vals, ez)[None]
    zf = np.zeros((nz, 10, ez))
    g8 = np.zeros((nz, 8, ez))
    zk = np.zeros((nz, 8, ez))
    for elem in range(ez):
        for k in range(10):
            zf[(7 * elem - 1 + k) % nz, :, elem] += basis[k]
        for k in range(8):
            g8[(7 * elem + k) % nz, k, elem] += 1.0
            zk[(7 * elem + k) % nz, :, elem] += stiffness[:, k]
    zf, g8, zk = zf.reshape(nz, -1), g8.reshape(nz, -1), zk.reshape(nz, -1)
    diag = np.diag(weights)
    kk = np.einsum("ai,bj->abij", stiffness, diag) + np.einsum("ai,bj->abij", diag, stiffness)
    kk = kk.reshape(64, 64)
    ww = np.outer(weights, weights).reshape(64, 1)
    inner = np.zeros((8, 8))
    inner[1:7, 1:7] = 1.0
    owned = np.zeros((8, 8))
    owned[:7, :7] = 1.0
    plate = inner.reshape(64, 1)
    first = np.array([1.0] * 7 + [0.0])
    last = 1.0 - first
    k_parts = {}
    m_parts = {}
    for name, left, right in (("11", first, first), ("12", first, last), ("22", last, last)):
        wz = float(np.sum(left * weights * right))
        kz = float(left @ stiffness @ right)
        k_parts[name] = float((plate.T @ kk @ plate).item()) * wz + float(np.sum(plate * ww)) * kz
        m_parts[name] = float(np.sum(plate * ww)) * wz
    elems = np.arange(ez)
    per = ez // c_dev
    r1 = (elems[None, :] // per == np.arange(c_dev)[:, None]).astype(np.float64)
    r2 = (((elems[None, :] + 1) % ez) // per == np.arange(c_dev)[:, None]).astype(np.float64)
    wide = LANES // c_dev
    zc = (np.arange(nz)[:, None] // span == np.arange(c_dev)[None, :]).astype(np.float64)
    return dict(
        qq=f32(qq), qqt=f32(qq.T), zf=f32(zf), zft=f32(zf.T), lam_ab=f32(lam_ab.reshape(160, 1)), lam_c=f32(lam_c),
        rep10=f32(np.tile(np.eye(ez), (1, 10))), rep8=f32(np.tile(np.eye(ez), (1, 8))),
        g8=f32(g8), g8t=f32(g8.T), zk=f32(zk), kk=f32(kk), ww=f32(ww), wz=f32(np.repeat(weights, ez)[None]),
        inner=f32(plate), owned=f32(owned.reshape(64, 1)),
        r1=f32(r1), r2=f32(r2), r1t=f32(np.tile(r1.T, (1, wide))), r2t=f32(np.tile(r2.T, (1, wide))),
        zct=f32(np.tile(zc, (1, wide))), eye=f32(np.eye(LANES)),
        zl=f32(np.tile(zc.T, (wide, 1))),
        k_parts=k_parts, m_parts=m_parts,
    )


def run(kernel, outs, *args, scratch=(), free=()):
    spaces = [pltpu.SMEM if a.dtype == jnp.int32 else pltpu.VMEM for a in args]
    size = sum(math.prod(s) for s in outs) + sum(math.prod(a.shape) for a in args)
    return pl.pallas_call(
        kernel,
        out_shape=[(jax.ShapeDtypeStruct if i in free else pltpu.VMEM)(shape, jnp.float32) for i, shape in enumerate(outs)],
        in_specs=[pl.BlockSpec(memory_space=space) for space in spaces],
        out_specs=[pl.BlockSpec(memory_space=pltpu.VMEM)] * len(outs),
        scratch_shapes=[pltpu.VMEM(shape, jnp.float32) for shape in scratch],
        compiler_params=pltpu.CompilerParams(vmem_limit_bytes=16 << 20),
        cost_estimate=pl.CostEstimate(flops=2 * 6 * 160 * 240 * 168, bytes_accessed=4 * size, transcendentals=0),
    )(*args)


def total(value):
    return jnp.sum(jnp.sum(value, axis=1, keepdims=True), axis=0, keepdims=True)


def total_row(row):
    return jnp.sum(row, axis=1, keepdims=True)


def as_col(row, eye):
    return jnp.sum(eye * row, axis=1, keepdims=True)


def as_row(col, eye):
    return jnp.sum(eye * col, axis=0, keepdims=True)


def lane_put(values):
    lane = lax.broadcasted_iota(jnp.int32, (1, LANES), 1)
    row = jnp.zeros((1, LANES), jnp.float32)
    for spot, value in enumerate(values):
        row = jnp.where(lane == spot, value, row)
    return row


def lane_get(row, spot):
    lane = lax.broadcasted_iota(jnp.int32, row.shape, 1)
    return jnp.sum(jnp.where(lane == spot, row, 0.0), axis=1, keepdims=True)


def lane_sel(spot):
    lane = lax.broadcasted_iota(jnp.int32, (1, LANES), 1)
    return jnp.where(lane // 8 == spot, 1.0, 0.0).astype(jnp.float32)


def rows_tile(rows):
    spot = lax.broadcasted_iota(jnp.int32, (8, LANES), 0)
    tile = jnp.zeros((8, LANES), jnp.float32)
    for place, row in enumerate(rows):
        tile = jnp.where(spot == place, row, tile)
    return tile


def first_kernel(k_parts, m_parts, width, idx_ref, b_ref, k_ref, m_ref, x_ref, r1_ref, r2_ref, r1t_ref, r2t_ref, zct_ref, out_ref, scr):
    k, m = k_ref[...], m_ref[...]
    e11, e12, e22 = (k * k_parts[name] + m * m_parts[name] for name in ("11", "12", "22"))
    r1, r2 = r1_ref[...], r2_ref[...]
    sel = lane_sel(idx_ref[0])
    small = (dot(r1 * e11 + r2 * e12, r1t_ref[...]) + dot(r1 * e12 + r2 * e22, r2t_ref[...])) * sel
    acc = b_ref[1]
    for x in range(2, 7):
        acc = acc + b_ref[x]
    line = jnp.sum(acc[1:7], axis=0, keepdims=True)
    rc = dot(line, zct_ref[...]) * sel
    nz, ez = b_ref.shape[2], k.shape[1]
    scr[...] = jnp.zeros_like(scr)
    scr[:, :LANES] = small
    scr[0:1, LANES : 2 * LANES] = rc
    scr[1:2, LANES : LANES + ez] = k
    scr[2:3, LANES : LANES + ez] = m
    for x in range(7):
        scr[:7, 2 * LANES + nz * x : 2 * LANES + nz * (x + 1)] = b_ref[x]
    for peer in range(out_ref.shape[0]):
        out_ref[peer, :, :width] = x_ref[:, peer * width : (peer + 1) * width]
        out_ref[peer, :, width:] = scr[...]


def split_group(xl_ref, width):
    rows = xl_ref.shape[0] * xl_ref.shape[1]
    small = xl_ref[:, :, width : width + LANES].reshape(rows, LANES)
    rc = jnp.sum(xl_ref[:, 0:1, width + LANES : width + 2 * LANES], axis=0)
    return xl_ref[:, :, :width].reshape(rows, width), small, rc


def spread(out_ref, row):
    out_ref[...] = jnp.broadcast_to(row[None], out_ref.shape)


def coarse_in_kernel(width, idx_ref, xl_ref, eye_ref, out_ref, bx_ref, hi_ref, lo_ref, k_ref, m_ref):
    factor, _, rc = split_group(xl_ref, width)
    rows = factor.shape[0]
    rc_col = as_col(rc, eye_ref[:rows])
    part = jnp.sum(rc_col * factor, axis=0, keepdims=True)
    spread(out_ref, jnp.concatenate([part, jnp.zeros((1, LANES), jnp.float32)], axis=1))
    count = xl_ref.shape[0]
    nz, ez = bx_ref.shape[2], k_ref.shape[1]
    base = width + 2 * LANES
    place = 0
    for apart in range(-4, 5):
        slot = lax.rem(idx_ref[0] + (apart + 2 * count), count)
        for x in (6,) if apart == -4 else (0, 1) if apart == 4 else range(7):
            bx_ref[place] = xl_ref[slot, :, base + nz * x : base + nz * (x + 1)]
            place += 1
        if -4 < apart < 4:
            k_ref[apart + 3 : apart + 4] = xl_ref[slot, 1:2, width + LANES : width + LANES + ez]
            m_ref[apart + 3 : apart + 4] = xl_ref[slot, 2:3, width + LANES : width + LANES + ez]
    k_ref[7:8] = k_ref[6:7]
    m_ref[7:8] = m_ref[6:7]
    hi_ref[...] = bx_ref[:, 6:7]
    lo_ref[...] = bx_ref[:, 0:2]


def coarse_out_kernel(width, sums_ref, xl_ref, eye_ref, h_ref, out_ref):
    factor, _, _ = split_group(xl_ref, width)
    rows = factor.shape[0]
    sums = jnp.sum(sums_ref[...], axis=0)
    part = jnp.sum(factor * sums[:, :width], axis=1, keepdims=True)
    x_part = as_row(part, eye_ref[:rows])
    spot = lax.broadcasted_iota(jnp.int32, (8, LANES), 0)
    tile = jnp.where(spot == 0, x_part, h_ref[...])
    out_ref[...] = jnp.broadcast_to(tile[None], out_ref.shape)


def coarse_mid_kernel(width, got_ref, xl_ref, eye_ref, out_ref, x_ref):
    factor, small, rc = split_group(xl_ref, width)
    rows = factor.shape[0]
    eye = eye_ref[:rows]
    got = jnp.sum(got_ref[...], axis=0)
    x0, h, scal = got[0:1], got[1:2], got[2:3]
    rc1_col = jnp.sum(small * x0 + eye * h, axis=1, keepdims=True)
    rc1 = as_row(rc1_col, eye)
    part = jnp.sum(rc1_col * factor, axis=0, keepdims=True)
    rho = lane_get(scal, 0) + total_row(rc * x0)
    den = lane_get(scal, 1) + total_row(x0 * (h + rc1))
    spread(out_ref, jnp.concatenate([part, lane_put([rho, den])], axis=1))
    x_ref[...] = x0


def pair_kernel(width, idx_ref, sums_ref, xl_ref, eye_ref, b_ref, q_ref, u_ref, au_ref, s_ref, as_ref, inner_ref, zct_ref,
                out_ref, scal_ref, r_ref):
    factor, _, _ = split_group(xl_ref, width)
    rows = factor.shape[0]
    sums = jnp.sum(sums_ref[...], axis=0)
    part = jnp.sum(factor * sums[:, :width], axis=1, keepdims=True)
    x_part = as_row(part, eye_ref[:rows])
    scal = sums[:, width:]
    rho, den = lane_get(scal, 0), lane_get(scal, 1)
    step = rho / den
    sel = lane_sel(idx_ref[0])
    r_ref[...] = jnp.zeros_like(r_ref)
    for x in range(7):
        r_ref[x, :7] = b_ref[x] - step * q_ref[x, :7]
    nz = b_ref.shape[2]
    flat = lambda ref: ref[...].reshape(64, nz)
    resid = flat(r_ref)
    t = flat(u_ref) - step * flat(s_ref)
    at = flat(au_ref) - step * flat(as_ref)
    inner = inner_ref[...]
    wr = dot(jnp.sum(inner * resid, axis=0, keepdims=True), zct_ref[...]) * sel
    wt = dot(jnp.sum(inner * at, axis=0, keepdims=True), zct_ref[...]) * sel
    tile = rows_tile([x_part, wr, wt, lane_put([total(resid * t), total(t * at)])])
    out_ref[...] = jnp.broadcast_to(tile[None], out_ref.shape)
    scal_ref[...] = lane_put([rho, den])


def last_in_kernel(width, got_ref, xl_ref, x0_ref, scal_ref, eye_ref, out_ref, x_ref):
    _, small, _ = split_group(xl_ref, width)
    eye = eye_ref[: small.shape[0]]
    got = jnp.sum(got_ref[...], axis=0)
    x1, wr, wt, scal = got[0:1], got[1:2], got[2:3], got[3:4]
    step = lane_get(scal_ref[...], 0) / lane_get(scal_ref[...], 1)
    c = x0_ref[...] - step * x1
    tc = as_row(jnp.sum(small * c, axis=1, keepdims=True), eye)
    rho1 = lane_get(scal, 0) + total_row(wr * c)
    en1 = lane_get(scal, 1) + total_row(c * (2.0 * wt + tc))
    spread(out_ref, lane_put([rho1, en1]))
    x_ref[...] = x1


def final_kernel(sums_ref, scal_ref, p_ref, w_ref, r_ref, qo_ref, v_ref, vl_ref, sol_ref, res_ref):
    got = jnp.sum(sums_ref[...], axis=0)
    rho1, en1 = lane_get(got, 0), lane_get(got, 1)
    rho, den = lane_get(scal_ref[...], 0), lane_get(scal_ref[...], 1)
    step = rho / den
    beta = rho1 / rho
    step1 = rho1 / (en1 - beta * rho1 / step)
    p_mult = step + step1 * (1.0 + beta)
    w_mult = step1 * step
    q_mult = step1 * (1.0 + beta)
    for x in range(7):
        sol_ref[x] = p_mult * p_ref[x, :7] - w_mult * w_ref[x, :7]
        top = w_mult * vl_ref[x]
        res_ref[x] = r_ref[x, :7] - q_mult * qo_ref[x, :7] + w_mult * v_ref[x, :7]
        res_ref[x, 0:1] = res_ref[x, 0:1] + top


SOLVE = ("rep10", "lam_ab", "lam_c", "qq", "qqt", "zf", "zft")
APPLY = ("rep8", "wz", "g8", "g8t", "zk", "kk", "ww")


def apply(block, k, m, rep8, wz, g8, g8t, zk, kk, ww):
    k_line, m_line = dot(k, rep8), dot(m, rep8) * wz
    spread_u = dot(block, g8)
    out = (k_line * wz) * dot(kk, spread_u) + ww * (k_line * dot(block, zk) + m_line * spread_u)
    return dot(out, g8t)


def solve_columns(block, k_ref, m_ref, first, count, consts, lines, acc):
    rep10, lam_ab, lam_c, qq, qqt, zf, zft = consts
    lines[...] = dot(block, zf[...])
    acc[...] = jnp.zeros_like(acc)
    lam = lam_ab[...] + lam_c[...]
    for c in range(count):
        k, m = k_ref[first + c : first + c + 1], m_ref[first + c : first + c + 1]
        den = dot(k, rep10[...]) * lam + dot(m, rep10[...])
        spectral = dot(qqt[...], lines[112 * c : 112 * c + 160]) / den
        low = max(128 - 112 * c, 0)
        high = min(112 * (count - 1) + 32 - 112 * c, 160)
        start = 112 * c + low - 128
        acc[start : start + high - low] = acc[start : start + high - low] + dot(qq[low:high], spectral)
    return dot(acc[...], zft[...])


def schwarz_b_kernel(bx_ref, yl_ref, yh_ref, k_ref, m_ref, *refs):
    consts, (out_ref, hi_ref, lo_ref, scr, lines, acc) = refs[:-6], refs[-6:]
    nz = bx_ref.shape[2]
    scr[...] = jnp.zeros_like(scr)
    scr[:, 1:8] = bx_ref[:, 0:7]
    scr[:, 0:1] = yl_ref[...]
    scr[:, 8:10] = yh_ref[...]
    out = solve_columns(scr[...].reshape(52 * 16, nz), k_ref, m_ref, 0, 7, consts, lines, acc)
    out_ref[...] = out.reshape(36, 16, nz)
    hi_ref[...] = out_ref[:, 8:10]
    lo_ref[...] = out_ref[:, 0:2]


def schwarz_q_kernel(qx_ref, yl_ref, yh_ref, k_ref, m_ref, *refs):
    consts, (q_ref, out_ref, hi_ref, lo_ref, scr, lines, acc) = refs[:-7], refs[-7:]
    nz = qx_ref.shape[2]
    scr[...] = jnp.zeros_like(scr)
    scr[:, 1:9] = qx_ref[...]
    scr[:, 0:1] = yl_ref[:, 0:1]
    scr[:, 1:2] = scr[:, 1:2] + yl_ref[:, 1:2]
    scr[:, 8:9] = scr[:, 8:9] + yh_ref[:, 0:1]
    scr[:, 9:10] = yh_ref[:, 1:2]
    q_ref[...] = scr[8:16, 1:9]
    out = solve_columns(scr[...].reshape(24 * 16, nz), k_ref, m_ref, 2, 3, consts, lines, acc)
    out_ref[...] = out.reshape(8, 16, nz)
    hi_ref[...] = out_ref[:, 8:10]
    lo_ref[...] = out_ref[:, 0:2]


def fold_v_kernel(v_ref, xl_ref, out_ref, hi_ref):
    out_ref[...] = v_ref[0:7]
    out_ref[0] = out_ref[0] + xl_ref[0]
    hi_ref[...] = out_ref[:, 7:8]


def gather_s(u_ref, y_ref, yl_ref, yh_ref):
    u_ref[...] = y_ref[:, 1:9]
    u_ref[:, 0:2] = u_ref[:, 0:2] + yl_ref[...]
    u_ref[:, 6:8] = u_ref[:, 6:8] + yh_ref[...]


def apply_u_kernel(idx_ref, b_ref, y_ref, yl_ref, yh_ref, k_ref, m_ref, inner_ref, zct_ref, *refs):
    consts, (u_ref, own_ref, au_ref, h_ref) = refs[:-4], refs[-4:]
    nz = u_ref.shape[2]
    gather_s(u_ref, y_ref, yl_ref, yh_ref)
    own_ref[...] = u_ref[14:22]
    u = own_ref[...].reshape(64, nz)
    au = apply(u, k_ref[...], m_ref[...], *(ref[...] for ref in consts))
    au_ref[...] = au.reshape(8, 8, nz)
    h = dot(jnp.sum(inner_ref[...] * au, axis=0, keepdims=True), zct_ref[...]) * lane_sel(idx_ref[0])
    acc = b_ref[0] * own_ref[0, :7]
    for x in range(1, 7):
        acc = acc + b_ref[x] * own_ref[x, :7]
    h_ref[...] = rows_tile([jnp.zeros((1, LANES), jnp.float32), h, lane_put([total(acc), total(u * au)])])


def apply_s_kernel(y_ref, yl_ref, yh_ref, k_ref, m_ref, *refs):
    consts, (s_ref, as_ref) = refs[:-2], refs[-2:]
    nz = s_ref.shape[2]
    gather_s(s_ref, y_ref, yl_ref, yh_ref)
    out = apply(s_ref[...].reshape(64, nz), k_ref[...], m_ref[...], *(ref[...] for ref in consts))
    as_ref[...] = out.reshape(8, 8, nz)


def apply_p_kernel(idx_ref, u_ref, x_ref, k_ref, m_ref, inner_ref, zl_ref, *refs):
    (rep8, wz, g8, g8t, zk, kk, ww), (p_ref, q_ref, hi_ref, lo_ref, field, su, sk, acc) = refs[:-8], refs[-8:]
    nz = u_ref.shape[2]
    count = idx_ref[1]
    x0 = x_ref[...]
    picks = [x0 * lane_sel(lax.rem(idx_ref[0] + (apart + 2 * count), count)) for apart in range(-2, 3)]
    lines = dot(rows_tile(picks), zl_ref[...])
    field[...] = u_ref[...]
    side = inner_ref[8:16]
    for c in range(5):
        add = side * lines[c : c + 1]
        for x in range(7 * c + 1, 7 * c + 7):
            field[x] = field[x] + add
    p_ref[...] = field[14:22]
    whole = field[...].reshape(36 * 8, nz)
    su[...] = dot(whole, g8[...])
    sk[...] = dot(whole, zk[...])
    acc[...] = jnp.zeros_like(acc)
    for c in range(5):
        k_line = dot(k_ref[c + 1 : c + 2], rep8[...])
        m_line = dot(m_ref[c + 1 : c + 2], rep8[...]) * wz[...]
        part = slice(56 * c, 56 * c + 64)
        u = su[part]
        out = (k_line * wz[...]) * dot(kk[...], u) + ww[...] * (k_line * sk[part] + m_line * u)
        acc[part] = acc[part] + out
    q_ref[...] = dot(acc[48:240], g8t[...]).reshape(24, 8, nz)
    hi_ref[...] = q_ref[:, 6:8]
    lo_ref[...] = q_ref[:, 0:2]


def apply_w_kernel(idx_ref, s_ref, x_ref, k_ref, m_ref, inner_ref, zl_ref, *refs):
    consts, (w_ref, v_ref, hi_ref) = refs[:-3], refs[-3:]
    nz = s_ref.shape[2]
    line = dot(x_ref[...] * lane_sel(idx_ref[0]), zl_ref[...])
    w = s_ref[...].reshape(64, nz) + inner_ref[...] * line
    w_ref[...] = w.reshape(8, 8, nz)
    out = apply(w, k_ref[...], m_ref[...], *(ref[...] for ref in consts)).reshape(8, 8, nz)
    v_ref[...] = out
    hi_ref[...] = out[7:8]


def shift(value, axis, step):
    count = lax.axis_size(axis)
    return lax.ppermute(value, axis, [(i, (i + step) % count) for i in range(count)])


def local(right_side, stiff_coef, mass_coef, coarse_factor):
    nz = right_side.shape[2]
    c_dev, n_coarse = coarse_factor.shape
    ez = stiff_coef.shape[2]
    n_gx, n_gy = lax.axis_size("gx"), lax.axis_size("gy")
    width = n_coarse // n_gx
    tab = {name: jnp.asarray(value) if isinstance(value, np.ndarray) else value for name, value in make_tables(ez, c_dev).items()}
    k = stiff_coef.reshape(1, ez)
    m = mass_coef.reshape(1, ez)
    b = right_side
    idx = jnp.stack([lax.axis_index("gx"), jnp.int32(n_gx)])
    solve_tab = [tab[name] for name in SOLVE]
    apply_tab = [tab[name] for name in APPLY]
    inner, zct, zl, eye = (tab[name] for name in ("inner", "zct", "zl", "eye"))

    def kernel(fn, *fixed):
        def call(*refs):
            return fn(*fixed, *refs)

        call.__name__ = fn.__name__
        return call

    def swap_gx(value):
        return lax.all_to_all(value, "gx", 0, 0)

    def swap_gy(value):
        return lax.all_to_all(value, "gy", 0, 0)

    group = (n_gx, c_dev, LANES)
    aux = -(-(2 * LANES + 7 * nz) // LANES) * LANES
    (pay,) = run(kernel(first_kernel, tab["k_parts"], tab["m_parts"], width), [(n_gx, c_dev, width + aux)],
                 idx, b, k, m, coarse_factor, tab["r1"], tab["r2"], tab["r1t"], tab["r2t"], zct, scratch=[(8, aux)])
    xl = swap_gx(pay)

    outs = [(n_gy, 1, width + LANES), (52, 8, nz), (52, 1, nz), (52, 2, nz), (8, ez), (8, ez)]
    pay, bx, hi, lo, ks, ms = run(kernel(coarse_in_kernel, width), outs, idx, xl, eye, free=(0,))
    y_low, y_high = shift(hi, "gy", 1), shift(lo, "gy", -1)
    sums = swap_gy(pay)

    sides = [(8, 2, nz), (8, 2, nz)]
    y, hi, lo = run(schwarz_b_kernel, [(36, 16, nz), (36, 2, nz), (36, 2, nz)], bx, y_low, y_high, ks, ms, *solve_tab,
                    scratch=[(52, 16, nz), (832, 10 * ez), (576, 10 * ez)])
    y_low, y_high = shift(hi, "gy", 1), shift(lo, "gy", -1)
    cube = (8, 8, nz)
    wide_u, u, au, h = run(apply_u_kernel, [(36, 8, nz), cube, cube, (8, LANES)], idx, b, y, y_low, y_high, k, m, inner, zct, *apply_tab,
                          free=(1, 2))

    (pay,) = run(kernel(coarse_out_kernel, width), [group], sums, xl, eye, h)
    got = swap_gx(pay)
    pay, x0 = run(kernel(coarse_mid_kernel, width), [(n_gy, 1, width + LANES), (1, LANES)], got, xl, eye, free=(0,))
    sums = swap_gy(pay)

    p, qx, hi, lo = run(apply_p_kernel, [cube, (24, 8, nz), (24, 2, nz), (24, 2, nz)], idx, wide_u, x0, ks, ms, inner, zl, *apply_tab,
                        scratch=[(36, 8, nz)] + [(288, 8 * ez)] * 3)
    y_low, y_high = shift(hi, "gy", 1), shift(lo, "gy", -1)
    q, y, hi, lo = run(schwarz_q_kernel, [cube, (8, 16, nz)] + sides, qx, y_low, y_high, ks, ms, *solve_tab,
                       scratch=[(24, 16, nz), (384, 10 * ez), (128, 10 * ez)])
    y_low, y_high = shift(hi, "gy", 1), shift(lo, "gy", -1)
    s, a_s = run(apply_s_kernel, [cube, cube], y, y_low, y_high, k, m, *apply_tab)

    pay, scal, resid = run(kernel(pair_kernel, width), [group, (1, LANES), cube], idx, sums, xl, eye, b, q, u, au, s, a_s, inner, zct)
    got = swap_gx(pay)
    pay, x1 = run(kernel(last_in_kernel, width), [(n_gy, 1, LANES), (1, LANES)], got, xl, x0, scal, eye, free=(0,))
    sums = swap_gy(pay)

    w, v, hi = run(apply_w_kernel, [cube, cube, (1, 8, nz)], idx, s, x1, k, m, inner, zl, *apply_tab)
    x_low = shift(hi, "gx", 1)
    v, hi = run(fold_v_kernel, [(7, 8, nz), (7, 1, nz)], v, x_low)
    y_low = shift(hi, "gy", 1)
    sol, res = run(final_kernel, [(7, 7, nz), (7, 7, nz)], sums, scal, p, w, resid, q, v, y_low, free=(0, 1))
    return sol, res


def solution(mesh):
    placed = (P("gx", "gy", None), P("gx", "gy", None), P("gx", "gy", None), P(("gx", "gy"), None))
    return jax.shard_map(
        local,
        mesh=mesh,
        in_specs=placed,
        out_specs=(P("gx", "gy", None), P("gx", "gy", None)),
        check_vma=False,
    )
```

```python
import math

import jax
import jax.numpy as jnp
import numpy as np
from jax import lax
from jax.experimental import pallas as pl
from jax.experimental.pallas import tpu as pltpu
from jax.sharding import PartitionSpec as P


HI = lax.Precision.HIGHEST
LANES = 128


def legendre_pair(position, degree):
    p_prev = 1.0
    p_now = position
    for order in range(2, degree + 1):
        p_next = ((2 * order - 1) * position * p_now - (order - 1) * p_prev) / order
        p_prev = p_now
        p_now = p_next
    return (p_now, p_prev)


def jacobi_eigen(matrix):
    size_n = matrix.shape[0]
    current = np.array(matrix)
    vectors = np.eye(size_n)
    for _ in range(20):
        for row_p in range(size_n - 1):
            for row_q in range(row_p + 1, size_n):
                off_value = current[row_p, row_q]
                if abs(off_value) > 1e-300:
                    theta = (current[row_q, row_q] - current[row_p, row_p]) / (2.0 * off_value)
                    sign_t = 1.0 if theta >= 0.0 else -1.0
                    tangent = sign_t / (abs(theta) + math.sqrt(theta * theta + 1.0))
                    cosine = 1.0 / math.sqrt(tangent * tangent + 1.0)
                    sine = tangent * cosine
                    rotation = np.eye(size_n)
                    rotation[row_p, row_p] = cosine
                    rotation[row_q, row_q] = cosine
                    rotation[row_p, row_q] = sine
                    rotation[row_q, row_p] = -sine
                    current = rotation.T @ current @ rotation
                    vectors = vectors @ rotation
    return (np.array([current[idx, idx] for idx in range(size_n)]), vectors)


def gll_tables():
    degree = 7
    guesses = [
        -0.8717401485096066,
        -0.5917001814331423,
        -0.2092992179024789,
        0.2092992179024789,
        0.5917001814331423,
        0.8717401485096066,
    ]
    interior = []
    for guess in guesses:
        position = guess
        for _ in range(30):
            p_now, p_prev = legendre_pair(position, degree)
            first = degree * (position * p_now - p_prev) / (position * position - 1.0)
            second = (2.0 * position * first - degree * (degree + 1) * p_now) / (
                1.0 - position * position
            )
            position = position - first / second
        interior.append(position)
    points = np.array([-1.0] + interior + [1.0])
    values = np.array([legendre_pair(float(pt), degree)[0] for pt in points])
    weights = 2.0 / (degree * (degree + 1) * values**2)
    deriv_mat = np.zeros((8, 8))
    for left_idx in range(8):
        for right_idx in range(8):
            if left_idx != right_idx:
                deriv_mat[left_idx, right_idx] = values[left_idx] / (
                    values[right_idx] * (points[left_idx] - points[right_idx])
                )
    deriv_mat[0, 0] = -degree * (degree + 1) / 4.0
    deriv_mat[7, 7] = degree * (degree + 1) / 4.0
    stiffness = deriv_mat.T @ (weights[:, None] * deriv_mat)
    ext_stiff = np.zeros((10, 10))
    ext_stiff[1:9, 1:9] += stiffness
    ext_stiff[0:2, 0:2] += stiffness[6:8, 6:8]
    ext_stiff[8:10, 8:10] += stiffness[0:2, 0:2]
    ext_mass = np.zeros(10)
    ext_mass[1:9] += weights
    ext_mass[0:2] += weights[6:8]
    ext_mass[8:10] += weights[0:2]
    inv_root = 1.0 / np.sqrt(ext_mass)
    eigen_vals, eigen_vecs = jacobi_eigen(inv_root[:, None] * ext_stiff * inv_root[None, :])
    eigen_basis = inv_root[:, None] * eigen_vecs
    return (stiffness, weights, eigen_basis, eigen_vals)


def dot(left, right):
    return jnp.dot(left, right, precision=HI, preferred_element_type=jnp.float32)


def make_tables(ez, c_dev):
    stiffness, weights, basis, vals = gll_tables()
    stiffness = stiffness.astype(np.float32).astype(np.float64)
    weights = weights.astype(np.float32).astype(np.float64)
    basis = basis.astype(np.float32).astype(np.float64)
    vals = vals.astype(np.float32).astype(np.float64)
    nz = 7 * ez
    span = nz // c_dev
    f32 = lambda table: np.asarray(table, np.float32)

    qq = np.zeros((10, 16, 10, 16))
    qq[:, :10, :, :10] = np.einsum("ia,jb->ijab", basis, basis)
    qq = qq.reshape(160, 160)
    lam_ab = np.ones((10, 16))
    lam_ab[:, :10] = vals[:, None] + vals[None, :]
    lam_c = np.repeat(vals, ez)[None]
    zf = np.zeros((nz, 10, ez))
    g8 = np.zeros((nz, 8, ez))
    zk = np.zeros((nz, 8, ez))
    for elem in range(ez):
        for k in range(10):
            zf[(7 * elem - 1 + k) % nz, :, elem] += basis[k]
        for k in range(8):
            g8[(7 * elem + k) % nz, k, elem] += 1.0
            zk[(7 * elem + k) % nz, :, elem] += stiffness[:, k]
    zf, g8, zk = zf.reshape(nz, -1), g8.reshape(nz, -1), zk.reshape(nz, -1)
    diag = np.diag(weights)
    kk = np.einsum("ai,bj->abij", stiffness, diag) + np.einsum("ai,bj->abij", diag, stiffness)
    kk = kk.reshape(64, 64)
    ww = np.outer(weights, weights).reshape(64, 1)
    inner = np.zeros((8, 8))
    inner[1:7, 1:7] = 1.0
    plate = inner.reshape(64, 1)
    first = np.array([1.0] * 7 + [0.0])
    last = 1.0 - first
    k_parts = {}
    m_parts = {}
    for name, left, right in (("11", first, first), ("12", first, last), ("22", last, last)):
        wz = float(np.sum(left * weights * right))
        kz = float(left @ stiffness @ right)
        k_parts[name] = float((plate.T @ kk @ plate).item()) * wz + float(np.sum(plate * ww)) * kz
        m_parts[name] = float(np.sum(plate * ww)) * wz
    wide = LANES // c_dev
    zc = (np.arange(nz)[:, None] // span == np.arange(c_dev)[None, :]).astype(np.float64)
    return dict(
        qq=f32(qq), qqt=f32(qq.T), zf=f32(zf), zft=f32(zf.T), lam_ab=f32(lam_ab.reshape(160, 1)), lam_c=f32(lam_c),
        rep10=f32(np.tile(np.eye(ez), (1, 10))), rep8=f32(np.tile(np.eye(ez), (1, 8))),
        g8=f32(g8), g8t=f32(g8.T), zk=f32(zk), kk=f32(kk), ww=f32(ww), wz=f32(np.repeat(weights, ez)[None]),
        inner=f32(plate),
        zct=f32(np.tile(zc, (1, wide))), eye=f32(np.eye(LANES)),
        zl=f32(np.tile(zc.T, (wide, 1))),
        k_parts=k_parts, m_parts=m_parts,
    )


def run(kernel, outs, *args, scratch=(), free=(), limit=16):
    spaces = [pltpu.SMEM if a.dtype == jnp.int32 else pltpu.VMEM for a in args]
    size = sum(math.prod(s) for s in outs) + sum(math.prod(a.shape) for a in args)
    return pl.pallas_call(
        kernel,
        out_shape=[(jax.ShapeDtypeStruct if i in free else pltpu.VMEM)(shape, jnp.float32) for i, shape in enumerate(outs)],
        in_specs=[pl.BlockSpec(memory_space=space) for space in spaces],
        out_specs=[pl.BlockSpec(memory_space=pltpu.VMEM)] * len(outs),
        scratch_shapes=[pltpu.VMEM(shape, jnp.float32) for shape in scratch],
        compiler_params=pltpu.CompilerParams(vmem_limit_bytes=limit << 20),
        cost_estimate=pl.CostEstimate(flops=2 * 6 * 160 * 240 * 168, bytes_accessed=4 * size, transcendentals=0),
    )(*args)


def total(value):
    return jnp.sum(jnp.sum(value, axis=1, keepdims=True), axis=0, keepdims=True)


def total_row(row):
    return jnp.sum(row, axis=1, keepdims=True)


def as_col(row, eye):
    return jnp.sum(eye * row, axis=1, keepdims=True)


def as_row(col, eye):
    return jnp.sum(eye * col, axis=0, keepdims=True)


def lane_put(values):
    lane = lax.broadcasted_iota(jnp.int32, (1, LANES), 1)
    row = jnp.zeros((1, LANES), jnp.float32)
    for spot, value in enumerate(values):
        row = jnp.where(lane == spot, value, row)
    return row


def lane_get(row, spot):
    lane = lax.broadcasted_iota(jnp.int32, row.shape, 1)
    return jnp.sum(jnp.where(lane == spot, row, 0.0), axis=1, keepdims=True)


def lane_sel(spot):
    lane = lax.broadcasted_iota(jnp.int32, (1, LANES), 1)
    return jnp.where(lane // 8 == spot, 1.0, 0.0).astype(jnp.float32)


def span_mask(shape, axis, size, move):
    row = lax.broadcasted_iota(jnp.int32, shape, axis) & 7
    start = row * size + move
    fine = lax.broadcasted_iota(jnp.int32, shape, 1 - axis)
    return jnp.where((fine >= start) & (fine < start + size), 1.0, 0.0).astype(jnp.float32)


def rows_tile(rows):
    spot = lax.broadcasted_iota(jnp.int32, (8, LANES), 0)
    tile = jnp.zeros((8, LANES), jnp.float32)
    for place, row in enumerate(rows):
        tile = jnp.where(spot == place, row, tile)
    return tile


def first_kernel(k_parts, m_parts, width, idx_ref, b_ref, k_ref, m_ref, x_ref, out_ref, scr):
    k, m = k_ref[...], m_ref[...]
    e11, e12, e22 = (k * k_parts[name] + m * m_parts[name] for name in ("11", "12", "22"))
    nz, ez = b_ref.shape[2], k.shape[1]
    per, span = ez // 8, nz // 8
    sel = lane_sel(idx_ref[0])
    owner = span_mask((8, ez), 0, per, 0)
    after = span_mask((8, ez), 0, per, -1) + span_mask((8, ez), 0, per, ez - 1)
    owner_t = span_mask((ez, LANES), 1, per, 0)
    after_t = span_mask((ez, LANES), 1, per, -1) + span_mask((ez, LANES), 1, per, ez - 1)
    small = (dot(owner * e11 + after * e12, owner_t) + dot(owner * e12 + after * e22, after_t)) * sel
    acc = b_ref[1]
    for x in range(2, 7):
        acc = acc + b_ref[x]
    line = jnp.sum(acc[1:7], axis=0, keepdims=True)
    rc = dot(line, span_mask((nz, LANES), 1, span, 0)) * sel
    scr[...] = jnp.zeros_like(scr)
    scr[:, :LANES] = small
    scr[0:1, LANES : 2 * LANES] = rc
    scr[1:2, LANES : LANES + ez] = k
    scr[2:3, LANES : LANES + ez] = m
    for x in range(7):
        scr[:7, 2 * LANES + nz * x : 2 * LANES + nz * (x + 1)] = b_ref[x]
    for peer in range(out_ref.shape[0]):
        out_ref[peer, :, :width] = x_ref[:, peer * width : (peer + 1) * width]
        out_ref[peer, :, width:] = scr[...]


def split_group(xl_ref, width):
    rows = xl_ref.shape[0] * xl_ref.shape[1]
    small = xl_ref[:, :, width : width + LANES].reshape(rows, LANES)
    rc = jnp.sum(xl_ref[:, 0:1, width + LANES : width + 2 * LANES], axis=0)
    return xl_ref[:, :, :width].reshape(rows, width), small, rc


def spread(out_ref, row):
    out_ref[...] = jnp.broadcast_to(row[None], out_ref.shape)


def coarse_in_kernel(width, idx_ref, xl_ref, eye_ref, out_ref, bx_ref, hi_ref, lo_ref, k_ref, m_ref):
    factor, _, rc = split_group(xl_ref, width)
    rows = factor.shape[0]
    rc_col = as_col(rc, eye_ref[:rows])
    part = jnp.sum(rc_col * factor, axis=0, keepdims=True)
    spread(out_ref, part)
    count = xl_ref.shape[0]
    nz, ez = bx_ref.shape[2], k_ref.shape[1]
    base = width + 2 * LANES
    place = 0
    for apart in range(-4, 5):
        slot = lax.rem(idx_ref[0] + (apart + 2 * count), count)
        for x in (6,) if apart == -4 else (0, 1) if apart == 4 else range(7):
            bx_ref[place] = xl_ref[slot, :, base + nz * x : base + nz * (x + 1)]
            place += 1
        if -4 < apart < 4:
            k_ref[apart + 3 : apart + 4] = xl_ref[slot, 1:2, width + LANES : width + LANES + ez]
            m_ref[apart + 3 : apart + 4] = xl_ref[slot, 2:3, width + LANES : width + LANES + ez]
    k_ref[7:8] = k_ref[6:7]
    m_ref[7:8] = m_ref[6:7]
    hi_ref[...] = bx_ref[:, 6:7]
    lo_ref[...] = bx_ref[:, 0:2]


def coarse_out_kernel(width, sums_ref, xl_ref, eye_ref, h_ref, out_ref):
    factor, _, _ = split_group(xl_ref, width)
    rows = factor.shape[0]
    sums = jnp.sum(sums_ref[...], axis=0)
    part = jnp.sum(factor * sums[:, :width], axis=1, keepdims=True)
    x_part = as_row(part, eye_ref[:rows])
    spot = lax.broadcasted_iota(jnp.int32, (8, LANES), 0)
    tile = jnp.where(spot == 0, x_part, h_ref[...])
    out_ref[...] = jnp.broadcast_to(tile[None], out_ref.shape)


def coarse_mid_kernel(width, got_ref, xl_ref, eye_ref, out_ref, x_ref):
    factor, small, rc = split_group(xl_ref, width)
    rows = factor.shape[0]
    eye = eye_ref[:rows]
    got = jnp.sum(got_ref[...], axis=0)
    x0, h, scal = got[0:1], got[1:2], got[2:3]
    rc1_col = jnp.sum(small * x0 + eye * h, axis=1, keepdims=True)
    rc1 = as_row(rc1_col, eye)
    part = jnp.sum(rc1_col * factor, axis=0, keepdims=True)
    rho = lane_get(scal, 0) + total_row(rc * x0)
    den = lane_get(scal, 1) + total_row(x0 * (h + rc1))
    spread(out_ref, jnp.concatenate([part, lane_put([rho, den])], axis=1))
    x_ref[...] = x0


def pair_kernel(width, idx_ref, sums_ref, xl_ref, eye_ref, b_ref, q_ref, u_ref, au_ref, s_ref, as_ref, inner_ref, zct_ref,
                out_ref, scal_ref, r_ref):
    factor, _, _ = split_group(xl_ref, width)
    rows = factor.shape[0]
    sums = jnp.sum(sums_ref[...], axis=0)
    part = jnp.sum(factor * sums[:, :width], axis=1, keepdims=True)
    x_part = as_row(part, eye_ref[:rows])
    scal = sums[:, width:]
    rho, den = lane_get(scal, 0), lane_get(scal, 1)
    step = rho / den
    sel = lane_sel(idx_ref[0])
    r_ref[...] = jnp.zeros_like(r_ref)
    for x in range(7):
        r_ref[x, :7] = b_ref[x] - step * q_ref[x, :7]
    nz = b_ref.shape[2]
    flat = lambda ref: ref[...].reshape(64, nz)
    resid = flat(r_ref)
    t = flat(u_ref) - step * flat(s_ref)
    at = flat(au_ref) - step * flat(as_ref)
    inner = inner_ref[...]
    wr = dot(jnp.sum(inner * resid, axis=0, keepdims=True), zct_ref[...]) * sel
    wt = dot(jnp.sum(inner * at, axis=0, keepdims=True), zct_ref[...]) * sel
    tile = rows_tile([x_part, wr, wt, lane_put([total(resid * t), total(t * at)])])
    out_ref[...] = jnp.broadcast_to(tile[None], out_ref.shape)
    scal_ref[...] = lane_put([rho, den])


def last_in_kernel(width, got_ref, xl_ref, x0_ref, scal_ref, eye_ref, out_ref, x_ref):
    _, small, _ = split_group(xl_ref, width)
    eye = eye_ref[: small.shape[0]]
    got = jnp.sum(got_ref[...], axis=0)
    x1, wr, wt, scal = got[0:1], got[1:2], got[2:3], got[3:4]
    step = lane_get(scal_ref[...], 0) / lane_get(scal_ref[...], 1)
    c = x0_ref[...] - step * x1
    tc = as_row(jnp.sum(small * c, axis=1, keepdims=True), eye)
    rho1 = lane_get(scal, 0) + total_row(wr * c)
    en1 = lane_get(scal, 1) + total_row(c * (2.0 * wt + tc))
    spread(out_ref, lane_put([rho1, en1]))
    x_ref[...] = x1


def final_kernel(sums_ref, scal_ref, p_ref, w_ref, r_ref, qo_ref, v_ref, vl_ref, sol_ref, res_ref):
    got = jnp.sum(sums_ref[...], axis=0)
    rho1, en1 = lane_get(got, 0), lane_get(got, 1)
    rho, den = lane_get(scal_ref[...], 0), lane_get(scal_ref[...], 1)
    step = rho / den
    beta = rho1 / rho
    step1 = rho1 / (en1 - beta * rho1 / step)
    p_mult = step + step1 * (1.0 + beta)
    w_mult = step1 * step
    q_mult = step1 * (1.0 + beta)
    for x in range(7):
        sol_ref[x] = p_mult * p_ref[x, :7] - w_mult * w_ref[x, :7]
        top = w_mult * vl_ref[x]
        res_ref[x] = r_ref[x, :7] - q_mult * qo_ref[x, :7] + w_mult * v_ref[x, :7]
        res_ref[x, 0:1] = res_ref[x, 0:1] + top


SOLVE = ("rep10", "lam_ab", "lam_c", "qq", "qqt", "zf", "zft")
APPLY = ("rep8", "wz", "g8", "g8t", "zk", "kk", "ww")


def apply(block, k, m, rep8, wz, g8, g8t, zk, kk, ww):
    k_line, m_line = dot(k, rep8), dot(m, rep8) * wz
    spread_u = dot(block, g8)
    out = (k_line * wz) * dot(kk, spread_u) + ww * (k_line * dot(block, zk) + m_line * spread_u)
    return dot(out, g8t)


def solve_columns(block, k_ref, m_ref, first, count, consts, lines, acc):
    rep10, lam_ab, lam_c, qq, qqt, zf, zft = consts
    lines[...] = dot(block, zf[...])
    acc[...] = jnp.zeros_like(acc)
    lam = lam_ab[...] + lam_c[...]
    for c in range(count):
        k, m = k_ref[first + c : first + c + 1], m_ref[first + c : first + c + 1]
        den = dot(k, rep10[...]) * lam + dot(m, rep10[...])
        spectral = dot(qqt[...], lines[112 * c : 112 * c + 160]) / den
        low = max(128 - 112 * c, 0)
        high = min(112 * (count - 1) + 32 - 112 * c, 160)
        start = 112 * c + low - 128
        acc[start : start + high - low] = acc[start : start + high - low] + dot(qq[low:high], spectral)
    return dot(acc[...], zft[...])


def schwarz_b_kernel(bx_ref, yl_ref, yh_ref, k_ref, m_ref, *refs):
    consts, (out_ref, hi_ref, lo_ref, scr, lines, acc) = refs[:-6], refs[-6:]
    nz = bx_ref.shape[2]
    scr[...] = jnp.zeros_like(scr)
    scr[:, 1:8] = bx_ref[:, 0:7]
    scr[:, 0:1] = yl_ref[...]
    scr[:, 8:10] = yh_ref[...]
    out = solve_columns(scr[...].reshape(52 * 16, nz), k_ref, m_ref, 0, 7, consts, lines, acc)
    out_ref[...] = out.reshape(36, 16, nz)
    hi_ref[...] = out_ref[:, 8:10]
    lo_ref[...] = out_ref[:, 0:2]


def schwarz_q_kernel(qx_ref, yl_ref, yh_ref, k_ref, m_ref, *refs):
    consts, (q_ref, out_ref, hi_ref, lo_ref, scr, lines, acc) = refs[:-7], refs[-7:]
    nz = qx_ref.shape[2]
    scr[...] = jnp.zeros_like(scr)
    scr[:, 1:9] = qx_ref[...]
    scr[:, 0:1] = yl_ref[:, 0:1]
    scr[:, 1:2] = scr[:, 1:2] + yl_ref[:, 1:2]
    scr[:, 8:9] = scr[:, 8:9] + yh_ref[:, 0:1]
    scr[:, 9:10] = yh_ref[:, 1:2]
    q_ref[...] = scr[8:16, 1:9]
    out = solve_columns(scr[...].reshape(24 * 16, nz), k_ref, m_ref, 2, 3, consts, lines, acc)
    out_ref[...] = out.reshape(8, 16, nz)
    hi_ref[...] = out_ref[:, 8:10]
    lo_ref[...] = out_ref[:, 0:2]


def fold_v_kernel(v_ref, xl_ref, out_ref, hi_ref):
    out_ref[...] = v_ref[0:7]
    out_ref[0] = out_ref[0] + xl_ref[0]
    hi_ref[...] = out_ref[:, 7:8]


def gather_s(u_ref, y_ref, yl_ref, yh_ref):
    u_ref[...] = y_ref[:, 1:9]
    u_ref[:, 0:2] = u_ref[:, 0:2] + yl_ref[...]
    u_ref[:, 6:8] = u_ref[:, 6:8] + yh_ref[...]


def apply_u_kernel(idx_ref, b_ref, y_ref, yl_ref, yh_ref, k_ref, m_ref, inner_ref, zct_ref, *refs):
    consts, (u_ref, own_ref, au_ref, h_ref) = refs[:-4], refs[-4:]
    nz = u_ref.shape[2]
    gather_s(u_ref, y_ref, yl_ref, yh_ref)
    own_ref[...] = u_ref[14:22]
    u = own_ref[...].reshape(64, nz)
    au = apply(u, k_ref[...], m_ref[...], *(ref[...] for ref in consts))
    au_ref[...] = au.reshape(8, 8, nz)
    h = dot(jnp.sum(inner_ref[...] * au, axis=0, keepdims=True), zct_ref[...]) * lane_sel(idx_ref[0])
    acc = b_ref[0] * own_ref[0, :7]
    for x in range(1, 7):
        acc = acc + b_ref[x] * own_ref[x, :7]
    h_ref[...] = rows_tile([jnp.zeros((1, LANES), jnp.float32), h, lane_put([total(acc), total(u * au)])])


def apply_s_kernel(y_ref, yl_ref, yh_ref, k_ref, m_ref, *refs):
    consts, (s_ref, as_ref) = refs[:-2], refs[-2:]
    nz = s_ref.shape[2]
    gather_s(s_ref, y_ref, yl_ref, yh_ref)
    out = apply(s_ref[...].reshape(64, nz), k_ref[...], m_ref[...], *(ref[...] for ref in consts))
    as_ref[...] = out.reshape(8, 8, nz)


def apply_p_kernel(idx_ref, u_ref, x_ref, k_ref, m_ref, inner_ref, zl_ref, *refs):
    (rep8, wz, g8, g8t, zk, kk, ww), (p_ref, q_ref, hi_ref, lo_ref, field, su, sk, acc) = refs[:-8], refs[-8:]
    nz = u_ref.shape[2]
    count = idx_ref[1]
    x0 = x_ref[...]
    picks = [x0 * lane_sel(lax.rem(idx_ref[0] + (apart + 2 * count), count)) for apart in range(-2, 3)]
    lines = dot(rows_tile(picks), zl_ref[...])
    field[...] = u_ref[...]
    side = inner_ref[8:16]
    for c in range(5):
        add = side * lines[c : c + 1]
        for x in range(7 * c + 1, 7 * c + 7):
            field[x] = field[x] + add
    p_ref[...] = field[14:22]
    whole = field[...].reshape(36 * 8, nz)
    su[...] = dot(whole, g8[...])
    sk[...] = dot(whole, zk[...])
    acc[...] = jnp.zeros_like(acc)
    for c in range(5):
        k_line = dot(k_ref[c + 1 : c + 2], rep8[...])
        m_line = dot(m_ref[c + 1 : c + 2], rep8[...]) * wz[...]
        part = slice(56 * c, 56 * c + 64)
        u = su[part]
        out = (k_line * wz[...]) * dot(kk[...], u) + ww[...] * (k_line * sk[part] + m_line * u)
        acc[part] = acc[part] + out
    q_ref[...] = dot(acc[48:240], g8t[...]).reshape(24, 8, nz)
    hi_ref[...] = q_ref[:, 6:8]
    lo_ref[...] = q_ref[:, 0:2]


def apply_w_kernel(idx_ref, s_ref, x_ref, k_ref, m_ref, inner_ref, zl_ref, *refs):
    consts, (w_ref, v_ref, hi_ref) = refs[:-3], refs[-3:]
    nz = s_ref.shape[2]
    line = dot(x_ref[...] * lane_sel(idx_ref[0]), zl_ref[...])
    w = s_ref[...].reshape(64, nz) + inner_ref[...] * line
    w_ref[...] = w.reshape(8, 8, nz)
    out = apply(w, k_ref[...], m_ref[...], *(ref[...] for ref in consts)).reshape(8, 8, nz)
    v_ref[...] = out
    hi_ref[...] = out[7:8]


def shift(value, axis, step):
    count = lax.axis_size(axis)
    return lax.ppermute(value, axis, [(i, (i + step) % count) for i in range(count)])


def local(right_side, stiff_coef, mass_coef, coarse_factor):
    nz = right_side.shape[2]
    c_dev, n_coarse = coarse_factor.shape
    ez = stiff_coef.shape[2]
    n_gx, n_gy = lax.axis_size("gx"), lax.axis_size("gy")
    width = n_coarse // n_gx
    tab = {name: jnp.asarray(value) if isinstance(value, np.ndarray) else value for name, value in make_tables(ez, c_dev).items()}
    k = stiff_coef.reshape(1, ez)
    m = mass_coef.reshape(1, ez)
    b = right_side
    idx = jnp.stack([lax.axis_index("gx"), jnp.int32(n_gx)])
    solve_tab = [tab[name] for name in SOLVE]
    apply_tab = [tab[name] for name in APPLY]
    inner, zct, zl, eye = (tab[name] for name in ("inner", "zct", "zl", "eye"))

    def kernel(fn, *fixed):
        def call(*refs):
            return fn(*fixed, *refs)

        call.__name__ = fn.__name__
        return call

    def swap_gx(value):
        return lax.all_to_all(value, "gx", 0, 0)

    def swap_gy(value):
        return lax.all_to_all(value, "gy", 0, 0)

    group = (n_gx, c_dev, LANES)
    aux = -(-(2 * LANES + 7 * nz) // LANES) * LANES
    (pay,) = run(kernel(first_kernel, tab["k_parts"], tab["m_parts"], width), [(n_gx, c_dev, width + aux)],
                 idx, b, k, m, coarse_factor, scratch=[(8, aux)], limit=56)
    xl = swap_gx(pay)

    outs = [(n_gy, 1, width), (52, 8, nz), (52, 1, nz), (52, 2, nz), (8, ez), (8, ez)]
    pay, bx, hi, lo, ks, ms = run(kernel(coarse_in_kernel, width), outs, idx, xl, eye, free=(0,))
    y_low, y_high = shift(hi, "gy", 1), shift(lo, "gy", -1)
    sums = swap_gy(pay)

    sides = [(8, 2, nz), (8, 2, nz)]
    y, hi, lo = run(schwarz_b_kernel, [(36, 16, nz), (36, 2, nz), (36, 2, nz)], bx, y_low, y_high, ks, ms, *solve_tab,
                    scratch=[(52, 16, nz), (832, 10 * ez), (576, 10 * ez)])
    y_low, y_high = shift(hi, "gy", 1), shift(lo, "gy", -1)
    cube = (8, 8, nz)
    wide_u, u, au, h = run(apply_u_kernel, [(36, 8, nz), cube, cube, (8, LANES)], idx, b, y, y_low, y_high, k, m, inner, zct, *apply_tab,
                          free=(1, 2))

    (pay,) = run(kernel(coarse_out_kernel, width), [group], sums, xl, eye, h)
    got = swap_gx(pay)
    pay, x0 = run(kernel(coarse_mid_kernel, width), [(n_gy, 1, width + LANES), (1, LANES)], got, xl, eye, free=(0,))
    sums = swap_gy(pay)

    p, qx, hi, lo = run(apply_p_kernel, [cube, (24, 8, nz), (24, 2, nz), (24, 2, nz)], idx, wide_u, x0, ks, ms, inner, zl, *apply_tab,
                        scratch=[(36, 8, nz)] + [(288, 8 * ez)] * 3)
    y_low, y_high = shift(hi, "gy", 1), shift(lo, "gy", -1)
    q, y, hi, lo = run(schwarz_q_kernel, [cube, (8, 16, nz)] + sides, qx, y_low, y_high, ks, ms, *solve_tab,
                       scratch=[(24, 16, nz), (384, 10 * ez), (128, 10 * ez)])
    y_low, y_high = shift(hi, "gy", 1), shift(lo, "gy", -1)
    s, a_s = run(apply_s_kernel, [cube, cube], y, y_low, y_high, k, m, *apply_tab)

    pay, scal, resid = run(kernel(pair_kernel, width), [group, (1, LANES), cube], idx, sums, xl, eye, b, q, u, au, s, a_s, inner, zct)
    got = swap_gx(pay)
    pay, x1 = run(kernel(last_in_kernel, width), [(n_gy, 1, LANES), (1, LANES)], got, xl, x0, scal, eye, free=(0,))
    sums = swap_gy(pay)

    w, v, hi = run(apply_w_kernel, [cube, cube, (1, 8, nz)], idx, s, x1, k, m, inner, zl, *apply_tab)
    x_low = shift(hi, "gx", 1)
    v, hi = run(fold_v_kernel, [(7, 8, nz), (7, 1, nz)], v, x_low)
    y_low = shift(hi, "gy", 1)
    sol, res = run(final_kernel, [(7, 7, nz), (7, 7, nz)], sums, scal, p, w, resid, q, v, y_low, free=(0, 1))
    return sol, res


def solution(mesh):
    placed = (P("gx", "gy", None), P("gx", "gy", None), P("gx", "gy", None), P(("gx", "gy"), None))

    return jax.shard_map(
        local,
        mesh=mesh,
        in_specs=placed,
        out_specs=(P("gx", "gy", None), P("gx", "gy", None)),
        check_vma=False,
    )
```

```python
import math

import jax
import jax.numpy as jnp
import numpy as np
from jax import lax
from jax.experimental import pallas as pl
from jax.experimental.pallas import tpu as pltpu
from jax.sharding import PartitionSpec as P


HI = lax.Precision.HIGHEST
LANES = 128


def legendre_pair(position, degree):
    p_prev = 1.0
    p_now = position
    for order in range(2, degree + 1):
        p_next = ((2 * order - 1) * position * p_now - (order - 1) * p_prev) / order
        p_prev = p_now
        p_now = p_next
    return (p_now, p_prev)


def jacobi_eigen(matrix):
    size_n = matrix.shape[0]
    current = np.array(matrix)
    vectors = np.eye(size_n)
    for _ in range(20):
        for row_p in range(size_n - 1):
            for row_q in range(row_p + 1, size_n):
                off_value = current[row_p, row_q]
                if abs(off_value) > 1e-300:
                    theta = (current[row_q, row_q] - current[row_p, row_p]) / (2.0 * off_value)
                    sign_t = 1.0 if theta >= 0.0 else -1.0
                    tangent = sign_t / (abs(theta) + math.sqrt(theta * theta + 1.0))
                    cosine = 1.0 / math.sqrt(tangent * tangent + 1.0)
                    sine = tangent * cosine
                    rotation = np.eye(size_n)
                    rotation[row_p, row_p] = cosine
                    rotation[row_q, row_q] = cosine
                    rotation[row_p, row_q] = sine
                    rotation[row_q, row_p] = -sine
                    current = rotation.T @ current @ rotation
                    vectors = vectors @ rotation
    return (np.array([current[idx, idx] for idx in range(size_n)]), vectors)


def gll_tables():
    degree = 7
    guesses = [
        -0.8717401485096066,
        -0.5917001814331423,
        -0.2092992179024789,
        0.2092992179024789,
        0.5917001814331423,
        0.8717401485096066,
    ]
    interior = []
    for guess in guesses:
        position = guess
        for _ in range(30):
            p_now, p_prev = legendre_pair(position, degree)
            first = degree * (position * p_now - p_prev) / (position * position - 1.0)
            second = (2.0 * position * first - degree * (degree + 1) * p_now) / (
                1.0 - position * position
            )
            position = position - first / second
        interior.append(position)
    points = np.array([-1.0] + interior + [1.0])
    values = np.array([legendre_pair(float(pt), degree)[0] for pt in points])
    weights = 2.0 / (degree * (degree + 1) * values**2)
    deriv_mat = np.zeros((8, 8))
    for left_idx in range(8):
        for right_idx in range(8):
            if left_idx != right_idx:
                deriv_mat[left_idx, right_idx] = values[left_idx] / (
                    values[right_idx] * (points[left_idx] - points[right_idx])
                )
    deriv_mat[0, 0] = -degree * (degree + 1) / 4.0
    deriv_mat[7, 7] = degree * (degree + 1) / 4.0
    stiffness = deriv_mat.T @ (weights[:, None] * deriv_mat)
    ext_stiff = np.zeros((10, 10))
    ext_stiff[1:9, 1:9] += stiffness
    ext_stiff[0:2, 0:2] += stiffness[6:8, 6:8]
    ext_stiff[8:10, 8:10] += stiffness[0:2, 0:2]
    ext_mass = np.zeros(10)
    ext_mass[1:9] += weights
    ext_mass[0:2] += weights[6:8]
    ext_mass[8:10] += weights[0:2]
    inv_root = 1.0 / np.sqrt(ext_mass)
    eigen_vals, eigen_vecs = jacobi_eigen(inv_root[:, None] * ext_stiff * inv_root[None, :])
    eigen_basis = inv_root[:, None] * eigen_vecs
    return (stiffness, weights, eigen_basis, eigen_vals)


def dot(left, right):
    return jnp.dot(left, right, precision=HI, preferred_element_type=jnp.float32)


def make_tables(ez, c_dev):
    stiffness, weights, basis, vals = gll_tables()
    stiffness = stiffness.astype(np.float32).astype(np.float64)
    weights = weights.astype(np.float32).astype(np.float64)
    basis = basis.astype(np.float32).astype(np.float64)
    vals = vals.astype(np.float32).astype(np.float64)
    nz = 7 * ez
    span = nz // c_dev
    f32 = lambda table: np.asarray(table, np.float32)

    qq = np.zeros((10, 16, 10, 16))
    qq[:, :10, :, :10] = np.einsum("ia,jb->ijab", basis, basis)
    qq = qq.reshape(160, 160)
    lam_ab = np.ones((10, 16))
    lam_ab[:, :10] = vals[:, None] + vals[None, :]
    lam_c = np.repeat(vals, ez)[None]
    zf = np.zeros((nz, 10, ez))
    g8 = np.zeros((nz, 8, ez))
    zk = np.zeros((nz, 8, ez))
    for elem in range(ez):
        for k in range(10):
            zf[(7 * elem - 1 + k) % nz, :, elem] += basis[k]
        for k in range(8):
            g8[(7 * elem + k) % nz, k, elem] += 1.0
            zk[(7 * elem + k) % nz, :, elem] += stiffness[:, k]
    zf, g8, zk = zf.reshape(nz, -1), g8.reshape(nz, -1), zk.reshape(nz, -1)
    diag = np.diag(weights)
    kk = np.einsum("ai,bj->abij", stiffness, diag) + np.einsum("ai,bj->abij", diag, stiffness)
    kk = kk.reshape(64, 64)
    ww = np.outer(weights, weights).reshape(64, 1)
    inner = np.zeros((8, 8))
    inner[1:7, 1:7] = 1.0
    plate = inner.reshape(64, 1)
    first = np.array([1.0] * 7 + [0.0])
    last = 1.0 - first
    face = np.zeros((8, 1))
    face[1:7, 0] = weights[1:7] * np.sum(stiffness[7, 1:7])
    k_parts = {}
    m_parts = {}
    for name, left, right in (("11", first, first), ("12", first, last), ("22", last, last)):
        wz = float(np.sum(left * weights * right))
        kz = float(left @ stiffness @ right)
        k_parts[name] = float((plate.T @ kk @ plate).item()) * wz + float(np.sum(plate * ww)) * kz
        m_parts[name] = float(np.sum(plate * ww)) * wz
    wide = LANES // c_dev
    zc = (np.arange(nz)[:, None] // span == np.arange(c_dev)[None, :]).astype(np.float64)
    return dict(
        qq=f32(qq), qqt=f32(qq.T), zf=f32(zf), zft=f32(zf.T), lam_ab=f32(lam_ab.reshape(160, 1)), lam_c=f32(lam_c),
        rep10=f32(np.tile(np.eye(ez), (1, 10))), rep8=f32(np.tile(np.eye(ez), (1, 8))),
        g8=f32(g8), g8t=f32(g8.T), zk=f32(zk), kk=f32(kk), ww=f32(ww), wz=f32(np.repeat(weights, ez)[None]),
        inner=f32(plate), face=f32(face),
        zct=f32(np.tile(zc, (1, wide))), eye=f32(np.eye(LANES)),
        zl=f32(np.tile(zc.T, (wide, 1))),
        k_parts=k_parts, m_parts=m_parts,
    )


def run(kernel, outs, *args, scratch=(), free=(), limit=16):
    spaces = [pltpu.SMEM if a.dtype == jnp.int32 else pltpu.VMEM for a in args]
    size = sum(math.prod(s) for s in outs) + sum(math.prod(a.shape) for a in args)
    return pl.pallas_call(
        kernel,
        out_shape=[(jax.ShapeDtypeStruct if i in free else pltpu.VMEM)(shape, jnp.float32) for i, shape in enumerate(outs)],
        in_specs=[pl.BlockSpec(memory_space=space) for space in spaces],
        out_specs=[pl.BlockSpec(memory_space=pltpu.VMEM)] * len(outs),
        scratch_shapes=[pltpu.VMEM(shape, jnp.float32) for shape in scratch],
        compiler_params=pltpu.CompilerParams(vmem_limit_bytes=limit << 20),
        cost_estimate=pl.CostEstimate(flops=2 * 6 * 160 * 240 * 168, bytes_accessed=4 * size, transcendentals=0),
    )(*args)


def total(value):
    return jnp.sum(jnp.sum(value, axis=1, keepdims=True), axis=0, keepdims=True)


def total_row(row):
    return jnp.sum(row, axis=1, keepdims=True)


def as_col(row, eye):
    return jnp.sum(eye * row, axis=1, keepdims=True)


def as_row(col, eye):
    return jnp.sum(eye * col, axis=0, keepdims=True)


def lane_put(values):
    lane = lax.broadcasted_iota(jnp.int32, (1, LANES), 1)
    row = jnp.zeros((1, LANES), jnp.float32)
    for spot, value in enumerate(values):
        row = jnp.where(lane == spot, value, row)
    return row


def lane_get(row, spot):
    lane = lax.broadcasted_iota(jnp.int32, row.shape, 1)
    return jnp.sum(jnp.where(lane == spot, row, 0.0), axis=1, keepdims=True)


def lane_sel(spot):
    lane = lax.broadcasted_iota(jnp.int32, (1, LANES), 1)
    return jnp.where(lane // 8 == spot, 1.0, 0.0).astype(jnp.float32)


def span_mask(shape, axis, size, move):
    row = lax.broadcasted_iota(jnp.int32, shape, axis) & 7
    start = row * size + move
    fine = lax.broadcasted_iota(jnp.int32, shape, 1 - axis)
    return jnp.where((fine >= start) & (fine < start + size), 1.0, 0.0).astype(jnp.float32)


def rows_tile(rows):
    spot = lax.broadcasted_iota(jnp.int32, (8, LANES), 0)
    tile = jnp.zeros((8, LANES), jnp.float32)
    for place, row in enumerate(rows):
        tile = jnp.where(spot == place, row, tile)
    return tile


def first_kernel(k_parts, m_parts, width, idx_ref, b_ref, k_ref, m_ref, x_ref, out_ref, scr):
    k, m = k_ref[...], m_ref[...]
    e11, e12, e22 = (k * k_parts[name] + m * m_parts[name] for name in ("11", "12", "22"))
    nz, ez = b_ref.shape[2], k.shape[1]
    per, span = ez // 8, nz // 8
    sel = lane_sel(idx_ref[0])
    owner = span_mask((8, ez), 0, per, 0)
    after = span_mask((8, ez), 0, per, -1) + span_mask((8, ez), 0, per, ez - 1)
    owner_t = span_mask((ez, LANES), 1, per, 0)
    after_t = span_mask((ez, LANES), 1, per, -1) + span_mask((ez, LANES), 1, per, ez - 1)
    small = (dot(owner * e11 + after * e12, owner_t) + dot(owner * e12 + after * e22, after_t)) * sel
    acc = b_ref[1]
    for x in range(2, 7):
        acc = acc + b_ref[x]
    line = jnp.sum(acc[1:7], axis=0, keepdims=True)
    rc = dot(line, span_mask((nz, LANES), 1, span, 0)) * sel
    scr[...] = jnp.zeros_like(scr)
    scr[:, :LANES] = small
    scr[0:1, LANES : 2 * LANES] = rc
    scr[1:2, LANES : LANES + ez] = k
    scr[2:3, LANES : LANES + ez] = m
    for x in range(7):
        scr[:7, 2 * LANES + nz * x : 2 * LANES + nz * (x + 1)] = b_ref[x]
    for peer in range(out_ref.shape[0]):
        out_ref[peer, :, :width] = x_ref[:, peer * width : (peer + 1) * width]
        out_ref[peer, :, width:] = scr[...]


def split_group(group_ref, width):
    rows = group_ref.shape[0] * group_ref.shape[1]
    return group_ref[:, :, :width].reshape(rows, width), group_ref[:, :, width : width + LANES].reshape(rows, LANES)


def spread(out_ref, row):
    out_ref[...] = jnp.broadcast_to(row[None], out_ref.shape)


def coarse_in_kernel(width, idx_ref, xl_ref, eye_ref, out_ref, bx_ref, hi_ref, lo_ref, k_ref, m_ref, group_ref, rc_ref):
    factor, _ = split_group(xl_ref, width)
    rc = jnp.sum(xl_ref[:, 0:1, width + LANES : width + 2 * LANES], axis=0)
    rc_ref[...] = rc
    group_ref[...] = xl_ref[:, :, : width + LANES]
    rows = factor.shape[0]
    rc_col = as_col(rc, eye_ref[:rows])
    part = jnp.sum(rc_col * factor, axis=0, keepdims=True)
    spread(out_ref, part)
    count = xl_ref.shape[0]
    nz, ez = bx_ref.shape[2], k_ref.shape[1]
    base = width + 2 * LANES
    place = 0
    for apart in range(-4, 5):
        slot = lax.rem(idx_ref[0] + (apart + 2 * count), count)
        for x in (6,) if apart == -4 else (0, 1) if apart == 4 else range(7):
            bx_ref[place] = xl_ref[slot, :, base + nz * x : base + nz * (x + 1)]
            place += 1
        if -4 < apart < 4:
            k_ref[apart + 3 : apart + 4] = xl_ref[slot, 1:2, width + LANES : width + LANES + ez]
            m_ref[apart + 3 : apart + 4] = xl_ref[slot, 2:3, width + LANES : width + LANES + ez]
    k_ref[7:8] = k_ref[6:7]
    m_ref[7:8] = m_ref[6:7]
    hi_ref[...] = bx_ref[:, 6:7]
    lo_ref[...] = bx_ref[:, 0:2]


def coarse_out_kernel(width, sums_ref, xl_ref, eye_ref, h_ref, out_ref):
    factor, _ = split_group(xl_ref, width)
    rows = factor.shape[0]
    sums = jnp.sum(sums_ref[...], axis=0)
    part = jnp.sum(factor * sums[:, :width], axis=1, keepdims=True)
    x_part = as_row(part, eye_ref[:rows])
    spot = lax.broadcasted_iota(jnp.int32, (8, LANES), 0)
    tile = jnp.where(spot == 0, x_part, h_ref[...])
    out_ref[...] = jnp.broadcast_to(tile[None], out_ref.shape)


def coarse_mid_kernel(width, got_ref, xl_ref, rc_ref, eye_ref, out_ref, x_ref):
    factor, small = split_group(xl_ref, width)
    rc = rc_ref[...]
    rows = factor.shape[0]
    eye = eye_ref[:rows]
    got = jnp.sum(got_ref[...], axis=0)
    x0, h, scal = got[0:1], got[1:2], got[2:3]
    rc1_col = jnp.sum(small * x0 + eye * h, axis=1, keepdims=True)
    rc1 = as_row(rc1_col, eye)
    part = jnp.sum(rc1_col * factor, axis=0, keepdims=True)
    rho = lane_get(scal, 0) + total_row(rc * x0)
    den = lane_get(scal, 1) + total_row(x0 * (h + rc1))
    spread(out_ref, jnp.concatenate([part, lane_put([rho, den])], axis=1))
    x_ref[...] = x0


def pair_kernel(width, idx_ref, sums_ref, xl_ref, eye_ref, b_ref, q_ref, u_ref, au_ref, s_ref, as_ref, inner_ref, zct_ref,
                out_ref, scal_ref, r_ref):
    factor, _ = split_group(xl_ref, width)
    rows = factor.shape[0]
    sums = jnp.sum(sums_ref[...], axis=0)
    part = jnp.sum(factor * sums[:, :width], axis=1, keepdims=True)
    x_part = as_row(part, eye_ref[:rows])
    scal = sums[:, width:]
    rho, den = lane_get(scal, 0), lane_get(scal, 1)
    step = rho / den
    sel = lane_sel(idx_ref[0])
    r_ref[...] = jnp.zeros_like(r_ref)
    for x in range(7):
        r_ref[x, :7] = b_ref[x] - step * q_ref[x, :7]
    nz = b_ref.shape[2]
    flat = lambda ref: ref[...].reshape(64, nz)
    resid = flat(r_ref)
    t = flat(u_ref) - step * flat(s_ref)
    at = flat(au_ref) - step * flat(as_ref)
    inner = inner_ref[...]
    wr = dot(jnp.sum(inner * resid, axis=0, keepdims=True), zct_ref[...]) * sel
    wt = dot(jnp.sum(inner * at, axis=0, keepdims=True), zct_ref[...]) * sel
    tile = rows_tile([x_part, wr, wt, lane_put([total(resid * t), total(t * at)])])
    out_ref[...] = jnp.broadcast_to(tile[None], out_ref.shape)
    scal_ref[...] = lane_put([rho, den])


def last_in_kernel(width, got_ref, xl_ref, x0_ref, scal_ref, eye_ref, out_ref, x_ref):
    _, small = split_group(xl_ref, width)
    eye = eye_ref[: small.shape[0]]
    got = jnp.sum(got_ref[...], axis=0)
    x1, wr, wt, scal = got[0:1], got[1:2], got[2:3], got[3:4]
    step = lane_get(scal_ref[...], 0) / lane_get(scal_ref[...], 1)
    c = x0_ref[...] - step * x1
    tc = as_row(jnp.sum(small * c, axis=1, keepdims=True), eye)
    rho1 = lane_get(scal, 0) + total_row(wr * c)
    en1 = lane_get(scal, 1) + total_row(c * (2.0 * wt + tc))
    spread(out_ref, lane_put([rho1, en1]))
    x_ref[...] = x1


def final_kernel(sums_ref, scal_ref, p_ref, w_ref, r_ref, qo_ref, v_ref, vl_ref, sol_ref, res_ref):
    got = jnp.sum(sums_ref[...], axis=0)
    rho1, en1 = lane_get(got, 0), lane_get(got, 1)
    rho, den = lane_get(scal_ref[...], 0), lane_get(scal_ref[...], 1)
    step = rho / den
    beta = rho1 / rho
    step1 = rho1 / (en1 - beta * rho1 / step)
    p_mult = step + step1 * (1.0 + beta)
    w_mult = step1 * step
    q_mult = step1 * (1.0 + beta)
    for x in range(7):
        sol_ref[x] = p_mult * p_ref[x, :7] - w_mult * w_ref[x, :7]
        top = w_mult * vl_ref[x]
        res_ref[x] = r_ref[x, :7] - q_mult * qo_ref[x, :7] + w_mult * v_ref[x, :7]
        res_ref[x, 0:1] = res_ref[x, 0:1] + top


SOLVE = ("rep10", "lam_ab", "lam_c", "qq", "qqt", "zf", "zft")
APPLY = ("rep8", "wz", "g8", "g8t", "zk", "kk", "ww")


def apply(block, k, m, rep8, wz, g8, g8t, zk, kk, ww):
    k_line, m_line = dot(k, rep8), dot(m, rep8) * wz
    spread_u = dot(block, g8)
    out = (k_line * wz) * dot(kk, spread_u) + ww * (k_line * dot(block, zk) + m_line * spread_u)
    return dot(out, g8t)


def solve_columns(block, k_ref, m_ref, first, count, consts, lines, acc):
    rep10, lam_ab, lam_c, qq, qqt, zf, zft = consts
    lines[...] = dot(block, zf[...])
    acc[...] = jnp.zeros_like(acc)
    lam = lam_ab[...] + lam_c[...]
    for c in range(count):
        k, m = k_ref[first + c : first + c + 1], m_ref[first + c : first + c + 1]
        den = dot(k, rep10[...]) * lam + dot(m, rep10[...])
        spectral = dot(qqt[...], lines[112 * c : 112 * c + 160]) / den
        low = max(128 - 112 * c, 0)
        high = min(112 * (count - 1) + 32 - 112 * c, 160)
        start = 112 * c + low - 128
        acc[start : start + high - low] = acc[start : start + high - low] + dot(qq[low:high], spectral)
    return dot(acc[...], zft[...])


def schwarz_b_kernel(bx_ref, yl_ref, yh_ref, k_ref, m_ref, *refs):
    consts, (out_ref, hi_ref, lo_ref, scr, lines, acc) = refs[:-6], refs[-6:]
    nz = bx_ref.shape[2]
    scr[...] = jnp.zeros_like(scr)
    scr[:, 1:8] = bx_ref[:, 0:7]
    scr[:, 0:1] = yl_ref[...]
    scr[:, 8:10] = yh_ref[...]
    out = solve_columns(scr[...].reshape(52 * 16, nz), k_ref, m_ref, 0, 7, consts, lines, acc)
    out_ref[...] = out.reshape(36, 16, nz)
    hi_ref[...] = out_ref[:, 8:10]
    lo_ref[...] = out_ref[:, 0:2]


def schwarz_q_kernel(qx_ref, yl_ref, yh_ref, k_ref, m_ref, *refs):
    consts, (q_ref, out_ref, hi_ref, lo_ref, scr, lines, acc) = refs[:-7], refs[-7:]
    nz = qx_ref.shape[2]
    scr[...] = jnp.zeros_like(scr)
    scr[:, 1:9] = qx_ref[...]
    scr[:, 0:1] = yl_ref[:, 0:1]
    scr[:, 1:2] = scr[:, 1:2] + yl_ref[:, 1:2]
    scr[:, 8:9] = scr[:, 8:9] + yh_ref[:, 0:1]
    scr[:, 9:10] = yh_ref[:, 1:2]
    q_ref[...] = scr[8:16, 1:9]
    out = solve_columns(scr[...].reshape(24 * 16, nz), k_ref, m_ref, 2, 3, consts, lines, acc)
    out_ref[...] = out.reshape(8, 16, nz)
    hi_ref[...] = out_ref[:, 8:10]
    lo_ref[...] = out_ref[:, 0:2]


def gather_s(u_ref, y_ref, yl_ref, yh_ref):
    u_ref[...] = y_ref[:, 1:9]
    u_ref[:, 0:2] = u_ref[:, 0:2] + yl_ref[...]
    u_ref[:, 6:8] = u_ref[:, 6:8] + yh_ref[...]


def apply_u_kernel(idx_ref, b_ref, y_ref, yl_ref, yh_ref, k_ref, m_ref, inner_ref, zct_ref, *refs):
    consts, (u_ref, own_ref, au_ref, h_ref) = refs[:-4], refs[-4:]
    nz = u_ref.shape[2]
    gather_s(u_ref, y_ref, yl_ref, yh_ref)
    own_ref[...] = u_ref[14:22]
    u = own_ref[...].reshape(64, nz)
    au = apply(u, k_ref[...], m_ref[...], *(ref[...] for ref in consts))
    au_ref[...] = au.reshape(8, 8, nz)
    h = dot(jnp.sum(inner_ref[...] * au, axis=0, keepdims=True), zct_ref[...]) * lane_sel(idx_ref[0])
    acc = b_ref[0] * own_ref[0, :7]
    for x in range(1, 7):
        acc = acc + b_ref[x] * own_ref[x, :7]
    h_ref[...] = rows_tile([jnp.zeros((1, LANES), jnp.float32), h, lane_put([total(acc), total(u * au)])])


def apply_s_kernel(y_ref, yl_ref, yh_ref, k_ref, m_ref, *refs):
    consts, (s_ref, as_ref, hi_ref) = refs[:-3], refs[-3:]
    nz = s_ref.shape[2]
    gather_s(s_ref, y_ref, yl_ref, yh_ref)
    out = apply(s_ref[...].reshape(64, nz), k_ref[...], m_ref[...], *(ref[...] for ref in consts))
    as_ref[...] = out.reshape(8, 8, nz)
    hi_ref[...] = as_ref[7:8]


def apply_p_kernel(idx_ref, u_ref, x_ref, k_ref, m_ref, inner_ref, zl_ref, *refs):
    (rep8, wz, g8, g8t, zk, kk, ww), (p_ref, q_ref, hi_ref, lo_ref, field, su, sk, acc) = refs[:-8], refs[-8:]
    nz = u_ref.shape[2]
    count = idx_ref[1]
    x0 = x_ref[...]
    picks = [x0 * lane_sel(lax.rem(idx_ref[0] + (apart + 2 * count), count)) for apart in range(-2, 3)]
    lines = dot(rows_tile(picks), zl_ref[...])
    field[...] = u_ref[...]
    side = inner_ref[8:16]
    for c in range(5):
        add = side * lines[c : c + 1]
        for x in range(7 * c + 1, 7 * c + 7):
            field[x] = field[x] + add
    p_ref[...] = field[14:22]
    whole = field[...].reshape(36 * 8, nz)
    su[...] = dot(whole, g8[...])
    sk[...] = dot(whole, zk[...])
    acc[...] = jnp.zeros_like(acc)
    for c in range(5):
        k_line = dot(k_ref[c + 1 : c + 2], rep8[...])
        m_line = dot(m_ref[c + 1 : c + 2], rep8[...]) * wz[...]
        part = slice(56 * c, 56 * c + 64)
        u = su[part]
        out = (k_line * wz[...]) * dot(kk[...], u) + ww[...] * (k_line * sk[part] + m_line * u)
        acc[part] = acc[part] + out
    q_ref[...] = dot(acc[48:240], g8t[...]).reshape(24, 8, nz)
    hi_ref[...] = q_ref[:, 6:8]
    lo_ref[...] = q_ref[:, 0:2]


def apply_w_kernel(idx_ref, s_ref, x_ref, side_ref, k_ref, m_ref, ks_ref, inner_ref, zl_ref, face_ref, *refs):
    consts, (w_ref, v_ref, hi_ref) = refs[:-3], refs[-3:]
    rep8, wz, g8, g8t = consts[:4]
    nz = s_ref.shape[2]
    x1 = x_ref[...]
    left = lax.rem(idx_ref[0] + idx_ref[1] - 1, idx_ref[1])
    lines = dot(rows_tile([x1 * lane_sel(idx_ref[0]), x1 * lane_sel(left)]), zl_ref[...])
    w = s_ref[...].reshape(64, nz) + inner_ref[...] * lines[0:1]
    w_ref[...] = w.reshape(8, 8, nz)
    out = apply(w, k_ref[...], m_ref[...], *(ref[...] for ref in consts)).reshape(8, 8, nz)
    v_ref[...] = out
    scale = dot(ks_ref[2:3], rep8[...]) * wz[...]
    share = dot(scale * dot(lines, g8[...]), g8t[...])[1:2]
    v_ref[0] = v_ref[0] + side_ref[0] + face_ref[...] * share
    hi_ref[...] = v_ref[0:7, 7:8]


def shift(value, axis, step):
    count = lax.axis_size(axis)
    return lax.ppermute(value, axis, [(i, (i + step) % count) for i in range(count)])


def local(right_side, stiff_coef, mass_coef, coarse_factor):
    nz = right_side.shape[2]
    c_dev, n_coarse = coarse_factor.shape
    ez = stiff_coef.shape[2]
    n_gx, n_gy = lax.axis_size("gx"), lax.axis_size("gy")
    width = n_coarse // n_gx
    tab = {name: jnp.asarray(value) if isinstance(value, np.ndarray) else value for name, value in make_tables(ez, c_dev).items()}
    k = stiff_coef.reshape(1, ez)
    m = mass_coef.reshape(1, ez)
    b = right_side
    idx = jnp.stack([lax.axis_index("gx"), jnp.int32(n_gx)])
    solve_tab = [tab[name] for name in SOLVE]
    apply_tab = [tab[name] for name in APPLY]
    inner, zct, zl, eye = (tab[name] for name in ("inner", "zct", "zl", "eye"))

    def kernel(fn, *fixed):
        def call(*refs):
            return fn(*fixed, *refs)

        call.__name__ = fn.__name__
        return call

    def swap_gx(value):
        return lax.all_to_all(value, "gx", 0, 0)

    def swap_gy(value):
        return lax.all_to_all(value, "gy", 0, 0)

    group = (n_gx, c_dev, LANES)
    aux = -(-(2 * LANES + 7 * nz) // LANES) * LANES
    (pay,) = run(kernel(first_kernel, tab["k_parts"], tab["m_parts"], width), [(n_gx, c_dev, width + aux)],
                 idx, b, k, m, coarse_factor, scratch=[(8, aux)], limit=56)
    xl = swap_gx(pay)

    outs = [(n_gy, 1, width), (52, 8, nz), (52, 1, nz), (52, 2, nz), (8, ez), (8, ez),
            (n_gx, c_dev, width + LANES), (1, LANES)]
    pay, bx, hi, lo, ks, ms, members, rc = run(kernel(coarse_in_kernel, width), outs, idx, xl, eye, free=(0,))
    y_low, y_high = shift(hi, "gy", 1), shift(lo, "gy", -1)
    sums = swap_gy(pay)

    sides = [(8, 2, nz), (8, 2, nz)]
    y, hi, lo = run(schwarz_b_kernel, [(36, 16, nz), (36, 2, nz), (36, 2, nz)], bx, y_low, y_high, ks, ms, *solve_tab,
                    scratch=[(52, 16, nz), (832, 10 * ez), (576, 10 * ez)])
    y_low, y_high = shift(hi, "gy", 1), shift(lo, "gy", -1)
    cube = (8, 8, nz)
    wide_u, u, au, h = run(apply_u_kernel, [(36, 8, nz), cube, cube, (8, LANES)], idx, b, y, y_low, y_high, k, m, inner, zct, *apply_tab,
                          free=(1, 2))

    (pay,) = run(kernel(coarse_out_kernel, width), [group], sums, members, eye, h)
    got = swap_gx(pay)
    pay, x0 = run(kernel(coarse_mid_kernel, width), [(n_gy, 1, width + LANES), (1, LANES)], got, members, rc, eye, free=(0,))
    sums = swap_gy(pay)

    p, qx, hi, lo = run(apply_p_kernel, [cube, (24, 8, nz), (24, 2, nz), (24, 2, nz)], idx, wide_u, x0, ks, ms, inner, zl, *apply_tab,
                        scratch=[(36, 8, nz)] + [(288, 8 * ez)] * 3)
    y_low, y_high = shift(hi, "gy", 1), shift(lo, "gy", -1)
    q, y, hi, lo = run(schwarz_q_kernel, [cube, (8, 16, nz)] + sides, qx, y_low, y_high, ks, ms, *solve_tab,
                       scratch=[(24, 16, nz), (384, 10 * ez), (128, 10 * ez)])
    y_low, y_high = shift(hi, "gy", 1), shift(lo, "gy", -1)
    s, a_s, hi = run(apply_s_kernel, [cube, cube, (1, 8, nz)], y, y_low, y_high, k, m, *apply_tab)
    side = shift(hi, "gx", 1)

    pay, scal, resid = run(kernel(pair_kernel, width), [group, (1, LANES), cube], idx, sums, members, eye, b, q, u, au, s, a_s, inner, zct)
    got = swap_gx(pay)
    pay, x1 = run(kernel(last_in_kernel, width), [(n_gy, 1, LANES), (1, LANES)], got, members, x0, scal, eye, free=(0,))
    sums = swap_gy(pay)

    w, v, hi = run(apply_w_kernel, [cube, cube, (7, 1, nz)], idx, s, x1, side, k, m, ks, inner, zl, tab["face"], *apply_tab)
    y_low = shift(hi, "gy", 1)
    sol, res = run(final_kernel, [(7, 7, nz), (7, 7, nz)], sums, scal, p, w, resid, q, v, y_low, free=(0, 1))
    return sol, res


def solution(mesh):
    placed = (P("gx", "gy", None), P("gx", "gy", None), P("gx", "gy", None), P(("gx", "gy"), None))

    return jax.shard_map(
        local,
        mesh=mesh,
        in_specs=placed,
        out_specs=(P("gx", "gy", None), P("gx", "gy", None)),
        check_vma=False,
    )
```

```python
import math

import jax
import jax.numpy as jnp
import numpy as np
from jax import lax
from jax.experimental import pallas as pl
from jax.experimental.pallas import tpu as pltpu
from jax.sharding import PartitionSpec as P


HI = lax.Precision.HIGHEST
LANES = 128


def legendre_pair(position, degree):
    p_prev = 1.0
    p_now = position
    for order in range(2, degree + 1):
        p_next = ((2 * order - 1) * position * p_now - (order - 1) * p_prev) / order
        p_prev = p_now
        p_now = p_next
    return (p_now, p_prev)


def jacobi_eigen(matrix):
    size_n = matrix.shape[0]
    current = np.array(matrix)
    vectors = np.eye(size_n)
    for _ in range(20):
        for row_p in range(size_n - 1):
            for row_q in range(row_p + 1, size_n):
                off_value = current[row_p, row_q]
                if abs(off_value) > 1e-300:
                    theta = (current[row_q, row_q] - current[row_p, row_p]) / (2.0 * off_value)
                    sign_t = 1.0 if theta >= 0.0 else -1.0
                    tangent = sign_t / (abs(theta) + math.sqrt(theta * theta + 1.0))
                    cosine = 1.0 / math.sqrt(tangent * tangent + 1.0)
                    sine = tangent * cosine
                    rotation = np.eye(size_n)
                    rotation[row_p, row_p] = cosine
                    rotation[row_q, row_q] = cosine
                    rotation[row_p, row_q] = sine
                    rotation[row_q, row_p] = -sine
                    current = rotation.T @ current @ rotation
                    vectors = vectors @ rotation
    return (np.array([current[idx, idx] for idx in range(size_n)]), vectors)


def gll_tables():
    degree = 7
    guesses = [
        -0.8717401485096066,
        -0.5917001814331423,
        -0.2092992179024789,
        0.2092992179024789,
        0.5917001814331423,
        0.8717401485096066,
    ]
    interior = []
    for guess in guesses:
        position = guess
        for _ in range(30):
            p_now, p_prev = legendre_pair(position, degree)
            first = degree * (position * p_now - p_prev) / (position * position - 1.0)
            second = (2.0 * position * first - degree * (degree + 1) * p_now) / (
                1.0 - position * position
            )
            position = position - first / second
        interior.append(position)
    points = np.array([-1.0] + interior + [1.0])
    values = np.array([legendre_pair(float(pt), degree)[0] for pt in points])
    weights = 2.0 / (degree * (degree + 1) * values**2)
    deriv_mat = np.zeros((8, 8))
    for left_idx in range(8):
        for right_idx in range(8):
            if left_idx != right_idx:
                deriv_mat[left_idx, right_idx] = values[left_idx] / (
                    values[right_idx] * (points[left_idx] - points[right_idx])
                )
    deriv_mat[0, 0] = -degree * (degree + 1) / 4.0
    deriv_mat[7, 7] = degree * (degree + 1) / 4.0
    stiffness = deriv_mat.T @ (weights[:, None] * deriv_mat)
    ext_stiff = np.zeros((10, 10))
    ext_stiff[1:9, 1:9] += stiffness
    ext_stiff[0:2, 0:2] += stiffness[6:8, 6:8]
    ext_stiff[8:10, 8:10] += stiffness[0:2, 0:2]
    ext_mass = np.zeros(10)
    ext_mass[1:9] += weights
    ext_mass[0:2] += weights[6:8]
    ext_mass[8:10] += weights[0:2]
    inv_root = 1.0 / np.sqrt(ext_mass)
    eigen_vals, eigen_vecs = jacobi_eigen(inv_root[:, None] * ext_stiff * inv_root[None, :])
    eigen_basis = inv_root[:, None] * eigen_vecs
    return (stiffness, weights, eigen_basis, eigen_vals)


def dot(left, right):
    return jnp.dot(left, right, precision=HI, preferred_element_type=jnp.float32)


def make_tables(ez, c_dev):
    stiffness, weights, basis, vals = gll_tables()
    stiffness = stiffness.astype(np.float32).astype(np.float64)
    weights = weights.astype(np.float32).astype(np.float64)
    basis = basis.astype(np.float32).astype(np.float64)
    vals = vals.astype(np.float32).astype(np.float64)
    nz = 7 * ez
    span = nz // c_dev
    f32 = lambda table: np.asarray(table, np.float32)

    qq = np.zeros((10, 16, 10, 16))
    qq[:, :10, :, :10] = np.einsum("ia,jb->ijab", basis, basis)
    qq = qq.reshape(160, 160)
    lam_ab = np.ones((10, 16))
    lam_ab[:, :10] = vals[:, None] + vals[None, :]
    lam_c = np.repeat(vals, ez)[None]
    zf = np.zeros((nz, 10, ez))
    g8 = np.zeros((nz, 8, ez))
    zk = np.zeros((nz, 8, ez))
    for elem in range(ez):
        for k in range(10):
            zf[(7 * elem - 1 + k) % nz, :, elem] += basis[k]
        for k in range(8):
            g8[(7 * elem + k) % nz, k, elem] += 1.0
            zk[(7 * elem + k) % nz, :, elem] += stiffness[:, k]
    zf, g8, zk = zf.reshape(nz, -1), g8.reshape(nz, -1), zk.reshape(nz, -1)
    diag = np.diag(weights)
    kk = np.einsum("ai,bj->abij", stiffness, diag) + np.einsum("ai,bj->abij", diag, stiffness)
    kk = kk.reshape(64, 64)
    ww = np.outer(weights, weights).reshape(64, 1)
    inner = np.zeros((8, 8))
    inner[1:7, 1:7] = 1.0
    plate = inner.reshape(64, 1)
    first = np.array([1.0] * 7 + [0.0])
    last = 1.0 - first
    face = np.zeros((8, 1))
    face[1:7, 0] = weights[1:7] * np.sum(stiffness[7, 1:7])
    k_parts = {}
    m_parts = {}
    for name, left, right in (("11", first, first), ("12", first, last), ("22", last, last)):
        wz = float(np.sum(left * weights * right))
        kz = float(left @ stiffness @ right)
        k_parts[name] = float((plate.T @ kk @ plate).item()) * wz + float(np.sum(plate * ww)) * kz
        m_parts[name] = float(np.sum(plate * ww)) * wz
    wide = LANES // c_dev
    zc = (np.arange(nz)[:, None] // span == np.arange(c_dev)[None, :]).astype(np.float64)
    return dict(
        qq=f32(qq), qqt=f32(qq.T), zf=f32(zf), zft=f32(zf.T), lam_ab=f32(lam_ab.reshape(160, 1)), lam_c=f32(lam_c),
        rep10=f32(np.tile(np.eye(ez), (1, 10))), rep8=f32(np.tile(np.eye(ez), (1, 8))),
        g8=f32(g8), g8t=f32(g8.T), zk=f32(zk), kk=f32(kk), ww=f32(ww), wz=f32(np.repeat(weights, ez)[None]),
        inner=f32(plate), face=f32(face),
        zct=f32(np.tile(zc, (1, wide))), eye=f32(np.eye(LANES)),
        zl=f32(np.tile(zc.T, (wide, 1))),
        k_parts=k_parts, m_parts=m_parts,
    )


def run(kernel, outs, *args, scratch=(), free=(), limit=16):
    spaces = [pltpu.SMEM if a.dtype == jnp.int32 else pltpu.VMEM for a in args]
    size = sum(math.prod(s) for s in outs) + sum(math.prod(a.shape) for a in args)
    return pl.pallas_call(
        kernel,
        out_shape=[(jax.ShapeDtypeStruct if i in free else pltpu.VMEM)(shape, jnp.float32) for i, shape in enumerate(outs)],
        in_specs=[pl.BlockSpec(memory_space=space) for space in spaces],
        out_specs=[pl.BlockSpec(memory_space=pltpu.VMEM)] * len(outs),
        scratch_shapes=[pltpu.VMEM(shape, jnp.float32) for shape in scratch],
        compiler_params=pltpu.CompilerParams(vmem_limit_bytes=limit << 20),
        cost_estimate=pl.CostEstimate(flops=2 * 6 * 160 * 240 * 168, bytes_accessed=4 * size, transcendentals=0),
    )(*args)


def total(value):
    return jnp.sum(jnp.sum(value, axis=1, keepdims=True), axis=0, keepdims=True)


def total_row(row):
    return jnp.sum(row, axis=1, keepdims=True)


def as_col(row, eye):
    return jnp.sum(eye * row, axis=1, keepdims=True)


def as_row(col, eye):
    return jnp.sum(eye * col, axis=0, keepdims=True)


def lane_put(values):
    lane = lax.broadcasted_iota(jnp.int32, (1, LANES), 1)
    row = jnp.zeros((1, LANES), jnp.float32)
    for spot, value in enumerate(values):
        row = jnp.where(lane == spot, value, row)
    return row


def lane_get(row, spot):
    lane = lax.broadcasted_iota(jnp.int32, row.shape, 1)
    return jnp.sum(jnp.where(lane == spot, row, 0.0), axis=1, keepdims=True)


def lane_sel(spot):
    lane = lax.broadcasted_iota(jnp.int32, (1, LANES), 1)
    return jnp.where(lane // 8 == spot, 1.0, 0.0).astype(jnp.float32)


def span_mask(shape, axis, size, move):
    row = lax.broadcasted_iota(jnp.int32, shape, axis) & 7
    start = row * size + move
    fine = lax.broadcasted_iota(jnp.int32, shape, 1 - axis)
    return jnp.where((fine >= start) & (fine < start + size), 1.0, 0.0).astype(jnp.float32)


def rows_tile(rows):
    spot = lax.broadcasted_iota(jnp.int32, (8, LANES), 0)
    tile = jnp.zeros((8, LANES), jnp.float32)
    for place, row in enumerate(rows):
        tile = jnp.where(spot == place, row, tile)
    return tile


def first_kernel(k_parts, m_parts, width, idx_ref, b_ref, k_ref, m_ref, x_ref, out_ref, scr):
    k, m = k_ref[...], m_ref[...]
    e11, e12, e22 = (k * k_parts[name] + m * m_parts[name] for name in ("11", "12", "22"))
    nz, ez = b_ref.shape[2], k.shape[1]
    per, span = ez // 8, nz // 8
    sel = lane_sel(idx_ref[0])
    owner = span_mask((8, ez), 0, per, 0)
    after = span_mask((8, ez), 0, per, -1) + span_mask((8, ez), 0, per, ez - 1)
    owner_t = span_mask((ez, LANES), 1, per, 0)
    after_t = span_mask((ez, LANES), 1, per, -1) + span_mask((ez, LANES), 1, per, ez - 1)
    small = (dot(owner * e11 + after * e12, owner_t) + dot(owner * e12 + after * e22, after_t)) * sel
    acc = b_ref[1]
    for x in range(2, 7):
        acc = acc + b_ref[x]
    line = jnp.sum(acc[1:7], axis=0, keepdims=True)
    rc = dot(line, span_mask((nz, LANES), 1, span, 0)) * sel
    scr[...] = jnp.zeros_like(scr)
    scr[:, :LANES] = small
    scr[0:1, LANES : 2 * LANES] = rc
    scr[1:2, LANES : LANES + ez] = k
    scr[2:3, LANES : LANES + ez] = m
    for x in range(7):
        scr[:7, 2 * LANES + nz * x : 2 * LANES + nz * (x + 1)] = b_ref[x]
    for peer in range(out_ref.shape[0]):
        out_ref[peer, :, :width] = x_ref[:, peer * width : (peer + 1) * width]
        out_ref[peer, :, width:] = scr[...]


def split_group(group_ref, width):
    rows = group_ref.shape[0] * group_ref.shape[1]
    return group_ref[:, :, :width].reshape(rows, width), group_ref[:, :, width : width + LANES].reshape(rows, LANES)


def spread(out_ref, row):
    out_ref[...] = jnp.broadcast_to(row[None], out_ref.shape)


def coarse_in_kernel(width, idx_ref, xl_ref, eye_ref, out_ref, bx_ref, hi_ref, lo_ref, k_ref, m_ref, group_ref, rc_ref):
    factor, _ = split_group(xl_ref, width)
    rc = jnp.sum(xl_ref[:, 0:1, width + LANES : width + 2 * LANES], axis=0)
    rc_ref[...] = rc
    group_ref[...] = xl_ref[:, :, : width + LANES]
    rows = factor.shape[0]
    rc_col = as_col(rc, eye_ref[:rows])
    part = jnp.sum(rc_col * factor, axis=0, keepdims=True)
    half = width // 2
    core = lax.broadcasted_iota(jnp.int32, out_ref.shape, 0) & 1
    out_ref[...] = jnp.where(core == 0, part[:, :half][None], part[:, half:][None])
    count = xl_ref.shape[0]
    nz, ez = bx_ref.shape[2], k_ref.shape[1]
    base = width + 2 * LANES
    place = 0
    for apart in range(-4, 5):
        slot = lax.rem(idx_ref[0] + (apart + 2 * count), count)
        for x in (6,) if apart == -4 else (0, 1) if apart == 4 else range(7):
            bx_ref[place] = xl_ref[slot, :, base + nz * x : base + nz * (x + 1)]
            place += 1
        if -4 < apart < 4:
            k_ref[apart + 3 : apart + 4] = xl_ref[slot, 1:2, width + LANES : width + LANES + ez]
            m_ref[apart + 3 : apart + 4] = xl_ref[slot, 2:3, width + LANES : width + LANES + ez]
    k_ref[7:8] = k_ref[6:7]
    m_ref[7:8] = m_ref[6:7]
    hi_ref[...] = bx_ref[:, 6:7]
    lo_ref[...] = bx_ref[:, 0:2]


def join_halves(width, idx_ref, mine_ref, other_ref):
    half = width // 2
    mine, other = mine_ref[:, :half], other_ref[:, :half]
    even = idx_ref[2] == 0
    return jnp.concatenate([jnp.where(even, mine, other), jnp.where(even, other, mine)], axis=1)


def coarse_out_kernel(width, idx_ref, mine_ref, other_ref, xl_ref, eye_ref, h_ref, out_ref):
    factor, _ = split_group(xl_ref, width)
    rows = factor.shape[0]
    part = jnp.sum(factor * join_halves(width, idx_ref, mine_ref, other_ref), axis=1, keepdims=True)
    x_part = as_row(part, eye_ref[:rows])
    spot = lax.broadcasted_iota(jnp.int32, (8, LANES), 0)
    tile = jnp.where(spot == 0, x_part, h_ref[...])
    out_ref[...] = jnp.broadcast_to(tile[None], out_ref.shape)


def coarse_mid_kernel(width, got_ref, xl_ref, rc_ref, eye_ref, out_ref, x_ref):
    factor, small = split_group(xl_ref, width)
    rc = rc_ref[...]
    rows = factor.shape[0]
    eye = eye_ref[:rows]
    got = jnp.sum(got_ref[...], axis=0)
    x0, h, scal = got[0:1], got[1:2], got[2:3]
    rc1_col = jnp.sum(small * x0 + eye * h, axis=1, keepdims=True)
    rc1 = as_row(rc1_col, eye)
    part = jnp.sum(rc1_col * factor, axis=0, keepdims=True)
    rho = lane_get(scal, 0) + total_row(rc * x0)
    den = lane_get(scal, 1) + total_row(x0 * (h + rc1))
    scal = lane_put([rho, den])
    half = width // 2
    core = lax.broadcasted_iota(jnp.int32, out_ref.shape, 0) & 1
    first = jnp.concatenate([part[:, :half], scal], axis=1)
    second = jnp.concatenate([part[:, half:], scal], axis=1)
    out_ref[...] = jnp.where(core == 0, first[None], second[None])
    x_ref[...] = x0


def sum_kernel(sums_ref, out_ref):
    out_ref[...] = jnp.sum(sums_ref[...], axis=0)


def pair_kernel(width, idx_ref, mine_ref, other_ref, xl_ref, eye_ref, b_ref, q_ref, u_ref, au_ref, s_ref, as_ref, inner_ref, zct_ref,
                out_ref, scal_ref, r_ref):
    factor, _ = split_group(xl_ref, width)
    rows = factor.shape[0]
    part = jnp.sum(factor * join_halves(width, idx_ref, mine_ref, other_ref), axis=1, keepdims=True)
    x_part = as_row(part, eye_ref[:rows])
    scal = mine_ref[:, width // 2 :]
    rho, den = lane_get(scal, 0), lane_get(scal, 1)
    step = rho / den
    sel = lane_sel(idx_ref[0])
    r_ref[...] = jnp.zeros_like(r_ref)
    for x in range(7):
        r_ref[x, :7] = b_ref[x] - step * q_ref[x, :7]
    nz = b_ref.shape[2]
    flat = lambda ref: ref[...].reshape(64, nz)
    resid = flat(r_ref)
    t = flat(u_ref) - step * flat(s_ref)
    at = flat(au_ref) - step * flat(as_ref)
    inner = inner_ref[...]
    wr = dot(jnp.sum(inner * resid, axis=0, keepdims=True), zct_ref[...]) * sel
    wt = dot(jnp.sum(inner * at, axis=0, keepdims=True), zct_ref[...]) * sel
    tile = rows_tile([x_part, wr, wt, lane_put([total(resid * t), total(t * at)])])
    out_ref[...] = jnp.broadcast_to(tile[None], out_ref.shape)
    scal_ref[...] = lane_put([rho, den])


def last_in_kernel(width, got_ref, xl_ref, x0_ref, scal_ref, eye_ref, out_ref, x_ref):
    _, small = split_group(xl_ref, width)
    eye = eye_ref[: small.shape[0]]
    got = jnp.sum(got_ref[...], axis=0)
    x1, wr, wt, scal = got[0:1], got[1:2], got[2:3], got[3:4]
    step = lane_get(scal_ref[...], 0) / lane_get(scal_ref[...], 1)
    c = x0_ref[...] - step * x1
    tc = as_row(jnp.sum(small * c, axis=1, keepdims=True), eye)
    rho1 = lane_get(scal, 0) + total_row(wr * c)
    en1 = lane_get(scal, 1) + total_row(c * (2.0 * wt + tc))
    spread(out_ref, lane_put([rho1, en1]))
    x_ref[...] = x1


def final_kernel(sums_ref, scal_ref, p_ref, w_ref, r_ref, qo_ref, v_ref, vl_ref, sol_ref, res_ref):
    got = jnp.sum(sums_ref[...], axis=0)
    rho1, en1 = lane_get(got, 0), lane_get(got, 1)
    rho, den = lane_get(scal_ref[...], 0), lane_get(scal_ref[...], 1)
    step = rho / den
    beta = rho1 / rho
    step1 = rho1 / (en1 - beta * rho1 / step)
    p_mult = step + step1 * (1.0 + beta)
    w_mult = step1 * step
    q_mult = step1 * (1.0 + beta)
    for x in range(7):
        sol_ref[x] = p_mult * p_ref[x, :7] - w_mult * w_ref[x, :7]
        top = w_mult * vl_ref[x]
        res_ref[x] = r_ref[x, :7] - q_mult * qo_ref[x, :7] + w_mult * v_ref[x, :7]
        res_ref[x, 0:1] = res_ref[x, 0:1] + top


SOLVE = ("rep10", "lam_ab", "lam_c", "qq", "qqt", "zf", "zft")
APPLY = ("rep8", "wz", "g8", "g8t", "zk", "kk", "ww")


def apply(block, k, m, rep8, wz, g8, g8t, zk, kk, ww):
    k_line, m_line = dot(k, rep8), dot(m, rep8) * wz
    spread_u = dot(block, g8)
    out = (k_line * wz) * dot(kk, spread_u) + ww * (k_line * dot(block, zk) + m_line * spread_u)
    return dot(out, g8t)


def solve_columns(block, k_ref, m_ref, first, count, consts, lines, acc):
    rep10, lam_ab, lam_c, qq, qqt, zf, zft = consts
    lines[...] = dot(block, zf[...])
    acc[...] = jnp.zeros_like(acc)
    lam = lam_ab[...] + lam_c[...]
    for c in range(count):
        k, m = k_ref[first + c : first + c + 1], m_ref[first + c : first + c + 1]
        den = dot(k, rep10[...]) * lam + dot(m, rep10[...])
        spectral = dot(qqt[...], lines[112 * c : 112 * c + 160]) / den
        low = max(128 - 112 * c, 0)
        high = min(112 * (count - 1) + 32 - 112 * c, 160)
        start = 112 * c + low - 128
        acc[start : start + high - low] = acc[start : start + high - low] + dot(qq[low:high], spectral)
    return dot(acc[...], zft[...])


def schwarz_b_kernel(bx_ref, yl_ref, yh_ref, k_ref, m_ref, *refs):
    consts, (out_ref, hi_ref, lo_ref, scr, lines, acc) = refs[:-6], refs[-6:]
    nz = bx_ref.shape[2]
    scr[...] = jnp.zeros_like(scr)
    scr[:, 1:8] = bx_ref[:, 0:7]
    scr[:, 0:1] = yl_ref[...]
    scr[:, 8:10] = yh_ref[...]
    out = solve_columns(scr[...].reshape(52 * 16, nz), k_ref, m_ref, 0, 7, consts, lines, acc)
    out_ref[...] = out.reshape(36, 16, nz)
    hi_ref[...] = out_ref[:, 8:10]
    lo_ref[...] = out_ref[:, 0:2]


def schwarz_q_kernel(qx_ref, yl_ref, yh_ref, k_ref, m_ref, *refs):
    consts, (q_ref, out_ref, hi_ref, lo_ref, scr, lines, acc) = refs[:-7], refs[-7:]
    nz = qx_ref.shape[2]
    scr[...] = jnp.zeros_like(scr)
    scr[:, 1:9] = qx_ref[...]
    scr[:, 0:1] = yl_ref[:, 0:1]
    scr[:, 1:2] = scr[:, 1:2] + yl_ref[:, 1:2]
    scr[:, 8:9] = scr[:, 8:9] + yh_ref[:, 0:1]
    scr[:, 9:10] = yh_ref[:, 1:2]
    q_ref[...] = scr[8:16, 1:9]
    out = solve_columns(scr[...].reshape(24 * 16, nz), k_ref, m_ref, 2, 3, consts, lines, acc)
    out_ref[...] = out.reshape(8, 16, nz)
    hi_ref[...] = out_ref[:, 8:10]
    lo_ref[...] = out_ref[:, 0:2]


def gather_s(u_ref, y_ref, yl_ref, yh_ref):
    u_ref[...] = y_ref[:, 1:9]
    u_ref[:, 0:2] = u_ref[:, 0:2] + yl_ref[...]
    u_ref[:, 6:8] = u_ref[:, 6:8] + yh_ref[...]


def apply_u_kernel(idx_ref, b_ref, y_ref, yl_ref, yh_ref, k_ref, m_ref, inner_ref, zct_ref, *refs):
    consts, (u_ref, own_ref, au_ref, h_ref) = refs[:-4], refs[-4:]
    nz = u_ref.shape[2]
    gather_s(u_ref, y_ref, yl_ref, yh_ref)
    own_ref[...] = u_ref[14:22]
    u = own_ref[...].reshape(64, nz)
    au = apply(u, k_ref[...], m_ref[...], *(ref[...] for ref in consts))
    au_ref[...] = au.reshape(8, 8, nz)
    h = dot(jnp.sum(inner_ref[...] * au, axis=0, keepdims=True), zct_ref[...]) * lane_sel(idx_ref[0])
    acc = b_ref[0] * own_ref[0, :7]
    for x in range(1, 7):
        acc = acc + b_ref[x] * own_ref[x, :7]
    h_ref[...] = rows_tile([jnp.zeros((1, LANES), jnp.float32), h, lane_put([total(acc), total(u * au)])])


def apply_s_kernel(y_ref, yl_ref, yh_ref, k_ref, m_ref, *refs):
    consts, (s_ref, as_ref, hi_ref) = refs[:-3], refs[-3:]
    nz = s_ref.shape[2]
    gather_s(s_ref, y_ref, yl_ref, yh_ref)
    out = apply(s_ref[...].reshape(64, nz), k_ref[...], m_ref[...], *(ref[...] for ref in consts))
    as_ref[...] = out.reshape(8, 8, nz)
    hi_ref[...] = as_ref[7:8]


def apply_p_kernel(idx_ref, u_ref, x_ref, k_ref, m_ref, inner_ref, zl_ref, *refs):
    (rep8, wz, g8, g8t, zk, kk, ww), (p_ref, q_ref, hi_ref, lo_ref, field, su, sk, acc) = refs[:-8], refs[-8:]
    nz = u_ref.shape[2]
    count = idx_ref[1]
    x0 = x_ref[...]
    picks = [x0 * lane_sel(lax.rem(idx_ref[0] + (apart + 2 * count), count)) for apart in range(-2, 3)]
    lines = dot(rows_tile(picks), zl_ref[...])
    field[...] = u_ref[...]
    side = inner_ref[8:16]
    for c in range(5):
        add = side * lines[c : c + 1]
        for x in range(7 * c + 1, 7 * c + 7):
            field[x] = field[x] + add
    p_ref[...] = field[14:22]
    whole = field[...].reshape(36 * 8, nz)
    su[...] = dot(whole, g8[...])
    sk[...] = dot(whole, zk[...])
    acc[...] = jnp.zeros_like(acc)
    for c in range(5):
        k_line = dot(k_ref[c + 1 : c + 2], rep8[...])
        m_line = dot(m_ref[c + 1 : c + 2], rep8[...]) * wz[...]
        part = slice(56 * c, 56 * c + 64)
        u = su[part]
        out = (k_line * wz[...]) * dot(kk[...], u) + ww[...] * (k_line * sk[part] + m_line * u)
        acc[part] = acc[part] + out
    q_ref[...] = dot(acc[48:240], g8t[...]).reshape(24, 8, nz)
    hi_ref[...] = q_ref[:, 6:8]
    lo_ref[...] = q_ref[:, 0:2]


def apply_w_kernel(idx_ref, s_ref, x_ref, side_ref, k_ref, m_ref, ks_ref, inner_ref, zl_ref, face_ref, *refs):
    consts, (w_ref, v_ref, hi_ref) = refs[:-3], refs[-3:]
    rep8, wz, g8, g8t = consts[:4]
    nz = s_ref.shape[2]
    x1 = x_ref[...]
    left = lax.rem(idx_ref[0] + idx_ref[1] - 1, idx_ref[1])
    lines = dot(rows_tile([x1 * lane_sel(idx_ref[0]), x1 * lane_sel(left)]), zl_ref[...])
    w = s_ref[...].reshape(64, nz) + inner_ref[...] * lines[0:1]
    w_ref[...] = w.reshape(8, 8, nz)
    out = apply(w, k_ref[...], m_ref[...], *(ref[...] for ref in consts)).reshape(8, 8, nz)
    v_ref[...] = out
    scale = dot(ks_ref[2:3], rep8[...]) * wz[...]
    share = dot(scale * dot(lines, g8[...]), g8t[...])[1:2]
    v_ref[0] = v_ref[0] + side_ref[0] + face_ref[...] * share
    hi_ref[...] = v_ref[0:7, 7:8]


def shift(value, axis, step):
    count = lax.axis_size(axis)
    return lax.ppermute(value, axis, [(i, (i + step) % count) for i in range(count)])


def local(right_side, stiff_coef, mass_coef, coarse_factor):
    nz = right_side.shape[2]
    c_dev, n_coarse = coarse_factor.shape
    ez = stiff_coef.shape[2]
    n_gx, n_gy = lax.axis_size("gx"), lax.axis_size("gy")
    width = n_coarse // n_gx
    tab = {name: jnp.asarray(value) if isinstance(value, np.ndarray) else value for name, value in make_tables(ez, c_dev).items()}
    k = stiff_coef.reshape(1, ez)
    m = mass_coef.reshape(1, ez)
    b = right_side
    idx = jnp.stack([lax.axis_index("gx"), jnp.int32(n_gx), lax.axis_index("gy") & 1])
    solve_tab = [tab[name] for name in SOLVE]
    apply_tab = [tab[name] for name in APPLY]
    inner, zct, zl, eye = (tab[name] for name in ("inner", "zct", "zl", "eye"))

    def kernel(fn, *fixed):
        def call(*refs):
            return fn(*fixed, *refs)

        call.__name__ = fn.__name__
        return call

    def swap_gx(value):
        return lax.all_to_all(value, "gx", 0, 0)

    def swap_gy(value):
        return lax.all_to_all(value, "gy", 0, 0)

    def halves(sums):
        (mine,) = run(sum_kernel, [sums.shape[1:]], sums)
        return mine, lax.ppermute(mine, "gy", [(i, i ^ 1) for i in range(n_gy)])

    group = (n_gx, c_dev, LANES)
    aux = -(-(2 * LANES + 7 * nz) // LANES) * LANES
    (pay,) = run(kernel(first_kernel, tab["k_parts"], tab["m_parts"], width), [(n_gx, c_dev, width + aux)],
                 idx, b, k, m, coarse_factor, scratch=[(8, aux)], limit=56)
    xl = swap_gx(pay)

    outs = [(n_gy, 1, width // 2), (52, 8, nz), (52, 1, nz), (52, 2, nz), (8, ez), (8, ez),
            (n_gx, c_dev, width + LANES), (1, LANES)]
    pay, bx, hi, lo, ks, ms, members, rc = run(kernel(coarse_in_kernel, width), outs, idx, xl, eye, free=(0,))
    y_low, y_high = shift(hi, "gy", 1), shift(lo, "gy", -1)
    sums = swap_gy(pay)

    sides = [(8, 2, nz), (8, 2, nz)]
    y, hi, lo = run(schwarz_b_kernel, [(36, 16, nz), (36, 2, nz), (36, 2, nz)], bx, y_low, y_high, ks, ms, *solve_tab,
                    scratch=[(52, 16, nz), (832, 10 * ez), (576, 10 * ez)])
    y_low, y_high = shift(hi, "gy", 1), shift(lo, "gy", -1)
    cube = (8, 8, nz)
    wide_u, u, au, h = run(apply_u_kernel, [(36, 8, nz), cube, cube, (8, LANES)], idx, b, y, y_low, y_high, k, m, inner, zct, *apply_tab,
                          free=(1, 2))

    mine, other = halves(sums)
    (pay,) = run(kernel(coarse_out_kernel, width), [group], idx, mine, other, members, eye, h)
    got = swap_gx(pay)
    pay, x0 = run(kernel(coarse_mid_kernel, width), [(n_gy, 1, width // 2 + LANES), (1, LANES)], got, members, rc, eye, free=(0,))
    sums = swap_gy(pay)

    p, qx, hi, lo = run(apply_p_kernel, [cube, (24, 8, nz), (24, 2, nz), (24, 2, nz)], idx, wide_u, x0, ks, ms, inner, zl, *apply_tab,
                        scratch=[(36, 8, nz)] + [(288, 8 * ez)] * 3)
    y_low, y_high = shift(hi, "gy", 1), shift(lo, "gy", -1)
    q, y, hi, lo = run(schwarz_q_kernel, [cube, (8, 16, nz)] + sides, qx, y_low, y_high, ks, ms, *solve_tab,
                       scratch=[(24, 16, nz), (384, 10 * ez), (128, 10 * ez)])
    y_low, y_high = shift(hi, "gy", 1), shift(lo, "gy", -1)
    s, a_s, hi = run(apply_s_kernel, [cube, cube, (1, 8, nz)], y, y_low, y_high, k, m, *apply_tab)
    side = shift(hi, "gx", 1)

    mine, other = halves(sums)
    pay, scal, resid = run(kernel(pair_kernel, width), [group, (1, LANES), cube], idx, mine, other, members, eye, b, q, u, au, s, a_s, inner, zct)
    got = swap_gx(pay)
    pay, x1 = run(kernel(last_in_kernel, width), [(n_gy, 1, LANES), (1, LANES)], got, members, x0, scal, eye, free=(0,))
    sums = swap_gy(pay)

    w, v, hi = run(apply_w_kernel, [cube, cube, (7, 1, nz)], idx, s, x1, side, k, m, ks, inner, zl, tab["face"], *apply_tab)
    y_low = shift(hi, "gy", 1)
    sol, res = run(final_kernel, [(7, 7, nz), (7, 7, nz)], sums, scal, p, w, resid, q, v, y_low, free=(0, 1))
    return sol, res


def solution(mesh):
    placed = (P("gx", "gy", None), P("gx", "gy", None), P("gx", "gy", None), P(("gx", "gy"), None))

    return jax.shard_map(
        local,
        mesh=mesh,
        in_specs=placed,
        out_specs=(P("gx", "gy", None), P("gx", "gy", None)),
        check_vma=False,
    )
```

```python
import math

import jax
import jax.numpy as jnp
import numpy as np
from jax import lax
from jax.experimental import pallas as pl
from jax.experimental.pallas import tpu as pltpu
from jax.sharding import PartitionSpec as P


HI = lax.Precision.HIGHEST
LANES = 128


def legendre_pair(position, degree):
    p_prev = 1.0
    p_now = position
    for order in range(2, degree + 1):
        p_next = ((2 * order - 1) * position * p_now - (order - 1) * p_prev) / order
        p_prev = p_now
        p_now = p_next
    return (p_now, p_prev)


def jacobi_eigen(matrix):
    size_n = matrix.shape[0]
    current = np.array(matrix)
    vectors = np.eye(size_n)
    for _ in range(20):
        for row_p in range(size_n - 1):
            for row_q in range(row_p + 1, size_n):
                off_value = current[row_p, row_q]
                if abs(off_value) > 1e-300:
                    theta = (current[row_q, row_q] - current[row_p, row_p]) / (2.0 * off_value)
                    sign_t = 1.0 if theta >= 0.0 else -1.0
                    tangent = sign_t / (abs(theta) + math.sqrt(theta * theta + 1.0))
                    cosine = 1.0 / math.sqrt(tangent * tangent + 1.0)
                    sine = tangent * cosine
                    rotation = np.eye(size_n)
                    rotation[row_p, row_p] = cosine
                    rotation[row_q, row_q] = cosine
                    rotation[row_p, row_q] = sine
                    rotation[row_q, row_p] = -sine
                    current = rotation.T @ current @ rotation
                    vectors = vectors @ rotation
    return (np.array([current[idx, idx] for idx in range(size_n)]), vectors)


def gll_tables():
    degree = 7
    guesses = [
        -0.8717401485096066,
        -0.5917001814331423,
        -0.2092992179024789,
        0.2092992179024789,
        0.5917001814331423,
        0.8717401485096066,
    ]
    interior = []
    for guess in guesses:
        position = guess
        for _ in range(30):
            p_now, p_prev = legendre_pair(position, degree)
            first = degree * (position * p_now - p_prev) / (position * position - 1.0)
            second = (2.0 * position * first - degree * (degree + 1) * p_now) / (
                1.0 - position * position
            )
            position = position - first / second
        interior.append(position)
    points = np.array([-1.0] + interior + [1.0])
    values = np.array([legendre_pair(float(pt), degree)[0] for pt in points])
    weights = 2.0 / (degree * (degree + 1) * values**2)
    deriv_mat = np.zeros((8, 8))
    for left_idx in range(8):
        for right_idx in range(8):
            if left_idx != right_idx:
                deriv_mat[left_idx, right_idx] = values[left_idx] / (
                    values[right_idx] * (points[left_idx] - points[right_idx])
                )
    deriv_mat[0, 0] = -degree * (degree + 1) / 4.0
    deriv_mat[7, 7] = degree * (degree + 1) / 4.0
    stiffness = deriv_mat.T @ (weights[:, None] * deriv_mat)
    ext_stiff = np.zeros((10, 10))
    ext_stiff[1:9, 1:9] += stiffness
    ext_stiff[0:2, 0:2] += stiffness[6:8, 6:8]
    ext_stiff[8:10, 8:10] += stiffness[0:2, 0:2]
    ext_mass = np.zeros(10)
    ext_mass[1:9] += weights
    ext_mass[0:2] += weights[6:8]
    ext_mass[8:10] += weights[0:2]
    inv_root = 1.0 / np.sqrt(ext_mass)
    eigen_vals, eigen_vecs = jacobi_eigen(inv_root[:, None] * ext_stiff * inv_root[None, :])
    eigen_basis = inv_root[:, None] * eigen_vecs
    return (stiffness, weights, eigen_basis, eigen_vals)


def dot(left, right):
    return jnp.dot(left, right, precision=HI, preferred_element_type=jnp.float32)


def make_tables(ez, c_dev):
    stiffness, weights, basis, vals = gll_tables()
    stiffness = stiffness.astype(np.float32).astype(np.float64)
    weights = weights.astype(np.float32).astype(np.float64)
    basis = basis.astype(np.float32).astype(np.float64)
    vals = vals.astype(np.float32).astype(np.float64)
    nz = 7 * ez
    span = nz // c_dev
    f32 = lambda table: np.asarray(table, np.float32)

    qq = np.zeros((10, 16, 10, 16))
    qq[:, :10, :, :10] = np.einsum("ia,jb->ijab", basis, basis)
    qq = qq.reshape(160, 160)
    lam_ab = np.ones((10, 16))
    lam_ab[:, :10] = vals[:, None] + vals[None, :]
    lam_c = np.repeat(vals, ez)[None]
    zf = np.zeros((nz, 10, ez))
    g8 = np.zeros((nz, 8, ez))
    zk = np.zeros((nz, 8, ez))
    for elem in range(ez):
        for k in range(10):
            zf[(7 * elem - 1 + k) % nz, :, elem] += basis[k]
        for k in range(8):
            g8[(7 * elem + k) % nz, k, elem] += 1.0
            zk[(7 * elem + k) % nz, :, elem] += stiffness[:, k]
    zf, g8, zk = zf.reshape(nz, -1), g8.reshape(nz, -1), zk.reshape(nz, -1)
    diag = np.diag(weights)
    kk = np.einsum("ai,bj->abij", stiffness, diag) + np.einsum("ai,bj->abij", diag, stiffness)
    kk = kk.reshape(64, 64)
    ww = np.outer(weights, weights).reshape(64, 1)
    inner = np.zeros((8, 8))
    inner[1:7, 1:7] = 1.0
    plate = inner.reshape(64, 1)
    first = np.array([1.0] * 7 + [0.0])
    last = 1.0 - first
    face = np.zeros((8, 1))
    face[1:7, 0] = weights[1:7] * np.sum(stiffness[7, 1:7])
    k_parts = {}
    m_parts = {}
    for name, left, right in (("11", first, first), ("12", first, last), ("22", last, last)):
        wz = float(np.sum(left * weights * right))
        kz = float(left @ stiffness @ right)
        k_parts[name] = float((plate.T @ kk @ plate).item()) * wz + float(np.sum(plate * ww)) * kz
        m_parts[name] = float(np.sum(plate * ww)) * wz
    wide = LANES // c_dev
    zc = (np.arange(nz)[:, None] // span == np.arange(c_dev)[None, :]).astype(np.float64)
    return dict(
        qq=f32(qq), qqt=f32(qq.T), zf=f32(zf), zft=f32(zf.T), lam_ab=f32(lam_ab.reshape(160, 1)), lam_c=f32(lam_c),
        rep10=f32(np.tile(np.eye(ez), (1, 10))), rep8=f32(np.tile(np.eye(ez), (1, 8))),
        g8=f32(g8), g8t=f32(g8.T), zk=f32(zk), kk=f32(kk), ww=f32(ww), wz=f32(np.repeat(weights, ez)[None]),
        inner=f32(plate), face=f32(face),
        zct=f32(np.tile(zc, (1, wide))), eye=f32(np.eye(LANES)),
        zl=f32(np.tile(zc.T, (wide, 1))),
        k_parts=k_parts, m_parts=m_parts,
    )


def run(kernel, outs, *args, scratch=(), free=(), limit=16):
    spaces = [pltpu.SMEM if a.dtype == jnp.int32 else pltpu.VMEM for a in args]
    size = sum(math.prod(s) for s in outs) + sum(math.prod(a.shape) for a in args)
    return pl.pallas_call(
        kernel,
        out_shape=[(jax.ShapeDtypeStruct if i in free else pltpu.VMEM)(shape, jnp.float32) for i, shape in enumerate(outs)],
        in_specs=[pl.BlockSpec(memory_space=space) for space in spaces],
        out_specs=[pl.BlockSpec(memory_space=pltpu.VMEM)] * len(outs),
        scratch_shapes=[pltpu.VMEM(shape, jnp.float32) for shape in scratch],
        compiler_params=pltpu.CompilerParams(vmem_limit_bytes=limit << 20),
        cost_estimate=pl.CostEstimate(flops=2 * 6 * 160 * 240 * 168, bytes_accessed=4 * size, transcendentals=0),
    )(*args)


def total(value):
    return jnp.sum(jnp.sum(value, axis=1, keepdims=True), axis=0, keepdims=True)


def total_row(row):
    return jnp.sum(row, axis=1, keepdims=True)


def as_col(row, eye):
    return jnp.sum(eye * row, axis=1, keepdims=True)


def as_row(col, eye):
    return jnp.sum(eye * col, axis=0, keepdims=True)


def lane_put(values):
    lane = lax.broadcasted_iota(jnp.int32, (1, LANES), 1)
    row = jnp.zeros((1, LANES), jnp.float32)
    for spot, value in enumerate(values):
        row = jnp.where(lane == spot, value, row)
    return row


def lane_get(row, spot):
    lane = lax.broadcasted_iota(jnp.int32, row.shape, 1)
    return jnp.sum(jnp.where(lane == spot, row, 0.0), axis=1, keepdims=True)


def lane_sel(spot):
    lane = lax.broadcasted_iota(jnp.int32, (1, LANES), 1)
    return jnp.where(lane // 8 == spot, 1.0, 0.0).astype(jnp.float32)


def span_mask(shape, axis, size, move):
    row = lax.broadcasted_iota(jnp.int32, shape, axis) & 7
    start = row * size + move
    fine = lax.broadcasted_iota(jnp.int32, shape, 1 - axis)
    return jnp.where((fine >= start) & (fine < start + size), 1.0, 0.0).astype(jnp.float32)


def rows_tile(rows):
    spot = lax.broadcasted_iota(jnp.int32, (8, LANES), 0)
    tile = jnp.zeros((8, LANES), jnp.float32)
    for place, row in enumerate(rows):
        tile = jnp.where(spot == place, row, tile)
    return tile


def first_kernel(k_parts, m_parts, width, idx_ref, b_ref, k_ref, m_ref, x_ref, out_ref, scr):
    k, m = k_ref[...], m_ref[...]
    e11, e12, e22 = (k * k_parts[name] + m * m_parts[name] for name in ("11", "12", "22"))
    nz, ez = b_ref.shape[2], k.shape[1]
    per, span = ez // 8, nz // 8
    sel = lane_sel(idx_ref[0])
    owner = span_mask((8, ez), 0, per, 0)
    after = span_mask((8, ez), 0, per, -1) + span_mask((8, ez), 0, per, ez - 1)
    owner_t = span_mask((ez, LANES), 1, per, 0)
    after_t = span_mask((ez, LANES), 1, per, -1) + span_mask((ez, LANES), 1, per, ez - 1)
    small = (dot(owner * e11 + after * e12, owner_t) + dot(owner * e12 + after * e22, after_t)) * sel
    acc = b_ref[1]
    for x in range(2, 7):
        acc = acc + b_ref[x]
    line = jnp.sum(acc[1:7], axis=0, keepdims=True)
    rc = dot(line, span_mask((nz, LANES), 1, span, 0)) * sel
    scr[...] = jnp.zeros_like(scr)
    scr[:, :LANES] = small
    scr[7:8, LANES : 2 * LANES] = rc
    scr[7:8, 2 * LANES : 2 * LANES + ez] = k
    scr[7:8, 3 * LANES : 3 * LANES + ez] = m
    for x in range(7):
        scr[:7, LANES + nz * x : LANES + nz * (x + 1)] = b_ref[x]
    for peer in range(out_ref.shape[0]):
        out_ref[peer, :, :width] = x_ref[:, peer * width : (peer + 1) * width]
        out_ref[peer, :, width:] = scr[...]


def split_group(group_ref, width):
    rows = group_ref.shape[0] * group_ref.shape[1]
    return group_ref[:, :, :width].reshape(rows, width), group_ref[:, :, width : width + LANES].reshape(rows, LANES)


def spread(out_ref, row):
    out_ref[...] = jnp.broadcast_to(row[None], out_ref.shape)


def coarse_in_kernel(width, idx_ref, xl_ref, eye_ref, out_ref, bx_ref, hi_ref, lo_ref, k_ref, m_ref, group_ref, rc_ref):
    factor, _ = split_group(xl_ref, width)
    base = width + LANES
    rc = jnp.sum(xl_ref[:, 7:8, base : base + LANES], axis=0)
    rc_ref[...] = rc
    group_ref[...] = xl_ref[:, :, : width + LANES]
    rows = factor.shape[0]
    rc_col = as_col(rc, eye_ref[:rows])
    part = jnp.sum(rc_col * factor, axis=0, keepdims=True)
    half = width // 2
    core = lax.broadcasted_iota(jnp.int32, out_ref.shape, 0) & 1
    out_ref[...] = jnp.where(core == 0, part[:, :half][None], part[:, half:][None])
    count = xl_ref.shape[0]
    nz, ez = bx_ref.shape[2], k_ref.shape[1]
    place = 0
    for apart in range(-4, 5):
        slot = lax.rem(idx_ref[0] + (apart + 2 * count), count)
        for x in (6,) if apart == -4 else (0, 1) if apart == 4 else range(7):
            bx_ref[place] = xl_ref[slot, :, base + nz * x : base + nz * (x + 1)]
            place += 1
        if -4 < apart < 4:
            k_ref[apart + 3 : apart + 4] = xl_ref[slot, 7:8, base + LANES : base + LANES + ez]
            m_ref[apart + 3 : apart + 4] = xl_ref[slot, 7:8, base + 2 * LANES : base + 2 * LANES + ez]
    k_ref[7:8] = k_ref[6:7]
    m_ref[7:8] = m_ref[6:7]
    hi_ref[...] = bx_ref[:, 6:7]
    lo_ref[...] = bx_ref[:, 0:2]


def join_halves(width, idx_ref, mine_ref, other_ref):
    half = width // 2
    mine, other = mine_ref[:, :half], other_ref[:, :half]
    even = idx_ref[2] == 0
    return jnp.concatenate([jnp.where(even, mine, other), jnp.where(even, other, mine)], axis=1)


def coarse_out_kernel(width, idx_ref, mine_ref, other_ref, xl_ref, eye_ref, h_ref, out_ref):
    factor, _ = split_group(xl_ref, width)
    rows = factor.shape[0]
    part = jnp.sum(factor * join_halves(width, idx_ref, mine_ref, other_ref), axis=1, keepdims=True)
    x_part = as_row(part, eye_ref[:rows])
    spread(out_ref, jnp.concatenate([x_part, h_ref[1:2], h_ref[2:3]], axis=1))


def coarse_mid_kernel(width, got_ref, xl_ref, rc_ref, eye_ref, out_ref, x_ref):
    factor, small = split_group(xl_ref, width)
    rc = rc_ref[...]
    rows = factor.shape[0]
    eye = eye_ref[:rows]
    got = jnp.sum(got_ref[...], axis=0)
    x0, h, scal = got[:, :LANES], got[:, LANES : 2 * LANES], got[:, 2 * LANES :]
    rc1_col = jnp.sum(small * x0 + eye * h, axis=1, keepdims=True)
    rc1 = as_row(rc1_col, eye)
    part = jnp.sum(rc1_col * factor, axis=0, keepdims=True)
    rho = lane_get(scal, 0) + total_row(rc * x0)
    den = lane_get(scal, 1) + total_row(x0 * (h + rc1))
    scal = lane_put([rho, den])
    half = width // 2
    core = lax.broadcasted_iota(jnp.int32, out_ref.shape, 0) & 1
    first = jnp.concatenate([part[:, :half], scal], axis=1)
    second = jnp.concatenate([part[:, half:], scal], axis=1)
    out_ref[...] = jnp.where(core == 0, first[None], second[None])
    x_ref[...] = x0


def sum_kernel(sums_ref, out_ref):
    out_ref[...] = jnp.sum(sums_ref[...], axis=0)


def pair_kernel(width, idx_ref, mine_ref, other_ref, xl_ref, eye_ref, b_ref, q_ref, u_ref, au_ref, s_ref, as_ref, inner_ref, zct_ref,
                out_ref, scal_ref, r_ref):
    factor, _ = split_group(xl_ref, width)
    rows = factor.shape[0]
    part = jnp.sum(factor * join_halves(width, idx_ref, mine_ref, other_ref), axis=1, keepdims=True)
    x_part = as_row(part, eye_ref[:rows])
    scal = mine_ref[:, width // 2 :]
    rho, den = lane_get(scal, 0), lane_get(scal, 1)
    step = rho / den
    sel = lane_sel(idx_ref[0])
    r_ref[...] = jnp.zeros_like(r_ref)
    for x in range(7):
        r_ref[x, :7] = b_ref[x] - step * q_ref[x, :7]
    nz = b_ref.shape[2]
    flat = lambda ref: ref[...].reshape(64, nz)
    resid = flat(r_ref)
    t = flat(u_ref) - step * flat(s_ref)
    at = flat(au_ref) - step * flat(as_ref)
    inner = inner_ref[...]
    wr = dot(jnp.sum(inner * resid, axis=0, keepdims=True), zct_ref[...]) * sel
    wt = dot(jnp.sum(inner * at, axis=0, keepdims=True), zct_ref[...]) * sel
    spread(out_ref, jnp.concatenate([x_part, wr, wt, lane_put([total(resid * t), total(t * at)])], axis=1))
    scal_ref[...] = lane_put([rho, den])


def last_in_kernel(width, got_ref, xl_ref, x0_ref, scal_ref, eye_ref, out_ref, x_ref):
    _, small = split_group(xl_ref, width)
    eye = eye_ref[: small.shape[0]]
    got = jnp.sum(got_ref[...], axis=0)
    x1, wr, wt, scal = (got[:, LANES * row : LANES * (row + 1)] for row in range(4))
    step = lane_get(scal_ref[...], 0) / lane_get(scal_ref[...], 1)
    c = x0_ref[...] - step * x1
    tc = as_row(jnp.sum(small * c, axis=1, keepdims=True), eye)
    rho1 = lane_get(scal, 0) + total_row(wr * c)
    en1 = lane_get(scal, 1) + total_row(c * (2.0 * wt + tc))
    spread(out_ref, lane_put([rho1, en1]))
    x_ref[...] = x1


def final_kernel(sums_ref, scal_ref, p_ref, w_ref, r_ref, qo_ref, v_ref, vl_ref, sol_ref, res_ref):
    got = jnp.sum(sums_ref[...], axis=0)
    rho1, en1 = lane_get(got, 0), lane_get(got, 1)
    rho, den = lane_get(scal_ref[...], 0), lane_get(scal_ref[...], 1)
    step = rho / den
    beta = rho1 / rho
    step1 = rho1 / (en1 - beta * rho1 / step)
    p_mult = step + step1 * (1.0 + beta)
    w_mult = step1 * step
    q_mult = step1 * (1.0 + beta)
    for x in range(7):
        sol_ref[x] = p_mult * p_ref[x, :7] - w_mult * w_ref[x, :7]
        top = w_mult * vl_ref[x]
        res_ref[x] = r_ref[x, :7] - q_mult * qo_ref[x, :7] + w_mult * v_ref[x, :7]
        res_ref[x, 0:1] = res_ref[x, 0:1] + top


SOLVE = ("rep10", "lam_ab", "lam_c", "qq", "qqt", "zf", "zft")
APPLY = ("rep8", "wz", "g8", "g8t", "zk", "kk", "ww")


def apply(block, k, m, rep8, wz, g8, g8t, zk, kk, ww):
    k_line, m_line = dot(k, rep8), dot(m, rep8) * wz
    spread_u = dot(block, g8)
    out = (k_line * wz) * dot(kk, spread_u) + ww * (k_line * dot(block, zk) + m_line * spread_u)
    return dot(out, g8t)


def solve_columns(block, k_ref, m_ref, first, count, consts, lines, acc):
    rep10, lam_ab, lam_c, qq, qqt, zf, zft = consts
    lines[...] = dot(block, zf[...])
    acc[...] = jnp.zeros_like(acc)
    lam = lam_ab[...] + lam_c[...]
    for c in range(count):
        k, m = k_ref[first + c : first + c + 1], m_ref[first + c : first + c + 1]
        den = dot(k, rep10[...]) * lam + dot(m, rep10[...])
        spectral = dot(qqt[...], lines[112 * c : 112 * c + 160]) / den
        low = max(128 - 112 * c, 0)
        high = min(112 * (count - 1) + 32 - 112 * c, 160)
        start = 112 * c + low - 128
        acc[start : start + high - low] = acc[start : start + high - low] + dot(qq[low:high], spectral)
    return dot(acc[...], zft[...])


def schwarz_b_kernel(bx_ref, yl_ref, yh_ref, k_ref, m_ref, *refs):
    consts, (out_ref, hi_ref, lo_ref, scr, lines, acc) = refs[:-6], refs[-6:]
    nz = bx_ref.shape[2]
    scr[...] = jnp.zeros_like(scr)
    scr[:, 1:8] = bx_ref[:, 0:7]
    scr[:, 0:1] = yl_ref[...]
    scr[:, 8:10] = yh_ref[...]
    out = solve_columns(scr[...].reshape(52 * 16, nz), k_ref, m_ref, 0, 7, consts, lines, acc)
    out_ref[...] = out.reshape(36, 16, nz)
    hi_ref[...] = out_ref[:, 8:10]
    lo_ref[...] = out_ref[:, 0:2]


def schwarz_q_kernel(qx_ref, yl_ref, yh_ref, k_ref, m_ref, *refs):
    consts, (q_ref, out_ref, hi_ref, lo_ref, scr, lines, acc) = refs[:-7], refs[-7:]
    nz = qx_ref.shape[2]
    scr[...] = jnp.zeros_like(scr)
    scr[:, 1:9] = qx_ref[...]
    scr[:, 0:1] = yl_ref[:, 0:1]
    scr[:, 1:2] = scr[:, 1:2] + yl_ref[:, 1:2]
    scr[:, 8:9] = scr[:, 8:9] + yh_ref[:, 0:1]
    scr[:, 9:10] = yh_ref[:, 1:2]
    q_ref[...] = scr[8:16, 1:9]
    out = solve_columns(scr[...].reshape(24 * 16, nz), k_ref, m_ref, 2, 3, consts, lines, acc)
    out_ref[...] = out.reshape(8, 16, nz)
    hi_ref[...] = out_ref[:, 8:10]
    lo_ref[...] = out_ref[:, 0:2]


def gather_s(u_ref, y_ref, yl_ref, yh_ref):
    u_ref[...] = y_ref[:, 1:9]
    u_ref[:, 0:2] = u_ref[:, 0:2] + yl_ref[...]
    u_ref[:, 6:8] = u_ref[:, 6:8] + yh_ref[...]


def apply_u_kernel(idx_ref, b_ref, y_ref, yl_ref, yh_ref, k_ref, m_ref, inner_ref, zct_ref, *refs):
    consts, (u_ref, own_ref, au_ref, h_ref) = refs[:-4], refs[-4:]
    nz = u_ref.shape[2]
    gather_s(u_ref, y_ref, yl_ref, yh_ref)
    own_ref[...] = u_ref[14:22]
    u = own_ref[...].reshape(64, nz)
    au = apply(u, k_ref[...], m_ref[...], *(ref[...] for ref in consts))
    au_ref[...] = au.reshape(8, 8, nz)
    h = dot(jnp.sum(inner_ref[...] * au, axis=0, keepdims=True), zct_ref[...]) * lane_sel(idx_ref[0])
    acc = b_ref[0] * own_ref[0, :7]
    for x in range(1, 7):
        acc = acc + b_ref[x] * own_ref[x, :7]
    h_ref[...] = rows_tile([jnp.zeros((1, LANES), jnp.float32), h, lane_put([total(acc), total(u * au)])])


def apply_s_kernel(y_ref, yl_ref, yh_ref, k_ref, m_ref, *refs):
    consts, (s_ref, as_ref, hi_ref) = refs[:-3], refs[-3:]
    nz = s_ref.shape[2]
    gather_s(s_ref, y_ref, yl_ref, yh_ref)
    out = apply(s_ref[...].reshape(64, nz), k_ref[...], m_ref[...], *(ref[...] for ref in consts))
    as_ref[...] = out.reshape(8, 8, nz)
    hi_ref[...] = as_ref[7:8]


def apply_p_kernel(idx_ref, u_ref, x_ref, k_ref, m_ref, inner_ref, zl_ref, *refs):
    (rep8, wz, g8, g8t, zk, kk, ww), (p_ref, q_ref, hi_ref, lo_ref, field, su, sk, acc) = refs[:-8], refs[-8:]
    nz = u_ref.shape[2]
    count = idx_ref[1]
    x0 = x_ref[...]
    picks = [x0 * lane_sel(lax.rem(idx_ref[0] + (apart + 2 * count), count)) for apart in range(-2, 3)]
    lines = dot(rows_tile(picks), zl_ref[...])
    field[...] = u_ref[...]
    side = inner_ref[8:16]
    for c in range(5):
        add = side * lines[c : c + 1]
        for x in range(7 * c + 1, 7 * c + 7):
            field[x] = field[x] + add
    p_ref[...] = field[14:22]
    whole = field[...].reshape(36 * 8, nz)
    su[...] = dot(whole, g8[...])
    sk[...] = dot(whole, zk[...])
    acc[...] = jnp.zeros_like(acc)
    for c in range(5):
        k_line = dot(k_ref[c + 1 : c + 2], rep8[...])
        m_line = dot(m_ref[c + 1 : c + 2], rep8[...]) * wz[...]
        part = slice(56 * c, 56 * c + 64)
        u = su[part]
        out = (k_line * wz[...]) * dot(kk[...], u) + ww[...] * (k_line * sk[part] + m_line * u)
        acc[part] = acc[part] + out
    q_ref[...] = dot(acc[48:240], g8t[...]).reshape(24, 8, nz)
    hi_ref[...] = q_ref[:, 6:8]
    lo_ref[...] = q_ref[:, 0:2]


def apply_w_kernel(idx_ref, s_ref, x_ref, side_ref, k_ref, m_ref, ks_ref, inner_ref, zl_ref, face_ref, *refs):
    consts, (w_ref, v_ref, hi_ref) = refs[:-3], refs[-3:]
    rep8, wz, g8, g8t = consts[:4]
    nz = s_ref.shape[2]
    x1 = x_ref[...]
    left = lax.rem(idx_ref[0] + idx_ref[1] - 1, idx_ref[1])
    lines = dot(rows_tile([x1 * lane_sel(idx_ref[0]), x1 * lane_sel(left)]), zl_ref[...])
    w = s_ref[...].reshape(64, nz) + inner_ref[...] * lines[0:1]
    w_ref[...] = w.reshape(8, 8, nz)
    out = apply(w, k_ref[...], m_ref[...], *(ref[...] for ref in consts)).reshape(8, 8, nz)
    v_ref[...] = out
    scale = dot(ks_ref[2:3], rep8[...]) * wz[...]
    share = dot(scale * dot(lines, g8[...]), g8t[...])[1:2]
    v_ref[0] = v_ref[0] + side_ref[0] + face_ref[...] * share
    hi_ref[...] = v_ref[0:7, 7:8]


def shift(value, axis, step):
    count = lax.axis_size(axis)
    return lax.ppermute(value, axis, [(i, (i + step) % count) for i in range(count)])


def local(right_side, stiff_coef, mass_coef, coarse_factor):
    nz = right_side.shape[2]
    c_dev, n_coarse = coarse_factor.shape
    ez = stiff_coef.shape[2]
    n_gx, n_gy = lax.axis_size("gx"), lax.axis_size("gy")
    width = n_coarse // n_gx
    tab = {name: jnp.asarray(value) if isinstance(value, np.ndarray) else value for name, value in make_tables(ez, c_dev).items()}
    k = stiff_coef.reshape(1, ez)
    m = mass_coef.reshape(1, ez)
    b = right_side
    idx = jnp.stack([lax.axis_index("gx"), jnp.int32(n_gx), lax.axis_index("gy") & 1])
    solve_tab = [tab[name] for name in SOLVE]
    apply_tab = [tab[name] for name in APPLY]
    inner, zct, zl, eye = (tab[name] for name in ("inner", "zct", "zl", "eye"))

    def kernel(fn, *fixed):
        def call(*refs):
            return fn(*fixed, *refs)

        call.__name__ = fn.__name__
        return call

    def swap_gx(value):
        return lax.all_to_all(value, "gx", 0, 0)

    def swap_gy(value):
        return lax.all_to_all(value, "gy", 0, 0)

    def halves(sums):
        (mine,) = run(sum_kernel, [sums.shape[1:]], sums)
        return mine, lax.ppermute(mine, "gy", [(i, i ^ 1) for i in range(n_gy)])

    aux = -(-(LANES + 7 * nz) // LANES) * LANES
    (pay,) = run(kernel(first_kernel, tab["k_parts"], tab["m_parts"], width), [(n_gx, c_dev, width + aux)],
                 idx, b, k, m, coarse_factor, scratch=[(8, aux)], limit=56)
    xl = swap_gx(pay)

    outs = [(n_gy, 1, width // 2), (52, 8, nz), (52, 1, nz), (52, 2, nz), (8, ez), (8, ez),
            (n_gx, c_dev, width + LANES), (1, LANES)]
    pay, bx, hi, lo, ks, ms, members, rc = run(kernel(coarse_in_kernel, width), outs, idx, xl, eye, free=(0,))
    y_low, y_high = shift(hi, "gy", 1), shift(lo, "gy", -1)
    sums = swap_gy(pay)

    sides = [(8, 2, nz), (8, 2, nz)]
    y, hi, lo = run(schwarz_b_kernel, [(36, 16, nz), (36, 2, nz), (36, 2, nz)], bx, y_low, y_high, ks, ms, *solve_tab,
                    scratch=[(52, 16, nz), (832, 10 * ez), (576, 10 * ez)])
    y_low, y_high = shift(hi, "gy", 1), shift(lo, "gy", -1)
    cube = (8, 8, nz)
    wide_u, u, au, h = run(apply_u_kernel, [(36, 8, nz), cube, cube, (8, LANES)], idx, b, y, y_low, y_high, k, m, inner, zct, *apply_tab,
                          free=(1, 2))

    mine, other = halves(sums)
    (pay,) = run(kernel(coarse_out_kernel, width), [(n_gx, 1, 3 * LANES)], idx, mine, other, members, eye, h)
    got = swap_gx(pay)
    pay, x0 = run(kernel(coarse_mid_kernel, width), [(n_gy, 1, width // 2 + LANES), (1, LANES)], got, members, rc, eye, free=(0,))
    sums = swap_gy(pay)

    p, qx, hi, lo = run(apply_p_kernel, [cube, (24, 8, nz), (24, 2, nz), (24, 2, nz)], idx, wide_u, x0, ks, ms, inner, zl, *apply_tab,
                        scratch=[(36, 8, nz)] + [(288, 8 * ez)] * 3)
    y_low, y_high = shift(hi, "gy", 1), shift(lo, "gy", -1)
    q, y, hi, lo = run(schwarz_q_kernel, [cube, (8, 16, nz)] + sides, qx, y_low, y_high, ks, ms, *solve_tab,
                       scratch=[(24, 16, nz), (384, 10 * ez), (128, 10 * ez)])
    y_low, y_high = shift(hi, "gy", 1), shift(lo, "gy", -1)
    s, a_s, hi = run(apply_s_kernel, [cube, cube, (1, 8, nz)], y, y_low, y_high, k, m, *apply_tab)
    side = shift(hi, "gx", 1)

    mine, other = halves(sums)
    pay, scal, resid = run(kernel(pair_kernel, width), [(n_gx, 1, 4 * LANES), (1, LANES), cube], idx, mine, other, members, eye, b, q, u, au, s, a_s, inner, zct)
    got = swap_gx(pay)
    pay, x1 = run(kernel(last_in_kernel, width), [(n_gy, 1, LANES), (1, LANES)], got, members, x0, scal, eye, free=(0,))
    sums = swap_gy(pay)

    w, v, hi = run(apply_w_kernel, [cube, cube, (7, 1, nz)], idx, s, x1, side, k, m, ks, inner, zl, tab["face"], *apply_tab)
    y_low = shift(hi, "gy", 1)
    sol, res = run(final_kernel, [(7, 7, nz), (7, 7, nz)], sums, scal, p, w, resid, q, v, y_low, free=(0, 1))
    return sol, res


def solution(mesh):
    placed = (P("gx", "gy", None), P("gx", "gy", None), P("gx", "gy", None), P(("gx", "gy"), None))

    return jax.shard_map(
        local,
        mesh=mesh,
        in_specs=placed,
        out_specs=(P("gx", "gy", None), P("gx", "gy", None)),
        check_vma=False,
    )
```

```python
import math

import jax
import jax.numpy as jnp
import numpy as np
from jax import lax
from jax.experimental import pallas as pl
from jax.experimental.pallas import tpu as pltpu
from jax.sharding import PartitionSpec as P


HI = lax.Precision.HIGHEST
LANES = 128


def legendre_pair(position, degree):
    p_prev = 1.0
    p_now = position
    for order in range(2, degree + 1):
        p_next = ((2 * order - 1) * position * p_now - (order - 1) * p_prev) / order
        p_prev = p_now
        p_now = p_next
    return (p_now, p_prev)


def jacobi_eigen(matrix):
    size_n = matrix.shape[0]
    current = np.array(matrix)
    vectors = np.eye(size_n)
    for _ in range(20):
        for row_p in range(size_n - 1):
            for row_q in range(row_p + 1, size_n):
                off_value = current[row_p, row_q]
                if abs(off_value) > 1e-300:
                    theta = (current[row_q, row_q] - current[row_p, row_p]) / (2.0 * off_value)
                    sign_t = 1.0 if theta >= 0.0 else -1.0
                    tangent = sign_t / (abs(theta) + math.sqrt(theta * theta + 1.0))
                    cosine = 1.0 / math.sqrt(tangent * tangent + 1.0)
                    sine = tangent * cosine
                    rotation = np.eye(size_n)
                    rotation[row_p, row_p] = cosine
                    rotation[row_q, row_q] = cosine
                    rotation[row_p, row_q] = sine
                    rotation[row_q, row_p] = -sine
                    current = rotation.T @ current @ rotation
                    vectors = vectors @ rotation
    return (np.array([current[idx, idx] for idx in range(size_n)]), vectors)


def gll_tables():
    degree = 7
    guesses = [
        -0.8717401485096066,
        -0.5917001814331423,
        -0.2092992179024789,
        0.2092992179024789,
        0.5917001814331423,
        0.8717401485096066,
    ]
    interior = []
    for guess in guesses:
        position = guess
        for _ in range(30):
            p_now, p_prev = legendre_pair(position, degree)
            first = degree * (position * p_now - p_prev) / (position * position - 1.0)
            second = (2.0 * position * first - degree * (degree + 1) * p_now) / (
                1.0 - position * position
            )
            position = position - first / second
        interior.append(position)
    points = np.array([-1.0] + interior + [1.0])
    values = np.array([legendre_pair(float(pt), degree)[0] for pt in points])
    weights = 2.0 / (degree * (degree + 1) * values**2)
    deriv_mat = np.zeros((8, 8))
    for left_idx in range(8):
        for right_idx in range(8):
            if left_idx != right_idx:
                deriv_mat[left_idx, right_idx] = values[left_idx] / (
                    values[right_idx] * (points[left_idx] - points[right_idx])
                )
    deriv_mat[0, 0] = -degree * (degree + 1) / 4.0
    deriv_mat[7, 7] = degree * (degree + 1) / 4.0
    stiffness = deriv_mat.T @ (weights[:, None] * deriv_mat)
    ext_stiff = np.zeros((10, 10))
    ext_stiff[1:9, 1:9] += stiffness
    ext_stiff[0:2, 0:2] += stiffness[6:8, 6:8]
    ext_stiff[8:10, 8:10] += stiffness[0:2, 0:2]
    ext_mass = np.zeros(10)
    ext_mass[1:9] += weights
    ext_mass[0:2] += weights[6:8]
    ext_mass[8:10] += weights[0:2]
    inv_root = 1.0 / np.sqrt(ext_mass)
    eigen_vals, eigen_vecs = jacobi_eigen(inv_root[:, None] * ext_stiff * inv_root[None, :])
    eigen_basis = inv_root[:, None] * eigen_vecs
    return (stiffness, weights, eigen_basis, eigen_vals)


def dot(left, right):
    return jnp.dot(left, right, precision=HI, preferred_element_type=jnp.float32)


def make_tables(ez, c_dev):
    stiffness, weights, basis, vals = gll_tables()
    stiffness = stiffness.astype(np.float32).astype(np.float64)
    weights = weights.astype(np.float32).astype(np.float64)
    basis = basis.astype(np.float32).astype(np.float64)
    vals = vals.astype(np.float32).astype(np.float64)
    nz = 7 * ez
    span = nz // c_dev
    f32 = lambda table: np.asarray(table, np.float32)

    qq = np.zeros((10, 16, 10, 16))
    qq[:, :10, :, :10] = np.einsum("ia,jb->ijab", basis, basis)
    qq = qq.reshape(160, 160)
    lam_ab = np.ones((10, 16))
    lam_ab[:, :10] = vals[:, None] + vals[None, :]
    lam_c = np.repeat(vals, ez)[None]
    zf = np.zeros((nz, 10, ez))
    g8 = np.zeros((nz, 8, ez))
    zk = np.zeros((nz, 8, ez))
    for elem in range(ez):
        for k in range(10):
            zf[(7 * elem - 1 + k) % nz, :, elem] += basis[k]
        for k in range(8):
            g8[(7 * elem + k) % nz, k, elem] += 1.0
            zk[(7 * elem + k) % nz, :, elem] += stiffness[:, k]
    zf, g8, zk = zf.reshape(nz, -1), g8.reshape(nz, -1), zk.reshape(nz, -1)
    diag = np.diag(weights)
    kk = np.einsum("ai,bj->abij", stiffness, diag) + np.einsum("ai,bj->abij", diag, stiffness)
    kk = kk.reshape(64, 64)
    ww = np.outer(weights, weights).reshape(64, 1)
    inner = np.zeros((8, 8))
    inner[1:7, 1:7] = 1.0
    plate = inner.reshape(64, 1)
    first = np.array([1.0] * 7 + [0.0])
    last = 1.0 - first
    face = np.zeros((8, 1))
    face[1:7, 0] = weights[1:7] * np.sum(stiffness[7, 1:7])
    k_parts = {}
    m_parts = {}
    for name, left, right in (("11", first, first), ("12", first, last), ("22", last, last)):
        wz = float(np.sum(left * weights * right))
        kz = float(left @ stiffness @ right)
        k_parts[name] = float((plate.T @ kk @ plate).item()) * wz + float(np.sum(plate * ww)) * kz
        m_parts[name] = float(np.sum(plate * ww)) * wz
    wide = LANES // c_dev
    zc = (np.arange(nz)[:, None] // span == np.arange(c_dev)[None, :]).astype(np.float64)
    return dict(
        qq=f32(qq), qqt=f32(qq.T), zf=f32(zf), zft=f32(zf.T), lam_ab=f32(lam_ab.reshape(160, 1)), lam_c=f32(lam_c),
        rep10=f32(np.tile(np.eye(ez), (1, 10))), rep8=f32(np.tile(np.eye(ez), (1, 8))),
        g8=f32(g8), g8t=f32(g8.T), zk=f32(zk), kk=f32(kk), ww=f32(ww), wz=f32(np.repeat(weights, ez)[None]),
        inner=f32(plate), face=f32(face),
        zct=f32(np.tile(zc, (1, wide))), eye=f32(np.eye(LANES)),
        zl=f32(np.tile(zc.T, (wide, 1))),
        k_parts=k_parts, m_parts=m_parts,
    )


def run(kernel, outs, *args, scratch=(), free=(), limit=16):
    spaces = [pltpu.SMEM if a.dtype == jnp.int32 else pltpu.VMEM for a in args]
    size = sum(math.prod(s) for s in outs) + sum(math.prod(a.shape) for a in args)
    return pl.pallas_call(
        kernel,
        out_shape=[(jax.ShapeDtypeStruct if i in free else pltpu.VMEM)(shape, jnp.float32) for i, shape in enumerate(outs)],
        in_specs=[pl.BlockSpec(memory_space=space) for space in spaces],
        out_specs=[pl.BlockSpec(memory_space=pltpu.VMEM)] * len(outs),
        scratch_shapes=[pltpu.VMEM(shape, jnp.float32) for shape in scratch],
        compiler_params=pltpu.CompilerParams(vmem_limit_bytes=limit << 20),
        cost_estimate=pl.CostEstimate(flops=2 * 6 * 160 * 240 * 168, bytes_accessed=4 * size, transcendentals=0),
    )(*args)


def total(value):
    return jnp.sum(jnp.sum(value, axis=1, keepdims=True), axis=0, keepdims=True)


def total_row(row):
    return jnp.sum(row, axis=1, keepdims=True)


def as_col(row, eye):
    return jnp.sum(eye * row, axis=1, keepdims=True)


def as_row(col, eye):
    return jnp.sum(eye * col, axis=0, keepdims=True)


def lane_put(values):
    lane = lax.broadcasted_iota(jnp.int32, (1, LANES), 1)
    row = jnp.zeros((1, LANES), jnp.float32)
    for spot, value in enumerate(values):
        row = jnp.where(lane == spot, value, row)
    return row


def lane_get(row, spot):
    lane = lax.broadcasted_iota(jnp.int32, row.shape, 1)
    return jnp.sum(jnp.where(lane == spot, row, 0.0), axis=1, keepdims=True)


def lane_sel(spot):
    lane = lax.broadcasted_iota(jnp.int32, (1, LANES), 1)
    return jnp.where(lane // 8 == spot, 1.0, 0.0).astype(jnp.float32)


def span_mask(shape, axis, size, move):
    row = lax.broadcasted_iota(jnp.int32, shape, axis) & 7
    start = row * size + move
    fine = lax.broadcasted_iota(jnp.int32, shape, 1 - axis)
    return jnp.where((fine >= start) & (fine < start + size), 1.0, 0.0).astype(jnp.float32)


def rows_tile(rows):
    spot = lax.broadcasted_iota(jnp.int32, (8, LANES), 0)
    tile = jnp.zeros((8, LANES), jnp.float32)
    for place, row in enumerate(rows):
        tile = jnp.where(spot == place, row, tile)
    return tile


def first_kernel(k_parts, m_parts, width, idx_ref, b_ref, k_ref, m_ref, x_ref, out_ref, scr):
    k, m = k_ref[...], m_ref[...]
    e11, e12, e22 = (k * k_parts[name] + m * m_parts[name] for name in ("11", "12", "22"))
    nz, ez = b_ref.shape[2], k.shape[1]
    per, span = ez // 8, nz // 8
    sel = lane_sel(idx_ref[0])
    owner = span_mask((8, ez), 0, per, 0)
    after = span_mask((8, ez), 0, per, -1) + span_mask((8, ez), 0, per, ez - 1)
    owner_t = span_mask((ez, LANES), 1, per, 0)
    after_t = span_mask((ez, LANES), 1, per, -1) + span_mask((ez, LANES), 1, per, ez - 1)
    small = (dot(owner * e11 + after * e12, owner_t) + dot(owner * e12 + after * e22, after_t)) * sel
    acc = b_ref[1]
    for x in range(2, 7):
        acc = acc + b_ref[x]
    line = jnp.sum(acc[1:7], axis=0, keepdims=True)
    rc = dot(line, span_mask((nz, LANES), 1, span, 0)) * sel
    scr[...] = jnp.zeros_like(scr)
    scr[:, :LANES] = small
    scr[7:8, LANES : 2 * LANES] = rc
    scr[7:8, 2 * LANES : 2 * LANES + ez] = k
    scr[7:8, 3 * LANES : 3 * LANES + ez] = m
    for x in range(7):
        scr[:7, LANES + nz * x : LANES + nz * (x + 1)] = b_ref[x]
    for peer in range(out_ref.shape[0]):
        out_ref[peer, :, :width] = x_ref[:, peer * width : (peer + 1) * width]
        out_ref[peer, :, width:] = scr[...]


def split_group(group_ref, width):
    rows = group_ref.shape[0] * group_ref.shape[1]
    return group_ref[:, :, :width].reshape(rows, width), group_ref[:, :, width : width + LANES].reshape(rows, LANES)


def spread(out_ref, row):
    out_ref[...] = jnp.broadcast_to(row[None], out_ref.shape)


def coarse_in_kernel(width, idx_ref, xl_ref, eye_ref, out_ref, bx_ref, hi_ref, lo_ref, k_ref, m_ref, group_ref, rc_ref):
    factor, _ = split_group(xl_ref, width)
    base = width + LANES
    rc = jnp.sum(xl_ref[:, 7:8, base : base + LANES], axis=0)
    rc_ref[...] = rc
    group_ref[...] = xl_ref[:, :, : width + LANES]
    rows = factor.shape[0]
    rc_col = as_col(rc, eye_ref[:rows])
    part = jnp.sum(rc_col * factor, axis=0, keepdims=True)
    half = width // 2
    core = lax.broadcasted_iota(jnp.int32, out_ref.shape, 0) & 1
    out_ref[...] = jnp.where(core == 0, part[:, :half][None], part[:, half:][None])
    count = xl_ref.shape[0]
    nz, ez = bx_ref.shape[2], k_ref.shape[1]
    place = 0
    for apart in range(-4, 5):
        slot = lax.rem(idx_ref[0] + (apart + 2 * count), count)
        for x in (6,) if apart == -4 else (0, 1) if apart == 4 else range(7):
            bx_ref[place] = xl_ref[slot, :, base + nz * x : base + nz * (x + 1)]
            place += 1
        if -4 < apart < 4:
            k_ref[apart + 3 : apart + 4] = xl_ref[slot, 7:8, base + LANES : base + LANES + ez]
            m_ref[apart + 3 : apart + 4] = xl_ref[slot, 7:8, base + 2 * LANES : base + 2 * LANES + ez]
    k_ref[7:8] = k_ref[6:7]
    m_ref[7:8] = m_ref[6:7]
    hi_ref[...] = bx_ref[:, 6:7]
    lo_ref[...] = bx_ref[:, 0:2]


def join_halves(width, idx_ref, mine_ref, other_ref):
    half = width // 2
    mine, other = mine_ref[:, :half], other_ref[:, :half]
    even = idx_ref[2] == 0
    return jnp.concatenate([jnp.where(even, mine, other), jnp.where(even, other, mine)], axis=1)


def coarse_out_kernel(width, idx_ref, mine_ref, other_ref, xl_ref, eye_ref, h_ref, out_ref):
    factor, _ = split_group(xl_ref, width)
    rows = factor.shape[0]
    part = jnp.sum(factor * join_halves(width, idx_ref, mine_ref, other_ref), axis=1, keepdims=True)
    x_part = as_row(part, eye_ref[:rows])
    spread(out_ref, jnp.concatenate([x_part, h_ref[1:2], h_ref[2:3]], axis=1))


def coarse_mid_kernel(width, got_ref, xl_ref, rc_ref, eye_ref, out_ref, x_ref):
    factor, small = split_group(xl_ref, width)
    rc = rc_ref[...]
    rows = factor.shape[0]
    eye = eye_ref[:rows]
    got = jnp.sum(got_ref[...], axis=0)
    x0, h, scal = got[:, :LANES], got[:, LANES : 2 * LANES], got[:, 2 * LANES :]
    rc1_col = jnp.sum(small * x0 + eye * h, axis=1, keepdims=True)
    rc1 = as_row(rc1_col, eye)
    part = jnp.sum(rc1_col * factor, axis=0, keepdims=True)
    rho = lane_get(scal, 0) + total_row(rc * x0)
    den = lane_get(scal, 1) + total_row(x0 * (h + rc1))
    scal = lane_put([rho, den])
    half = width // 2
    core = lax.broadcasted_iota(jnp.int32, out_ref.shape, 0) & 1
    first = jnp.concatenate([part[:, :half], scal], axis=1)
    second = jnp.concatenate([part[:, half:], scal], axis=1)
    out_ref[...] = jnp.where(core == 0, first[None], second[None])
    x_ref[...] = x0


def sum_kernel(sums_ref, out_ref):
    out_ref[...] = jnp.sum(sums_ref[...], axis=0)


def pair_kernel(width, idx_ref, mine_ref, other_ref, xl_ref, eye_ref, b_ref, q_ref, u_ref, au_ref, s_ref, as_ref, inner_ref, zct_ref,
                out_ref, scal_ref, r_ref):
    factor, _ = split_group(xl_ref, width)
    rows = factor.shape[0]
    part = jnp.sum(factor * join_halves(width, idx_ref, mine_ref, other_ref), axis=1, keepdims=True)
    x_part = as_row(part, eye_ref[:rows])
    scal = mine_ref[:, width // 2 :]
    rho, den = lane_get(scal, 0), lane_get(scal, 1)
    step = rho / den
    sel = lane_sel(idx_ref[0])
    r_ref[...] = jnp.zeros_like(r_ref)
    for x in range(7):
        r_ref[x, :7] = b_ref[x] - step * q_ref[x, :7]
    nz = b_ref.shape[2]
    flat = lambda ref: ref[...].reshape(64, nz)
    resid = flat(r_ref)
    t = flat(u_ref) - step * flat(s_ref)
    at = flat(au_ref) - step * flat(as_ref)
    inner = inner_ref[...]
    wr = dot(jnp.sum(inner * resid, axis=0, keepdims=True), zct_ref[...]) * sel
    wt = dot(jnp.sum(inner * at, axis=0, keepdims=True), zct_ref[...]) * sel
    spread(out_ref, jnp.concatenate([x_part, wr, wt, lane_put([total(resid * t), total(t * at)])], axis=1))
    scal_ref[...] = lane_put([rho, den])


def last_in_kernel(width, got_ref, xl_ref, x0_ref, scal_ref, eye_ref, out_ref, x_ref):
    _, small = split_group(xl_ref, width)
    eye = eye_ref[: small.shape[0]]
    got = jnp.sum(got_ref[...], axis=0)
    x1, wr, wt, scal = (got[:, LANES * row : LANES * (row + 1)] for row in range(4))
    step = lane_get(scal_ref[...], 0) / lane_get(scal_ref[...], 1)
    c = x0_ref[...] - step * x1
    tc = as_row(jnp.sum(small * c, axis=1, keepdims=True), eye)
    rho1 = lane_get(scal, 0) + total_row(wr * c)
    en1 = lane_get(scal, 1) + total_row(c * (2.0 * wt + tc))
    spread(out_ref, lane_put([rho1, en1]))
    x_ref[...] = x1


def final_kernel(sums_ref, scal_ref, p_ref, w_ref, r_ref, qo_ref, v_ref, vl_ref, sol_ref, res_ref):
    got = jnp.sum(sums_ref[...], axis=0)
    rho1, en1 = lane_get(got, 0), lane_get(got, 1)
    rho, den = lane_get(scal_ref[...], 0), lane_get(scal_ref[...], 1)
    step = rho / den
    beta = rho1 / rho
    step1 = rho1 / (en1 - beta * rho1 / step)
    p_mult = step + step1 * (1.0 + beta)
    w_mult = step1 * step
    q_mult = step1 * (1.0 + beta)
    for x in range(7):
        sol_ref[x] = p_mult * p_ref[x, :7] - w_mult * w_ref[x, :7]
        top = w_mult * vl_ref[x]
        res_ref[x] = r_ref[x, :7] - q_mult * qo_ref[x, :7] + w_mult * v_ref[x, :7]
        res_ref[x, 0:1] = res_ref[x, 0:1] + top


SOLVE = ("rep10", "lam_ab", "lam_c", "qq", "qqt", "zf", "zft")
APPLY = ("rep8", "wz", "g8", "g8t", "zk", "kk", "ww")


def apply(block, k, m, rep8, wz, g8, g8t, zk, kk, ww):
    k_line, m_line = dot(k, rep8), dot(m, rep8) * wz
    spread_u = dot(block, g8)
    out = (k_line * wz) * dot(kk, spread_u) + ww * (k_line * dot(block, zk) + m_line * spread_u)
    return dot(out, g8t)


def solve_columns(block, k_ref, m_ref, first, count, consts, lines, acc):
    rep10, lam_ab, lam_c, qq, qqt, zf, zft = consts
    lines[...] = dot(block, zf[...])
    acc[...] = jnp.zeros_like(acc)
    lam = lam_ab[...] + lam_c[...]
    k_lines, m_lines = dot(k_ref[...], rep10[...]), dot(m_ref[...], rep10[...])
    for c in range(count):
        spot = slice(first + c, first + c + 1)
        den = k_lines[spot] * lam + m_lines[spot]
        spectral = dot(qqt[...], lines[112 * c : 112 * c + 160]) / den
        low = max(128 - 112 * c, 0)
        high = min(112 * (count - 1) + 32 - 112 * c, 160)
        start = 112 * c + low - 128
        acc[start : start + high - low] = acc[start : start + high - low] + dot(qq[low:high], spectral)
    return dot(acc[...], zft[...])


def schwarz_b_kernel(bx_ref, yl_ref, yh_ref, k_ref, m_ref, *refs):
    consts, (out_ref, hi_ref, lo_ref, scr, lines, acc) = refs[:-6], refs[-6:]
    nz = bx_ref.shape[2]
    scr[...] = jnp.zeros_like(scr)
    scr[:, 1:8] = bx_ref[:, 0:7]
    scr[:, 0:1] = yl_ref[...]
    scr[:, 8:10] = yh_ref[...]
    out = solve_columns(scr[...].reshape(52 * 16, nz), k_ref, m_ref, 0, 7, consts, lines, acc)
    out_ref[...] = out.reshape(36, 16, nz)
    hi_ref[...] = out_ref[:, 8:10]
    lo_ref[...] = out_ref[:, 0:2]


def schwarz_q_kernel(qx_ref, yl_ref, yh_ref, k_ref, m_ref, *refs):
    consts, (q_ref, out_ref, hi_ref, lo_ref, scr, lines, acc) = refs[:-7], refs[-7:]
    nz = qx_ref.shape[2]
    scr[...] = jnp.zeros_like(scr)
    scr[:, 1:9] = qx_ref[...]
    scr[:, 0:1] = yl_ref[:, 0:1]
    scr[:, 1:2] = scr[:, 1:2] + yl_ref[:, 1:2]
    scr[:, 8:9] = scr[:, 8:9] + yh_ref[:, 0:1]
    scr[:, 9:10] = yh_ref[:, 1:2]
    q_ref[...] = scr[8:16, 1:9]
    out = solve_columns(scr[...].reshape(24 * 16, nz), k_ref, m_ref, 2, 3, consts, lines, acc)
    out_ref[...] = out.reshape(8, 16, nz)
    hi_ref[...] = out_ref[:, 8:10]
    lo_ref[...] = out_ref[:, 0:2]


def gather_s(u_ref, y_ref, yl_ref, yh_ref):
    u_ref[...] = y_ref[:, 1:9]
    u_ref[:, 0:2] = u_ref[:, 0:2] + yl_ref[...]
    u_ref[:, 6:8] = u_ref[:, 6:8] + yh_ref[...]


def apply_u_kernel(idx_ref, b_ref, y_ref, yl_ref, yh_ref, k_ref, m_ref, inner_ref, zct_ref, *refs):
    consts, (u_ref, own_ref, au_ref, h_ref) = refs[:-4], refs[-4:]
    nz = u_ref.shape[2]
    gather_s(u_ref, y_ref, yl_ref, yh_ref)
    own_ref[...] = u_ref[14:22]
    u = own_ref[...].reshape(64, nz)
    au = apply(u, k_ref[...], m_ref[...], *(ref[...] for ref in consts))
    au_ref[...] = au.reshape(8, 8, nz)
    h = dot(jnp.sum(inner_ref[...] * au, axis=0, keepdims=True), zct_ref[...]) * lane_sel(idx_ref[0])
    acc = b_ref[0] * own_ref[0, :7]
    for x in range(1, 7):
        acc = acc + b_ref[x] * own_ref[x, :7]
    h_ref[...] = rows_tile([jnp.zeros((1, LANES), jnp.float32), h, lane_put([total(acc), total(u * au)])])


def apply_s_kernel(y_ref, yl_ref, yh_ref, k_ref, m_ref, *refs):
    consts, (s_ref, as_ref, hi_ref) = refs[:-3], refs[-3:]
    nz = s_ref.shape[2]
    gather_s(s_ref, y_ref, yl_ref, yh_ref)
    out = apply(s_ref[...].reshape(64, nz), k_ref[...], m_ref[...], *(ref[...] for ref in consts))
    as_ref[...] = out.reshape(8, 8, nz)
    hi_ref[...] = as_ref[7:8]


def apply_p_kernel(idx_ref, u_ref, x_ref, k_ref, m_ref, inner_ref, zl_ref, *refs):
    (rep8, wz, g8, g8t, zk, kk, ww), (p_ref, q_ref, hi_ref, lo_ref, field, su, sk, acc) = refs[:-8], refs[-8:]
    nz = u_ref.shape[2]
    count = idx_ref[1]
    x0 = x_ref[...]
    picks = [x0 * lane_sel(lax.rem(idx_ref[0] + (apart + 2 * count), count)) for apart in range(-2, 3)]
    lines = dot(rows_tile(picks), zl_ref[...])
    field[...] = u_ref[...]
    side = inner_ref[8:16]
    for c in range(5):
        add = side * lines[c : c + 1]
        for x in range(7 * c + 1, 7 * c + 7):
            field[x] = field[x] + add
    p_ref[...] = field[14:22]
    whole = field[...].reshape(36 * 8, nz)
    su[...] = dot(whole, g8[...])
    sk[...] = dot(whole, zk[...])
    acc[...] = jnp.zeros_like(acc)
    k_lines, m_lines = dot(k_ref[...], rep8[...]), dot(m_ref[...], rep8[...]) * wz[...]
    for c in range(5):
        k_line, m_line = k_lines[c + 1 : c + 2], m_lines[c + 1 : c + 2]
        part = slice(56 * c, 56 * c + 64)
        u = su[part]
        out = (k_line * wz[...]) * dot(kk[...], u) + ww[...] * (k_line * sk[part] + m_line * u)
        acc[part] = acc[part] + out
    q_ref[...] = dot(acc[48:240], g8t[...]).reshape(24, 8, nz)
    hi_ref[...] = q_ref[:, 6:8]
    lo_ref[...] = q_ref[:, 0:2]


def apply_w_kernel(idx_ref, s_ref, x_ref, side_ref, k_ref, m_ref, ks_ref, inner_ref, zl_ref, face_ref, *refs):
    consts, (w_ref, v_ref, hi_ref) = refs[:-3], refs[-3:]
    rep8, wz, g8, g8t = consts[:4]
    nz = s_ref.shape[2]
    x1 = x_ref[...]
    left = lax.rem(idx_ref[0] + idx_ref[1] - 1, idx_ref[1])
    lines = dot(rows_tile([x1 * lane_sel(idx_ref[0]), x1 * lane_sel(left)]), zl_ref[...])
    w = s_ref[...].reshape(64, nz) + inner_ref[...] * lines[0:1]
    w_ref[...] = w.reshape(8, 8, nz)
    out = apply(w, k_ref[...], m_ref[...], *(ref[...] for ref in consts)).reshape(8, 8, nz)
    v_ref[...] = out
    scale = dot(ks_ref[2:3], rep8[...]) * wz[...]
    share = dot(scale * dot(lines, g8[...]), g8t[...])[1:2]
    v_ref[0] = v_ref[0] + side_ref[0] + face_ref[...] * share
    hi_ref[...] = v_ref[0:7, 7:8]


def shift(value, axis, step):
    count = lax.axis_size(axis)
    return lax.ppermute(value, axis, [(i, (i + step) % count) for i in range(count)])


def local(right_side, stiff_coef, mass_coef, coarse_factor):
    nz = right_side.shape[2]
    c_dev, n_coarse = coarse_factor.shape
    ez = stiff_coef.shape[2]
    n_gx, n_gy = lax.axis_size("gx"), lax.axis_size("gy")
    width = n_coarse // n_gx
    tab = {name: jnp.asarray(value) if isinstance(value, np.ndarray) else value for name, value in make_tables(ez, c_dev).items()}
    k = stiff_coef.reshape(1, ez)
    m = mass_coef.reshape(1, ez)
    b = right_side
    idx = jnp.stack([lax.axis_index("gx"), jnp.int32(n_gx), lax.axis_index("gy") & 1])
    solve_tab = [tab[name] for name in SOLVE]
    apply_tab = [tab[name] for name in APPLY]
    inner, zct, zl, eye = (tab[name] for name in ("inner", "zct", "zl", "eye"))

    def kernel(fn, *fixed):
        def call(*refs):
            return fn(*fixed, *refs)

        call.__name__ = fn.__name__
        return call

    def swap_gx(value):
        return lax.all_to_all(value, "gx", 0, 0)

    def swap_gy(value):
        return lax.all_to_all(value, "gy", 0, 0)

    def halves(sums):
        (mine,) = run(sum_kernel, [sums.shape[1:]], sums)
        return mine, lax.ppermute(mine, "gy", [(i, i ^ 1) for i in range(n_gy)])

    aux = -(-(LANES + 7 * nz) // LANES) * LANES
    (pay,) = run(kernel(first_kernel, tab["k_parts"], tab["m_parts"], width), [(n_gx, c_dev, width + aux)],
                 idx, b, k, m, coarse_factor, scratch=[(8, aux)], limit=56)
    xl = swap_gx(pay)

    outs = [(n_gy, 1, width // 2), (52, 8, nz), (52, 1, nz), (52, 2, nz), (8, ez), (8, ez),
            (n_gx, c_dev, width + LANES), (1, LANES)]
    pay, bx, hi, lo, ks, ms, members, rc = run(kernel(coarse_in_kernel, width), outs, idx, xl, eye, free=(0,))
    y_low, y_high = shift(hi, "gy", 1), shift(lo, "gy", -1)
    sums = swap_gy(pay)

    sides = [(8, 2, nz), (8, 2, nz)]
    y, hi, lo = run(schwarz_b_kernel, [(36, 16, nz), (36, 2, nz), (36, 2, nz)], bx, y_low, y_high, ks, ms, *solve_tab,
                    scratch=[(52, 16, nz), (832, 10 * ez), (576, 10 * ez)])
    y_low, y_high = shift(hi, "gy", 1), shift(lo, "gy", -1)
    cube = (8, 8, nz)
    wide_u, u, au, h = run(apply_u_kernel, [(36, 8, nz), cube, cube, (8, LANES)], idx, b, y, y_low, y_high, k, m, inner, zct, *apply_tab,
                          free=(1, 2))

    mine, other = halves(sums)
    (pay,) = run(kernel(coarse_out_kernel, width), [(n_gx, 1, 3 * LANES)], idx, mine, other, members, eye, h)
    got = swap_gx(pay)
    pay, x0 = run(kernel(coarse_mid_kernel, width), [(n_gy, 1, width // 2 + LANES), (1, LANES)], got, members, rc, eye, free=(0,))
    sums = swap_gy(pay)

    p, qx, hi, lo = run(apply_p_kernel, [cube, (24, 8, nz), (24, 2, nz), (24, 2, nz)], idx, wide_u, x0, ks, ms, inner, zl, *apply_tab,
                        scratch=[(36, 8, nz)] + [(288, 8 * ez)] * 3)
    y_low, y_high = shift(hi, "gy", 1), shift(lo, "gy", -1)
    q, y, hi, lo = run(schwarz_q_kernel, [cube, (8, 16, nz)] + sides, qx, y_low, y_high, ks, ms, *solve_tab,
                       scratch=[(24, 16, nz), (384, 10 * ez), (128, 10 * ez)])
    y_low, y_high = shift(hi, "gy", 1), shift(lo, "gy", -1)
    s, a_s, hi = run(apply_s_kernel, [cube, cube, (1, 8, nz)], y, y_low, y_high, k, m, *apply_tab)
    side = shift(hi, "gx", 1)

    mine, other = halves(sums)
    pay, scal, resid = run(kernel(pair_kernel, width), [(n_gx, 1, 4 * LANES), (1, LANES), cube], idx, mine, other, members, eye, b, q, u, au, s, a_s, inner, zct)
    got = swap_gx(pay)
    pay, x1 = run(kernel(last_in_kernel, width), [(n_gy, 1, LANES), (1, LANES)], got, members, x0, scal, eye, free=(0,))
    sums = swap_gy(pay)

    w, v, hi = run(apply_w_kernel, [cube, cube, (7, 1, nz)], idx, s, x1, side, k, m, ks, inner, zl, tab["face"], *apply_tab)
    y_low = shift(hi, "gy", 1)
    sol, res = run(final_kernel, [(7, 7, nz), (7, 7, nz)], sums, scal, p, w, resid, q, v, y_low, free=(0, 1))
    return sol, res


def solution(mesh):
    placed = (P("gx", "gy", None), P("gx", "gy", None), P("gx", "gy", None), P(("gx", "gy"), None))

    return jax.shard_map(
        local,
        mesh=mesh,
        in_specs=placed,
        out_specs=(P("gx", "gy", None), P("gx", "gy", None)),
        check_vma=False,
    )
```
